256 devices in a mesh: seq: 32 (over x, z), chan: 8 (over y, core).
Axes of the slice: x: 4, y: 4, z: 8, core: 2. Of those that a mesh axis runs over, the one named last changes fastest.
Arguments:
- query_rows: bfloat16 [8192, 2048], P('seq', 'chan'), may hold values from -6 to 6
- key_rows: bfloat16 [8192, 2048], P('seq', 'chan'), may hold values from -6 to 6
- value_rows: bfloat16 [8192, 2048], P('seq', 'chan'), may hold values from -6 to 6
- long_filter: float32 [8192, 2048], P('seq', 'chan'), may hold values from -2 to 2
- short_taps: float32 [3, 3, 2048], P(None, None, ('seq', 'chan')), may hold values from -3 to 3
- skip_gain: float32 [2048], P(('seq', 'chan')), may hold values from -3 to 3
- cotangent: bfloat16 [8192, 2048], P('seq', 'chan'), may hold values from -6 to 6
Outputs:
- gated_out: bfloat16 [8192, 2048], P('seq', 'chan')
- query_grad: bfloat16 [8192, 2048], P('seq', 'chan')
- key_grad: bfloat16 [8192, 2048], P('seq', 'chan')
- value_grad: bfloat16 [8192, 2048], P('seq', 'chan')
- filter_grad: float32 [8192, 2048], P('seq', 'chan')
- taps_grad: float32 [3, 3, 2048], P(None, None, 'chan')
- skip_grad: float32 [2048], P('chan')
The draws below stay inside these ranges and needn't reach their ends.
All inputs are finite; a program needn't handle non-finite values.
Results may differ from the reference program's by a relative error of at most 0.00135.
Values may be sent and summed in bfloat16 or wider, within the bound.
A program may use at most 64 MiB of HBM per device.

```python
import math
import jax
import jax.numpy as jnp

C = 2048
SEQ = 8192


def draw_long_filter(key, part):
    key_rate, key_noise = jax.random.split(jax.random.fold_in(key, 7), 2)
    position = jnp.arange(SEQ, dtype=jnp.float32)[:, None]
    low_rate = math.log(30.0)
    high_rate = math.log(SEQ * 4.0)
    horizon = jnp.exp(jax.random.uniform(key_rate, (1, C), jnp.float32, low_rate, high_rate))
    envelope = jnp.exp(-position / horizon)
    scaling = 1.0 / jnp.sqrt(0.5 * horizon * (1.0 - jnp.exp(-2.0 * SEQ / horizon)) + 1.0)
    rough = jax.random.truncated_normal(key_noise, -4.0, 4.0, (SEQ, C), jnp.float32)
    return rough * envelope * scaling


def levels(rng, shape, shards, low, high):
    factor_of = 1.0
    for axis_at, shards_of in shards:
        heights = jax.random.uniform(jax.random.fold_in(jax.random.fold_in(rng, 6), axis_at), (shards_of,), jnp.float32, low / len(shards), high / len(shards))
        factor_of = factor_of * jnp.repeat(jnp.exp(heights), shape[axis_at] // shards_of).reshape((-1,) + (1,) * (len(shape) - 1 - axis_at))
    return factor_of


def centred(stream_key, shape, spread, reach, shards=(), held_as=jnp.bfloat16):
    drawn = spread * jax.random.normal(stream_key, shape, jnp.float32)
    if shards:
        drawn = drawn * levels(stream_key, shape, shards, -0.22, 0.18)
    return jnp.clip(drawn, -reach, reach).astype(held_as)


def setup_inputs(seed: int = 0) -> dict:
    streams_of = jax.random.split(jax.random.key(seed), 8)
    query_rows = centred(streams_of[0], (SEQ, C), 1.0, 6.0, ((0, 32), (1, 8)))
    key_rows = centred(streams_of[1], (SEQ, C), 1.0, 6.0, ((0, 32), (1, 8)))
    value_rows = centred(streams_of[2], (SEQ, C), 1.0, 6.0, ((0, 32), (1, 8)))
    long_filter = draw_long_filter(jax.random.fold_in(streams_of[7], 71), 0)
    short_taps = centred(streams_of[4], (3, 3, C), 0.6, 3.0, ((2, 256),), jnp.float32)
    skip_gain = centred(streams_of[5], (C,), 0.7, 3.0, ((0, 256),), jnp.float32)
    cotangent = centred(streams_of[6], (SEQ, C), 1.0, 6.0, ((0, 32), (1, 8)))
    return dict(query_rows=query_rows, key_rows=key_rows, value_rows=value_rows, long_filter=long_filter, short_taps=short_taps, skip_gain=skip_gain, cotangent=cotangent)


def delay(signal, steps):
    if steps == 0:
        return signal
    zeros_block = jnp.zeros((steps,) + signal.shape[1:], signal.dtype)
    return jnp.concatenate([zeros_block, signal[:-steps]], axis=0)


def advance(signal, steps):
    if steps == 0:
        return signal
    zeros_block = jnp.zeros((steps,) + signal.shape[1:], signal.dtype)
    return jnp.concatenate([signal[steps:], zeros_block], axis=0)


def reference(query_rows, key_rows, value_rows, long_filter, short_taps, skip_gain, cotangent):
    length = query_rows.shape[0]
    points = 2 * length
    grad_scale = length ** -0.5
    inputs = [query_rows.astype(jnp.float32), key_rows.astype(jnp.float32), value_rows.astype(jnp.float32)]
    convs = []
    for stream in range(3):
        total = short_taps[stream, 0] * inputs[stream]
        for offset in range(1, 3):
            total = total + short_taps[stream, offset] * delay(inputs[stream], offset)
        convs.append(total)
    query_conv, key_conv, value_conv = convs
    product = key_conv * value_conv
    prod_spec = jnp.fft.rfft(product, n=points, axis=0)
    filt_spec = jnp.fft.rfft(long_filter, n=points, axis=0)
    mixed_conv = jnp.fft.irfft(prod_spec * filt_spec, n=points, axis=0)[:length] + skip_gain * product
    gated_out = (query_conv * mixed_conv).astype(jnp.bfloat16)
    upstream = cotangent.astype(jnp.float32)
    gated_grad = upstream * query_conv
    query_conv_grad = upstream * mixed_conv
    grad_spec = jnp.fft.rfft(gated_grad, n=points, axis=0)
    product_grad = jnp.fft.irfft(grad_spec * jnp.conj(filt_spec), n=points, axis=0)[:length] + skip_gain * gated_grad
    filter_grad = grad_scale * jnp.fft.irfft(grad_spec * jnp.conj(prod_spec), n=points, axis=0)[:length]
    skip_grad = grad_scale * jnp.sum(gated_grad * product, axis=0)
    key_conv_grad = product_grad * value_conv
    value_conv_grad = product_grad * key_conv
    conv_grads = [query_conv_grad, key_conv_grad, value_conv_grad]
    input_grads = []
    tap_rows = []
    for stream in range(3):
        total = short_taps[stream, 0] * conv_grads[stream]
        for offset in range(1, 3):
            total = total + short_taps[stream, offset] * advance(conv_grads[stream], offset)
        input_grads.append(total.astype(jnp.bfloat16))
        tap_rows.append(jnp.stack([grad_scale * jnp.sum(conv_grads[stream] * delay(inputs[stream], offset), axis=0) for offset in range(3)]))
    taps_grad = jnp.stack(tap_rows)
    return (gated_out, input_grads[0], input_grads[1], input_grads[2], filter_grad, taps_grad, skip_grad)
```

```python
import functools
import math

import jax
import jax.numpy as jnp
import ml_dtypes
import numpy as np
from jax import lax
from jax.experimental import pallas as pl
from jax.experimental.pallas import tpu as pltpu
from jax.sharding import PartitionSpec as P

F32 = jnp.float32
BF16 = jnp.bfloat16
MESH = pl.DeviceIdType.MESH


def halves(table):
    high = table.astype(np.float32).astype(ml_dtypes.bfloat16)
    low = (table - high.astype(np.float64)).astype(np.float32).astype(ml_dtypes.bfloat16)
    return np.stack([high, low])


def transform_tables(blocks, width, group):
    total = blocks * width
    shifted = np.arange(blocks) - 0.25
    outer = 2.0 * np.pi / blocks * np.outer(shifted, np.arange(blocks))
    eye = np.eye(group)
    left = np.concatenate([np.kron(np.cos(outer), eye), np.kron(-np.sin(outer), eye)], axis=0)
    back = left.T / total
    inner = 2.0 * np.pi / width * (np.outer(np.arange(width), np.arange(width)) % width)
    right = np.stack([halves(np.cos(inner)), halves(np.sin(inner))])
    turn = 2.0 * np.pi / total * np.outer(shifted, np.arange(width))
    twist = np.stack([np.cos(turn), np.sin(turn)]).astype(np.float32)
    twist = np.repeat(twist, group, axis=1)
    return halves(left), halves(back), right, twist


def split(value):
    high = value.astype(BF16)
    return high, (value - high.astype(F32)).astype(BF16)


def dot(left, right):
    return jnp.dot(left, right, preferred_element_type=F32)


def dot3(left, right):
    return dot(left[0], right[0]) + dot(left[0], right[1]) + dot(left[1], right[0])


def delayed(value, steps):
    before = jnp.concatenate([jnp.zeros_like(value[:1]), value[:-1]], axis=0)
    lane = lax.broadcasted_iota(jnp.int32, value.shape, 2)
    return jnp.where(
        lane < steps, pltpu.roll(before, steps, 2), pltpu.roll(value, steps, 2)
    )


def advanced(value, steps):
    width = value.shape[2]
    after = jnp.concatenate([value[1:], jnp.zeros_like(value[:1])], axis=0)
    lane = lax.broadcasted_iota(jnp.int32, value.shape, 2)
    return jnp.where(
        lane >= width - steps,
        pltpu.roll(after, width - steps, 2),
        pltpu.roll(value, width - steps, 2),
    )


def total_of(value):
    return jnp.sum(jnp.sum(value, axis=0), axis=1, keepdims=True)


def kernel(
    nseq,
    nchan,
    group,
    scale,
    q_ref,
    k_ref,
    v_ref,
    c_ref,
    h_ref,
    side_ref,
    left_hbm,
    back_hbm,
    right_hbm,
    twist_hbm,
    go_ref,
    qg_ref,
    kg_ref,
    vg_ref,
    fg_ref,
    sums_ref,
    left,
    back,
    right,
    twist,
    send_h,
    send_kv,
    send_qc,
    got_h,
    got_kv,
    got_qc,
    side,
    out_gq,
    out_f,
    out_kv,
    out_s,
    in_gq,
    in_f,
    in_kv,
    in_s,
    x_q,
    x_k,
    x_v,
    x_c,
    x_p,
    x_g,
    d_q,
    d_k,
    d_v,
    spec_h,
    spec_p,
    spec_g,
    table_sem,
    send_sem,
    recv_sem,
    side_sem,
):
    me = lax.axis_index("seq")
    mine = lax.axis_index("chan")
    rows, width = q_ref.shape

    tables = [
        pltpu.make_async_copy(src, dst, table_sem.at[i])
        for i, (src, dst) in enumerate(
            [(left_hbm, left), (back_hbm, back), (right_hbm, right), (twist_hbm, twist)]
        )
    ]
    for copy in tables:
        copy.start()

    per = nseq // nchan
    to_seq = nchan * lax.rem(me, per) + mine
    to_chan = lax.div(me, per)
    from_seq = per * mine + lax.div(me, nchan)
    from_chan = lax.rem(me, nchan)
    stays = jnp.logical_and(to_seq == me, to_chan == mine)

    barrier = pltpu.get_barrier_semaphore()

    def greet(step, carry):
        peer = lax.rem(me + step, nseq)
        pl.semaphore_signal(barrier, inc=1, device_id=(peer, mine), device_id_type=MESH)
        return carry

    lax.fori_loop(1, nseq, greet, 0)

    @pl.when(jnp.logical_not(stays))
    def _():
        pl.semaphore_signal(
            barrier, inc=1, device_id=(from_seq, from_chan), device_id_type=MESH
        )

    send_h[...] = h_ref[...].T.reshape(nseq, group, width)

    @pl.when(stays)
    def _():
        pl.semaphore_wait(barrier, nseq - 1)

    @pl.when(jnp.logical_not(stays))
    def _():
        pl.semaphore_wait(barrier, nseq)

    def copy_to(source, target, index, peer):
        return pltpu.make_async_remote_copy(
            src_ref=source.at[peer],
            dst_ref=target.at[me],
            send_sem=send_sem.at[index],
            recv_sem=recv_sem.at[index],
            device_id=(peer, mine),
            device_id_type=MESH,
        )

    def send_all(source, target, index):
        def body(step, carry):
            copy_to(source, target, index, lax.rem(me + step, nseq)).start()
            return carry

        lax.fori_loop(1, nseq, body, 0)
        target[me] = source[me]

    def arrived(target, index):
        part = target.at[pl.ds(0, nseq - 1)]
        pltpu.make_async_copy(part, part, recv_sem.at[index]).wait()

    def sent(source, index):
        part = source.at[pl.ds(0, nseq - 1)]
        pltpu.make_async_copy(part, part, send_sem.at[index]).wait()

    send_all(send_h, got_h, 0)

    side_copy = pltpu.make_async_remote_copy(
        src_ref=side_ref,
        dst_ref=side,
        send_sem=side_sem.at[0],
        recv_sem=side_sem.at[1],
        device_id=(to_seq, to_chan),
        device_id_type=MESH,
    )

    @pl.when(jnp.logical_not(stays))
    def _():
        side_copy.start()

    @pl.when(stays)
    def _():
        side[...] = side_ref[...]

    def paired(first, second):
        shape = (nseq, group, width)
        one = first[...].astype(F32).T.reshape(shape)
        two = second[...].astype(F32).T.reshape(shape)
        return jnp.concatenate([one, two], axis=1).astype(BF16)

    send_kv[...] = paired(k_ref, v_ref)
    send_all(send_kv, got_kv, 1)
    send_qc[...] = paired(q_ref, c_ref)
    send_all(send_qc, got_qc, 2)

    for copy in tables:
        copy.wait()

    def forward(signal, spec):
        parts = split(signal.reshape(rows, width))
        wave = dot3((left[0], left[1]), parts)
        real, imag = wave[:rows], wave[rows:]
        cosine, sine = twist[0], twist[1]
        turned_real = split(real * cosine + imag * sine)
        turned_imag = split(imag * cosine - real * sine)
        cos_parts = (right[0, 0], right[0, 1])
        sin_parts = (right[1, 0], right[1, 1])
        spec[0] = dot3(turned_real, cos_parts) + dot3(turned_imag, sin_parts)
        spec[1] = dot3(turned_imag, cos_parts) - dot3(turned_real, sin_parts)

    def inverse(real, imag):
        real, imag = split(real), split(imag)
        cos_parts = (right[0, 0], right[0, 1])
        sin_parts = (right[1, 0], right[1, 1])
        wave_real = dot3(real, cos_parts) - dot3(imag, sin_parts)
        wave_imag = dot3(imag, cos_parts) + dot3(real, sin_parts)
        cosine, sine = twist[0], twist[1]
        turned_real = split(wave_real * cosine - wave_imag * sine)
        turned_imag = split(wave_imag * cosine + wave_real * sine)
        signal = dot3((back[0, :, :rows], back[1, :, :rows]), turned_real)
        signal = signal + dot3((back[0, :, rows:], back[1, :, rows:]), turned_imag)
        return signal.reshape(nseq, group, width)

    arrived(got_h, 0)
    forward(got_h[...], spec_h)

    @pl.when(jnp.logical_not(stays))
    def _():
        side_copy.wait()

    taps = [[side[:, 3 * s + i : 3 * s + i + 1] for i in range(3)] for s in range(3)]
    gain = side[:, 9:10]

    def short(value, keep, coeffs):
        one, two = delayed(value, 1), delayed(value, 2)
        keep[0] = one
        keep[1] = two
        return coeffs[0] * value + coeffs[1] * one + coeffs[2] * two

    arrived(got_kv, 1)
    both = got_kv[...].astype(F32)
    x_k[...] = both[:, :group]
    x_v[...] = both[:, group:]
    key_conv = short(x_k[...], d_k, taps[1])
    value_conv = short(x_v[...], d_v, taps[2])
    x_p[...] = key_conv * value_conv
    forward(x_p[...], spec_p)
    h_re, h_im = spec_h[0], spec_h[1]
    p_re, p_im = spec_p[0], spec_p[1]
    mixed = inverse(p_re * h_re - p_im * h_im, p_re * h_im + p_im * h_re)
    mixed = mixed + gain * x_p[...]

    arrived(got_qc, 2)
    both = got_qc[...].astype(F32)
    x_q[...] = both[:, :group]
    x_c[...] = both[:, group:]
    query_conv = short(x_q[...], d_q, taps[0])
    x_g[...] = x_c[...] * query_conv
    query_conv_grad = x_c[...] * mixed

    def spread(grad, coeffs):
        return (
            coeffs[0] * grad + coeffs[1] * advanced(grad, 1) + coeffs[2] * advanced(grad, 2)
        )

    out_gq[...] = jnp.concatenate(
        [query_conv * mixed, spread(query_conv_grad, taps[0])], axis=1
    ).astype(BF16)
    send_all(out_gq, in_gq, 3)
    sums = [
        total_of(query_conv_grad * x_q[...]),
        total_of(query_conv_grad * d_q[0]),
        total_of(query_conv_grad * d_q[1]),
    ]

    forward(x_g[...], spec_g)
    g_re, g_im = spec_g[0], spec_g[1]
    p_re, p_im = spec_p[0], spec_p[1]
    out_f[...] = scale * inverse(p_re * g_re + p_im * g_im, p_re * g_im - p_im * g_re)
    send_all(out_f, in_f, 4)
    h_re, h_im = spec_h[0], spec_h[1]
    product_grad = inverse(h_re * g_re + h_im * g_im, h_re * g_im - h_im * g_re)
    product_grad = product_grad + gain * x_g[...]

    key_conv = taps[1][0] * x_k[...] + taps[1][1] * d_k[0] + taps[1][2] * d_k[1]
    value_conv = taps[2][0] * x_v[...] + taps[2][1] * d_v[0] + taps[2][2] * d_v[1]
    key_conv_grad = product_grad * value_conv
    value_conv_grad = product_grad * key_conv
    out_kv[...] = jnp.concatenate(
        [spread(key_conv_grad, taps[1]), spread(value_conv_grad, taps[2])], axis=1
    ).astype(BF16)
    send_all(out_kv, in_kv, 5)
    sums += [
        total_of(key_conv_grad * x_k[...]),
        total_of(key_conv_grad * d_k[0]),
        total_of(key_conv_grad * d_k[1]),
        total_of(value_conv_grad * x_v[...]),
        total_of(value_conv_grad * d_v[0]),
        total_of(value_conv_grad * d_v[1]),
        total_of(x_g[...] * x_p[...]),
    ]
    lane = lax.broadcasted_iota(jnp.int32, (group, 128), 1)
    place = lax.broadcasted_iota(jnp.int32, (group, 128), 0)
    packed = jnp.zeros((group, 128), F32)
    for index, value in enumerate(sums):
        packed = jnp.where(lane == group * index + place, value, packed)
    packed = scale * jnp.sum(packed, axis=0, keepdims=True)
    out_s[...] = jnp.broadcast_to(packed[None], out_s.shape)
    send_all(out_s, in_s, 6)

    def unpaired(source, first, second):
        both = source[...].astype(F32)
        first[...] = both[:, :group].reshape(rows, width).T.astype(BF16)
        second[...] = both[:, group:].reshape(rows, width).T.astype(BF16)

    arrived(in_gq, 3)
    unpaired(in_gq, go_ref, qg_ref)
    arrived(in_f, 4)
    fg_ref[...] = in_f[...].reshape(rows, width).T
    arrived(in_kv, 5)
    unpaired(in_kv, kg_ref, vg_ref)
    arrived(in_s, 6)
    sums_ref[...] = in_s[...]

    for index, source in enumerate([send_h, send_kv, send_qc, out_gq, out_f, out_kv, out_s]):
        sent(source, index)


def per_device(query_rows, key_rows, value_rows, long_filter, short_taps, skip_gain, cotangent):
    rows, channels = query_rows.shape
    nseq, nchan = lax.axis_size("seq"), lax.axis_size("chan")
    group = channels // nseq
    scale = 1.0 / math.sqrt(rows * nseq)
    tables = [jnp.asarray(t) for t in transform_tables(nseq, rows, group)]
    side = jnp.concatenate([short_taps.reshape(9, group), skip_gain.reshape(1, group)], axis=0)
    side = jnp.pad(side.T, ((0, 0), (0, 128 - 10)))
    block = jax.ShapeDtypeStruct((rows, channels), BF16)
    vmem = pl.BlockSpec(memory_space=pltpu.VMEM)
    hbm = pl.BlockSpec(memory_space=pl.ANY)
    one, two = (nseq, group, rows), (nseq, 2 * group, rows)
    spec = pltpu.VMEM((2, nseq * group, rows), F32)
    outs = pl.pallas_call(
        functools.partial(kernel, nseq, nchan, group, scale),
        out_shape=(
            block,
            block,
            block,
            block,
            jax.ShapeDtypeStruct((rows, channels), F32),
            jax.ShapeDtypeStruct((nseq, 1, 128), F32),
        ),
        in_specs=[vmem] * 6 + [hbm] * 4,
        out_specs=[vmem] * 6,
        scratch_shapes=[pltpu.VMEM(t.shape, t.dtype) for t in tables]
        + [
            pltpu.VMEM(one, F32),
            pltpu.VMEM(two, BF16),
            pltpu.VMEM(two, BF16),
            pltpu.VMEM(one, F32),
            pltpu.VMEM(two, BF16),
            pltpu.VMEM(two, BF16),
            pltpu.VMEM((group, 128), F32),
            pltpu.VMEM(two, BF16),
            pltpu.VMEM(one, F32),
            pltpu.VMEM(two, BF16),
            pltpu.VMEM((nseq, 1, 128), F32),
            pltpu.VMEM(two, BF16),
            pltpu.VMEM(one, F32),
            pltpu.VMEM(two, BF16),
            pltpu.VMEM((nseq, 1, 128), F32),
        ]
        + [pltpu.VMEM(one, F32)] * 6
        + [pltpu.VMEM((2,) + one, F32)] * 3
        + [spec] * 3
        + [
            pltpu.SemaphoreType.DMA((4,)),
            pltpu.SemaphoreType.DMA((7,)),
            pltpu.SemaphoreType.DMA((7,)),
            pltpu.SemaphoreType.DMA((2,)),
        ],
        compiler_params=pltpu.CompilerParams(
            collective_id=0, has_side_effects=True, vmem_limit_bytes=48 << 20
        ),
        name="hyena",
    )(query_rows, key_rows, value_rows, cotangent, long_filter, side, *tables)
    sums = outs[5].reshape(nseq, 128)[:, : 10 * group].reshape(nseq, 10, group)
    sums = sums.transpose(1, 0, 2).reshape(10, channels)
    return outs[:5] + (sums[:9].reshape(3, 3, channels), sums[9])


def solution(mesh):
    in_specs = (
        P("seq", "chan"),
        P("seq", "chan"),
        P("seq", "chan"),
        P("seq", "chan"),
        P(None, None, ("seq", "chan")),
        P(("seq", "chan")),
        P("seq", "chan"),
    )
    out_specs = (
        P("seq", "chan"),
        P("seq", "chan"),
        P("seq", "chan"),
        P("seq", "chan"),
        P("seq", "chan"),
        P(None, None, "chan"),
        P("chan"),
    )
    return jax.shard_map(
        per_device, mesh=mesh, in_specs=in_specs, out_specs=out_specs, check_vma=False
    )
```

```python
import functools
import math

import jax
import jax.numpy as jnp
import ml_dtypes
import numpy as np
from jax import lax
from jax.experimental import pallas as pl
from jax.experimental.pallas import tpu as pltpu
from jax.sharding import PartitionSpec as P

F32 = jnp.float32
BF16 = jnp.bfloat16
MESH = pl.DeviceIdType.MESH


def halves(table):
    high = table.astype(np.float32).astype(ml_dtypes.bfloat16)
    low = (table - high.astype(np.float64)).astype(np.float32).astype(ml_dtypes.bfloat16)
    return np.stack([high, low])


def transform_tables(blocks, width, group):
    total = blocks * width
    shifted = np.arange(blocks) - 0.25
    outer = 2.0 * np.pi / blocks * np.outer(shifted, np.arange(blocks))
    eye = np.eye(group)
    left = np.concatenate([np.kron(np.cos(outer), eye), np.kron(-np.sin(outer), eye)], axis=0)
    back = left.T / total
    inner = 2.0 * np.pi / width * (np.outer(np.arange(width), np.arange(width)) % width)
    right = np.stack([halves(np.cos(inner)), halves(np.sin(inner))])
    turn = 2.0 * np.pi / total * np.outer(shifted, np.arange(width))
    twist = np.stack([np.cos(turn), np.sin(turn)]).astype(np.float32)
    twist = np.repeat(twist, group, axis=1)
    return halves(left), halves(back), right, twist


def split(value):
    high = value.astype(BF16)
    return high, (value - high.astype(F32)).astype(BF16)


def dot(left, right):
    return jnp.dot(left, right, preferred_element_type=F32)


def dot3(left, right):
    return dot(left[0], right[0]) + dot(left[0], right[1]) + dot(left[1], right[0])


def delayed(value, steps):
    before = jnp.concatenate([jnp.zeros_like(value[:1]), value[:-1]], axis=0)
    lane = lax.broadcasted_iota(jnp.int32, value.shape, 2)
    return jnp.where(
        lane < steps, pltpu.roll(before, steps, 2), pltpu.roll(value, steps, 2)
    )


def advanced(value, steps):
    width = value.shape[2]
    after = jnp.concatenate([value[1:], jnp.zeros_like(value[:1])], axis=0)
    lane = lax.broadcasted_iota(jnp.int32, value.shape, 2)
    return jnp.where(
        lane >= width - steps,
        pltpu.roll(after, width - steps, 2),
        pltpu.roll(value, width - steps, 2),
    )


def total_of(value):
    return jnp.sum(jnp.sum(value, axis=0), axis=1, keepdims=True)


def kernel(
    nseq,
    nchan,
    group,
    scale,
    q_hbm,
    k_hbm,
    v_hbm,
    c_hbm,
    h_hbm,
    taps_hbm,
    gain_hbm,
    left_hbm,
    back_hbm,
    right_hbm,
    twist_hbm,
    go_hbm,
    qg_hbm,
    kg_hbm,
    vg_hbm,
    fg_hbm,
    sums_hbm,
    q_ref,
    k_ref,
    v_ref,
    c_ref,
    h_ref,
    taps_own,
    gain_own,
    left,
    back,
    right,
    twist,
    send_h,
    send_kv,
    send_qc,
    got_h,
    got_kv,
    got_qc,
    taps_ref,
    gain_ref,
    out_gq,
    out_f,
    out_kv,
    out_s,
    in_gq,
    in_f,
    in_kv,
    in_s,
    x_q,
    x_k,
    x_v,
    x_c,
    x_p,
    x_g,
    d_q,
    d_k,
    d_v,
    spec_h,
    spec_p,
    spec_g,
    go_ref,
    qg_ref,
    kg_ref,
    vg_ref,
    fg_ref,
    input_sem,
    out_sem,
    table_sem,
    send_sem,
    recv_sem,
    side_sem,
):
    me = lax.axis_index("seq")
    mine = lax.axis_index("chan")
    rows, width = q_hbm.shape

    inputs = [
        pltpu.make_async_copy(src, dst, input_sem.at[i])
        for i, (src, dst) in enumerate(
            [
                (h_hbm, h_ref),
                (k_hbm, k_ref),
                (v_hbm, v_ref),
                (q_hbm, q_ref),
                (c_hbm, c_ref),
                (taps_hbm, taps_own),
                (gain_hbm, gain_own),
            ]
        )
    ]
    tables = [
        pltpu.make_async_copy(src, dst, table_sem.at[i])
        for i, (src, dst) in enumerate(
            [(left_hbm, left), (twist_hbm, twist), (right_hbm, right), (back_hbm, back)]
        )
    ]
    for copy in inputs + tables:
        copy.start()

    per = nseq // nchan
    to_seq = nchan * lax.rem(me, per) + mine
    to_chan = lax.div(me, per)
    from_seq = per * mine + lax.div(me, nchan)
    from_chan = lax.rem(me, nchan)
    stays = jnp.logical_and(to_seq == me, to_chan == mine)

    barrier = pltpu.get_barrier_semaphore()

    def greet(step, carry):
        peer = lax.rem(me + step, nseq)
        pl.semaphore_signal(barrier, inc=1, device_id=(peer, mine), device_id_type=MESH)
        return carry

    lax.fori_loop(1, nseq, greet, 0)

    @pl.when(jnp.logical_not(stays))
    def _():
        pl.semaphore_signal(
            barrier, inc=1, device_id=(from_seq, from_chan), device_id_type=MESH
        )

    inputs[0].wait()
    send_h[...] = h_ref[...].T.reshape(nseq, group, width)

    @pl.when(stays)
    def _():
        pl.semaphore_wait(barrier, nseq - 1)

    @pl.when(jnp.logical_not(stays))
    def _():
        pl.semaphore_wait(barrier, nseq)

    def copy_to(source, target, index, peer):
        return pltpu.make_async_remote_copy(
            src_ref=source.at[peer],
            dst_ref=target.at[me],
            send_sem=send_sem.at[index],
            recv_sem=recv_sem.at[index],
            device_id=(peer, mine),
            device_id_type=MESH,
        )

    def send_all(source, target, index):
        def body(step, carry):
            copy_to(source, target, index, lax.rem(me + step, nseq)).start()
            return carry

        lax.fori_loop(1, nseq, body, 0)
        target[me] = source[me]

    def arrived(target, index):
        part = target.at[pl.ds(0, nseq - 1)]
        pltpu.make_async_copy(part, part, recv_sem.at[index]).wait()

    def sent(source, index):
        part = source.at[pl.ds(0, nseq - 1)]
        pltpu.make_async_copy(part, part, send_sem.at[index]).wait()

    send_all(send_h, got_h, 0)

    side_copies = [
        pltpu.make_async_remote_copy(
            src_ref=src,
            dst_ref=dst,
            send_sem=side_sem.at[i],
            recv_sem=side_sem.at[2 + i],
            device_id=(to_seq, to_chan),
            device_id_type=MESH,
        )
        for i, (src, dst) in enumerate([(taps_own, taps_ref), (gain_own, gain_ref)])
    ]
    inputs[5].wait()
    inputs[6].wait()

    @pl.when(jnp.logical_not(stays))
    def _():
        for copy in side_copies:
            copy.start()

    @pl.when(stays)
    def _():
        taps_ref[...] = taps_own[...]
        gain_ref[...] = gain_own[...]

    def paired(first, second):
        shape = (nseq, group, width)
        one = first[...].astype(F32).T.reshape(shape)
        two = second[...].astype(F32).T.reshape(shape)
        return jnp.concatenate([one, two], axis=1).astype(BF16)

    inputs[1].wait()
    inputs[2].wait()
    send_kv[...] = paired(k_ref, v_ref)
    send_all(send_kv, got_kv, 1)
    inputs[3].wait()
    inputs[4].wait()
    send_qc[...] = paired(q_ref, c_ref)
    send_all(send_qc, got_qc, 2)

    for copy in tables:
        copy.wait()

    def forward(signal, spec):
        parts = split(signal.reshape(rows, width))
        wave = dot3((left[0], left[1]), parts)
        real, imag = wave[:rows], wave[rows:]
        cosine, sine = twist[0], twist[1]
        turned_real = split(real * cosine + imag * sine)
        turned_imag = split(imag * cosine - real * sine)
        cos_parts = (right[0, 0], right[0, 1])
        sin_parts = (right[1, 0], right[1, 1])
        spec[0] = dot3(turned_real, cos_parts) + dot3(turned_imag, sin_parts)
        spec[1] = dot3(turned_imag, cos_parts) - dot3(turned_real, sin_parts)

    def inverse(real, imag):
        real, imag = split(real), split(imag)
        cos_parts = (right[0, 0], right[0, 1])
        sin_parts = (right[1, 0], right[1, 1])
        wave_real = dot3(real, cos_parts) - dot3(imag, sin_parts)
        wave_imag = dot3(imag, cos_parts) + dot3(real, sin_parts)
        cosine, sine = twist[0], twist[1]
        turned_real = split(wave_real * cosine - wave_imag * sine)
        turned_imag = split(wave_imag * cosine + wave_real * sine)
        signal = dot3((back[0, :, :rows], back[1, :, :rows]), turned_real)
        signal = signal + dot3((back[0, :, rows:], back[1, :, rows:]), turned_imag)
        return signal.reshape(nseq, group, width)

    arrived(got_h, 0)
    forward(got_h[...], spec_h)

    @pl.when(jnp.logical_not(stays))
    def _():
        for copy in side_copies:
            copy.wait()

    diagonal = lax.broadcasted_iota(jnp.int32, (group, group), 0) == lax.broadcasted_iota(
        jnp.int32, (group, group), 1
    )

    def column(row):
        spread_out = jnp.broadcast_to(row, (group, group))
        return jnp.sum(jnp.where(diagonal, spread_out, 0.0), axis=1, keepdims=True)

    taps = [[column(taps_ref[s, i : i + 1, :]) for i in range(3)] for s in range(3)]
    gain = column(gain_ref[...])

    def short(value, keep, coeffs):
        one, two = delayed(value, 1), delayed(value, 2)
        keep[0] = one
        keep[1] = two
        return coeffs[0] * value + coeffs[1] * one + coeffs[2] * two

    arrived(got_kv, 1)
    both = got_kv[...].astype(F32)
    x_k[...] = both[:, :group]
    x_v[...] = both[:, group:]
    key_conv = short(x_k[...], d_k, taps[1])
    value_conv = short(x_v[...], d_v, taps[2])
    x_p[...] = key_conv * value_conv
    forward(x_p[...], spec_p)
    h_re, h_im = spec_h[0], spec_h[1]
    p_re, p_im = spec_p[0], spec_p[1]
    mixed = inverse(p_re * h_re - p_im * h_im, p_re * h_im + p_im * h_re)
    mixed = mixed + gain * x_p[...]

    arrived(got_qc, 2)
    both = got_qc[...].astype(F32)
    x_q[...] = both[:, :group]
    x_c[...] = both[:, group:]
    query_conv = short(x_q[...], d_q, taps[0])
    x_g[...] = x_c[...] * query_conv
    query_conv_grad = x_c[...] * mixed

    def spread(grad, coeffs):
        return (
            coeffs[0] * grad + coeffs[1] * advanced(grad, 1) + coeffs[2] * advanced(grad, 2)
        )

    out_gq[...] = jnp.concatenate(
        [query_conv * mixed, spread(query_conv_grad, taps[0])], axis=1
    ).astype(BF16)
    send_all(out_gq, in_gq, 3)
    sums = [
        total_of(query_conv_grad * x_q[...]),
        total_of(query_conv_grad * d_q[0]),
        total_of(query_conv_grad * d_q[1]),
    ]

    forward(x_g[...], spec_g)
    g_re, g_im = spec_g[0], spec_g[1]
    p_re, p_im = spec_p[0], spec_p[1]
    out_f[...] = scale * inverse(p_re * g_re + p_im * g_im, p_re * g_im - p_im * g_re)
    send_all(out_f, in_f, 4)
    h_re, h_im = spec_h[0], spec_h[1]
    product_grad = inverse(h_re * g_re + h_im * g_im, h_re * g_im - h_im * g_re)
    product_grad = product_grad + gain * x_g[...]

    key_conv = taps[1][0] * x_k[...] + taps[1][1] * d_k[0] + taps[1][2] * d_k[1]
    value_conv = taps[2][0] * x_v[...] + taps[2][1] * d_v[0] + taps[2][2] * d_v[1]
    key_conv_grad = product_grad * value_conv
    value_conv_grad = product_grad * key_conv
    out_kv[...] = jnp.concatenate(
        [spread(key_conv_grad, taps[1]), spread(value_conv_grad, taps[2])], axis=1
    ).astype(BF16)
    send_all(out_kv, in_kv, 5)
    sums += [
        total_of(key_conv_grad * x_k[...]),
        total_of(key_conv_grad * d_k[0]),
        total_of(key_conv_grad * d_k[1]),
        total_of(value_conv_grad * x_v[...]),
        total_of(value_conv_grad * d_v[0]),
        total_of(value_conv_grad * d_v[1]),
        total_of(x_g[...] * x_p[...]),
    ]
    lane = lax.broadcasted_iota(jnp.int32, (group, 128), 1)
    place = lax.broadcasted_iota(jnp.int32, (group, 128), 0)
    packed = jnp.zeros((group, 128), F32)
    for index, value in enumerate(sums):
        packed = jnp.where(lane == group * index + place, value, packed)
    packed = scale * jnp.sum(packed, axis=0, keepdims=True)
    out_s[...] = jnp.broadcast_to(packed[None], out_s.shape)
    send_all(out_s, in_s, 6)

    def unpaired(source, first, second):
        both = source[...].astype(F32)
        first[...] = both[:, :group].reshape(rows, width).T.astype(BF16)
        second[...] = both[:, group:].reshape(rows, width).T.astype(BF16)

    writes = [
        pltpu.make_async_copy(src, dst, out_sem.at[i])
        for i, (src, dst) in enumerate(
            [
                (go_ref, go_hbm),
                (qg_ref, qg_hbm),
                (fg_ref, fg_hbm),
                (kg_ref, kg_hbm),
                (vg_ref, vg_hbm),
                (in_s, sums_hbm),
            ]
        )
    ]
    arrived(in_gq, 3)
    unpaired(in_gq, go_ref, qg_ref)
    writes[0].start()
    writes[1].start()
    arrived(in_f, 4)
    fg_ref[...] = in_f[...].reshape(rows, width).T
    writes[2].start()
    arrived(in_kv, 5)
    unpaired(in_kv, kg_ref, vg_ref)
    writes[3].start()
    writes[4].start()
    arrived(in_s, 6)
    writes[5].start()
    for copy in writes:
        copy.wait()

    for index, source in enumerate([send_h, send_kv, send_qc, out_gq, out_f, out_kv, out_s]):
        sent(source, index)


def deliver(go, qg, kg, vg, fg, sums, go_out, qg_out, kg_out, vg_out, fg_out, taps_out, gain_out, held, sem):
    nseq, group = sums.shape[0], gain_out.shape[1] // sums.shape[0]
    pairs = [(sums, held), (go, go_out), (qg, qg_out), (kg, kg_out), (vg, vg_out), (fg, fg_out)]
    copies = [pltpu.make_async_copy(src, dst, sem.at[i]) for i, (src, dst) in enumerate(pairs)]
    for copy in copies:
        copy.start()
    copies[0].wait()
    table = held[...].reshape(nseq, 128)
    turned = jnp.concatenate(
        [table if r == 0 else pltpu.roll(table, 128 - group * r, 1) for r in range(10)], axis=0
    )
    width = gain_out.shape[1]
    channel = lax.broadcasted_iota(jnp.int32, (128, width), 1)
    pick = lax.rem(channel, group) == lax.broadcasted_iota(jnp.int32, (128, width), 0)
    wide = jnp.dot(
        turned,
        pick.astype(F32),
        preferred_element_type=F32,
        precision=lax.Precision.HIGHEST,
    ).reshape(10, nseq, width)
    owner = lax.div(lax.broadcasted_iota(jnp.int32, (nseq, width), 1), group)
    keep = owner == lax.broadcasted_iota(jnp.int32, (nseq, width), 0)
    rows = [jnp.sum(jnp.where(keep, wide[r], 0.0), axis=0, keepdims=True) for r in range(10)]
    for r in range(9):
        taps_out[r // 3, r % 3 : r % 3 + 1, :] = rows[r]
    gain_out[...] = rows[9]
    for copy in copies[1:]:
        copy.wait()


def per_device(query_rows, key_rows, value_rows, long_filter, short_taps, skip_gain, cotangent):
    rows, channels = query_rows.shape
    nseq, nchan = lax.axis_size("seq"), lax.axis_size("chan")
    group = channels // nseq
    scale = 1.0 / math.sqrt(rows * nseq)
    tables = [jnp.asarray(t) for t in transform_tables(nseq, rows, group)]
    block = jax.ShapeDtypeStruct((rows, channels), BF16)
    vmem = pl.BlockSpec(memory_space=pltpu.VMEM)
    hbm = pl.BlockSpec(memory_space=pltpu.HBM)
    one, two = (nseq, group, rows), (nseq, 2 * group, rows)
    spec = pltpu.VMEM((2, nseq * group, rows), F32)
    outs = pl.pallas_call(
        functools.partial(kernel, nseq, nchan, group, scale),
        out_shape=(
            block,
            block,
            block,
            block,
            jax.ShapeDtypeStruct((rows, channels), F32),
            jax.ShapeDtypeStruct((nseq, 1, 128), F32),
        ),
        in_specs=[hbm] * 11,
        out_specs=[hbm] * 6,
        scratch_shapes=[pltpu.VMEM((rows, channels), BF16)] * 4
        + [
            pltpu.VMEM((rows, channels), F32),
            pltpu.VMEM((3, 3, group), F32),
            pltpu.VMEM((1, group), F32),
        ]
        + [pltpu.VMEM(t.shape, t.dtype) for t in tables]
        + [
            pltpu.VMEM(one, F32),
            pltpu.VMEM(two, BF16),
            pltpu.VMEM(two, BF16),
            pltpu.VMEM(one, F32),
            pltpu.VMEM(two, BF16),
            pltpu.VMEM(two, BF16),
            pltpu.VMEM((3, 3, group), F32),
            pltpu.VMEM((1, group), F32),
            pltpu.VMEM(two, BF16),
            pltpu.VMEM(one, F32),
            pltpu.VMEM(two, BF16),
            pltpu.VMEM((nseq, 1, 128), F32),
            pltpu.VMEM(two, BF16),
            pltpu.VMEM(one, F32),
            pltpu.VMEM(two, BF16),
            pltpu.VMEM((nseq, 1, 128), F32),
        ]
        + [pltpu.VMEM(one, F32)] * 6
        + [pltpu.VMEM((2,) + one, F32)] * 3
        + [spec] * 3
        + [pltpu.VMEM((rows, channels), BF16)] * 4
        + [pltpu.VMEM((rows, channels), F32)]
        + [
            pltpu.SemaphoreType.DMA((7,)),
            pltpu.SemaphoreType.DMA((6,)),
            pltpu.SemaphoreType.DMA((4,)),
            pltpu.SemaphoreType.DMA((7,)),
            pltpu.SemaphoreType.DMA((7,)),
            pltpu.SemaphoreType.DMA((4,)),
        ],
        compiler_params=pltpu.CompilerParams(
            collective_id=0, has_side_effects=True, vmem_limit_bytes=60 << 20
        ),
        name="hyena",
    )(query_rows, key_rows, value_rows, cotangent, long_filter, short_taps, skip_gain[None], *tables)
    moved = pl.pallas_call(
        deliver,
        out_shape=tuple(jax.ShapeDtypeStruct(o.shape, o.dtype) for o in outs[:5])
        + (
            jax.ShapeDtypeStruct((3, 3, channels), F32),
            jax.ShapeDtypeStruct((1, channels), F32),
        ),
        in_specs=[hbm] * 6,
        out_specs=[hbm] * 5 + [vmem] * 2,
        scratch_shapes=[pltpu.VMEM((nseq, 1, 128), F32), pltpu.SemaphoreType.DMA((6,))],
        name="deliver",
    )(*outs)
    return tuple(moved[:6]) + (moved[6].reshape(channels),)


def solution(mesh):
    in_specs = (
        P("seq", "chan"),
        P("seq", "chan"),
        P("seq", "chan"),
        P("seq", "chan"),
        P(None, None, ("seq", "chan")),
        P(("seq", "chan")),
        P("seq", "chan"),
    )
    out_specs = (
        P("seq", "chan"),
        P("seq", "chan"),
        P("seq", "chan"),
        P("seq", "chan"),
        P("seq", "chan"),
        P(None, None, "chan"),
        P("chan"),
    )
    return jax.shard_map(
        per_device, mesh=mesh, in_specs=in_specs, out_specs=out_specs, check_vma=False
    )
```

```python
import functools
import math

import jax
import jax.numpy as jnp
import ml_dtypes
import numpy as np
from jax import lax
from jax.experimental import pallas as pl
from jax.experimental.pallas import tpu as pltpu
from jax.sharding import PartitionSpec as P

F32 = jnp.float32
BF16 = jnp.bfloat16
MESH = pl.DeviceIdType.MESH


def halves(table):
    high = table.astype(np.float32).astype(ml_dtypes.bfloat16)
    low = (table - high.astype(np.float64)).astype(np.float32).astype(ml_dtypes.bfloat16)
    return np.stack([high, low])


def transform_tables(blocks, width, group):
    total = blocks * width
    shifted = np.arange(blocks) - 0.25
    outer = 2.0 * np.pi / blocks * np.outer(shifted, np.arange(blocks))
    eye = np.eye(group)
    left = np.concatenate([np.kron(np.cos(outer), eye), np.kron(-np.sin(outer), eye)], axis=0)
    back = left.T / total
    inner = 2.0 * np.pi / width * (np.outer(np.arange(width), np.arange(width)) % width)
    right = np.stack([halves(np.cos(inner)), halves(np.sin(inner))])
    turn = 2.0 * np.pi / total * np.outer(shifted, np.arange(width))
    twist = np.stack([np.cos(turn), np.sin(turn)]).astype(np.float32)
    twist = np.repeat(twist, group, axis=1)
    return halves(left), halves(back), right, twist


def split(value):
    high = value.astype(BF16)
    return high, (value - high.astype(F32)).astype(BF16)


def dot(left, right):
    return jnp.dot(left, right, preferred_element_type=F32)


def dot3(left, right):
    return dot(left[0], right[0]) + dot(left[0], right[1]) + dot(left[1], right[0])


def delayed(value, steps):
    before = jnp.concatenate([jnp.zeros_like(value[:1]), value[:-1]], axis=0)
    lane = lax.broadcasted_iota(jnp.int32, value.shape, 2)
    return jnp.where(
        lane < steps, pltpu.roll(before, steps, 2), pltpu.roll(value, steps, 2)
    )


def advanced(value, steps):
    width = value.shape[2]
    after = jnp.concatenate([value[1:], jnp.zeros_like(value[:1])], axis=0)
    lane = lax.broadcasted_iota(jnp.int32, value.shape, 2)
    return jnp.where(
        lane >= width - steps,
        pltpu.roll(after, width - steps, 2),
        pltpu.roll(value, width - steps, 2),
    )


def total_of(value):
    return jnp.sum(jnp.sum(value, axis=0), axis=1, keepdims=True)


def kernel(
    nseq,
    nchan,
    group,
    scale,
    q_hbm,
    k_hbm,
    v_hbm,
    c_hbm,
    h_hbm,
    taps_hbm,
    gain_hbm,
    left_hbm,
    back_hbm,
    right_hbm,
    twist_hbm,
    go_ref,
    qg_ref,
    kg_ref,
    vg_ref,
    fg_ref,
    sums_ref,
    q_ref,
    k_ref,
    v_ref,
    c_ref,
    h_ref,
    taps_own,
    gain_own,
    left,
    back,
    right,
    twist,
    send_h,
    send_kv,
    send_qc,
    got_h,
    got_kv,
    got_qc,
    taps_ref,
    gain_ref,
    out_gq,
    out_f,
    out_kv,
    out_s,
    in_gq,
    in_f,
    in_kv,
    in_s,
    x_q,
    x_k,
    x_v,
    x_c,
    x_p,
    x_g,
    d_q,
    d_k,
    d_v,
    spec_h,
    spec_p,
    spec_g,
    input_sem,
    table_sem,
    send_sem,
    recv_sem,
    side_sem,
):
    me = lax.axis_index("seq")
    mine = lax.axis_index("chan")
    rows, width = q_hbm.shape

    inputs = [
        pltpu.make_async_copy(src, dst, input_sem.at[i])
        for i, (src, dst) in enumerate(
            [
                (h_hbm, h_ref),
                (k_hbm, k_ref),
                (v_hbm, v_ref),
                (q_hbm, q_ref),
                (c_hbm, c_ref),
                (taps_hbm, taps_own),
                (gain_hbm, gain_own),
            ]
        )
    ]
    tables = [
        pltpu.make_async_copy(src, dst, table_sem.at[i])
        for i, (src, dst) in enumerate(
            [(left_hbm, left), (twist_hbm, twist), (right_hbm, right), (back_hbm, back)]
        )
    ]
    for copy in inputs + tables:
        copy.start()

    per = nseq // nchan
    to_seq = nchan * lax.rem(me, per) + mine
    to_chan = lax.div(me, per)
    from_seq = per * mine + lax.div(me, nchan)
    from_chan = lax.rem(me, nchan)
    stays = jnp.logical_and(to_seq == me, to_chan == mine)

    barrier = pltpu.get_barrier_semaphore()

    def greet(step, carry):
        peer = lax.rem(me + step, nseq)
        pl.semaphore_signal(barrier, inc=1, device_id=(peer, mine), device_id_type=MESH)
        return carry

    lax.fori_loop(1, nseq, greet, 0)

    @pl.when(jnp.logical_not(stays))
    def _():
        pl.semaphore_signal(
            barrier, inc=1, device_id=(from_seq, from_chan), device_id_type=MESH
        )

    inputs[0].wait()
    send_h[...] = h_ref[...].T.reshape(nseq, group, width)

    @pl.when(stays)
    def _():
        pl.semaphore_wait(barrier, nseq - 1)

    @pl.when(jnp.logical_not(stays))
    def _():
        pl.semaphore_wait(barrier, nseq)

    def copy_to(source, target, index, peer):
        return pltpu.make_async_remote_copy(
            src_ref=source.at[peer],
            dst_ref=target.at[me],
            send_sem=send_sem.at[index],
            recv_sem=recv_sem.at[index],
            device_id=(peer, mine),
            device_id_type=MESH,
        )

    def send_all(source, target, index):
        def body(step, carry):
            copy_to(source, target, index, lax.rem(me + step, nseq)).start()
            return carry

        lax.fori_loop(1, nseq, body, 0)
        target[me] = source[me]

    def arrived(target, index):
        part = target.at[pl.ds(0, nseq - 1)]
        pltpu.make_async_copy(part, part, recv_sem.at[index]).wait()

    def sent(source, index):
        part = source.at[pl.ds(0, nseq - 1)]
        pltpu.make_async_copy(part, part, send_sem.at[index]).wait()

    send_all(send_h, got_h, 0)

    side_copies = [
        pltpu.make_async_remote_copy(
            src_ref=src,
            dst_ref=dst,
            send_sem=side_sem.at[i],
            recv_sem=side_sem.at[2 + i],
            device_id=(to_seq, to_chan),
            device_id_type=MESH,
        )
        for i, (src, dst) in enumerate([(taps_own, taps_ref), (gain_own, gain_ref)])
    ]
    inputs[5].wait()
    inputs[6].wait()

    @pl.when(jnp.logical_not(stays))
    def _():
        for copy in side_copies:
            copy.start()

    @pl.when(stays)
    def _():
        taps_ref[...] = taps_own[...]
        gain_ref[...] = gain_own[...]

    def paired(first, second):
        shape = (nseq, group, width)
        one = first[...].astype(F32).T.reshape(shape)
        two = second[...].astype(F32).T.reshape(shape)
        return jnp.concatenate([one, two], axis=1).astype(BF16)

    inputs[1].wait()
    inputs[2].wait()
    send_kv[...] = paired(k_ref, v_ref)
    send_all(send_kv, got_kv, 1)
    inputs[3].wait()
    inputs[4].wait()
    send_qc[...] = paired(q_ref, c_ref)
    send_all(send_qc, got_qc, 2)

    for copy in tables:
        copy.wait()

    def forward(signal, spec):
        parts = split(signal.reshape(rows, width))
        wave = dot3((left[0], left[1]), parts)
        real, imag = wave[:rows], wave[rows:]
        cosine, sine = twist[0], twist[1]
        turned_real = split(real * cosine + imag * sine)
        turned_imag = split(imag * cosine - real * sine)
        cos_parts = (right[0, 0], right[0, 1])
        sin_parts = (right[1, 0], right[1, 1])
        spec[0] = dot3(turned_real, cos_parts) + dot3(turned_imag, sin_parts)
        spec[1] = dot3(turned_imag, cos_parts) - dot3(turned_real, sin_parts)

    def inverse(real, imag):
        real, imag = split(real), split(imag)
        cos_parts = (right[0, 0], right[0, 1])
        sin_parts = (right[1, 0], right[1, 1])
        wave_real = dot3(real, cos_parts) - dot3(imag, sin_parts)
        wave_imag = dot3(imag, cos_parts) + dot3(real, sin_parts)
        cosine, sine = twist[0], twist[1]
        turned_real = split(wave_real * cosine - wave_imag * sine)
        turned_imag = split(wave_imag * cosine + wave_real * sine)
        signal = dot3((back[0, :, :rows], back[1, :, :rows]), turned_real)
        signal = signal + dot3((back[0, :, rows:], back[1, :, rows:]), turned_imag)
        return signal.reshape(nseq, group, width)

    arrived(got_h, 0)
    forward(got_h[...], spec_h)

    @pl.when(jnp.logical_not(stays))
    def _():
        for copy in side_copies:
            copy.wait()

    diagonal = lax.broadcasted_iota(jnp.int32, (group, group), 0) == lax.broadcasted_iota(
        jnp.int32, (group, group), 1
    )

    def column(row):
        spread_out = jnp.broadcast_to(row, (group, group))
        return jnp.sum(jnp.where(diagonal, spread_out, 0.0), axis=1, keepdims=True)

    taps = [[column(taps_ref[s, i : i + 1, :]) for i in range(3)] for s in range(3)]
    gain = column(gain_ref[...])

    def short(value, keep, coeffs):
        one, two = delayed(value, 1), delayed(value, 2)
        keep[0] = one
        keep[1] = two
        return coeffs[0] * value + coeffs[1] * one + coeffs[2] * two

    arrived(got_kv, 1)
    both = got_kv[...].astype(F32)
    x_k[...] = both[:, :group]
    x_v[...] = both[:, group:]
    key_conv = short(x_k[...], d_k, taps[1])
    value_conv = short(x_v[...], d_v, taps[2])
    x_p[...] = key_conv * value_conv
    forward(x_p[...], spec_p)
    h_re, h_im = spec_h[0], spec_h[1]
    p_re, p_im = spec_p[0], spec_p[1]
    mixed = inverse(p_re * h_re - p_im * h_im, p_re * h_im + p_im * h_re)
    mixed = mixed + gain * x_p[...]

    arrived(got_qc, 2)
    both = got_qc[...].astype(F32)
    x_q[...] = both[:, :group]
    x_c[...] = both[:, group:]
    query_conv = short(x_q[...], d_q, taps[0])
    x_g[...] = x_c[...] * query_conv
    query_conv_grad = x_c[...] * mixed

    def spread(grad, coeffs):
        return (
            coeffs[0] * grad + coeffs[1] * advanced(grad, 1) + coeffs[2] * advanced(grad, 2)
        )

    out_gq[...] = jnp.concatenate(
        [query_conv * mixed, spread(query_conv_grad, taps[0])], axis=1
    ).astype(BF16)
    send_all(out_gq, in_gq, 3)
    sums = [
        total_of(query_conv_grad * x_q[...]),
        total_of(query_conv_grad * d_q[0]),
        total_of(query_conv_grad * d_q[1]),
    ]

    forward(x_g[...], spec_g)
    g_re, g_im = spec_g[0], spec_g[1]
    p_re, p_im = spec_p[0], spec_p[1]
    out_f[...] = scale * inverse(p_re * g_re + p_im * g_im, p_re * g_im - p_im * g_re)
    send_all(out_f, in_f, 4)
    h_re, h_im = spec_h[0], spec_h[1]
    product_grad = inverse(h_re * g_re + h_im * g_im, h_re * g_im - h_im * g_re)
    product_grad = product_grad + gain * x_g[...]

    key_conv = taps[1][0] * x_k[...] + taps[1][1] * d_k[0] + taps[1][2] * d_k[1]
    value_conv = taps[2][0] * x_v[...] + taps[2][1] * d_v[0] + taps[2][2] * d_v[1]
    key_conv_grad = product_grad * value_conv
    value_conv_grad = product_grad * key_conv
    out_kv[...] = jnp.concatenate(
        [spread(key_conv_grad, taps[1]), spread(value_conv_grad, taps[2])], axis=1
    ).astype(BF16)
    send_all(out_kv, in_kv, 5)
    sums += [
        total_of(key_conv_grad * x_k[...]),
        total_of(key_conv_grad * d_k[0]),
        total_of(key_conv_grad * d_k[1]),
        total_of(value_conv_grad * x_v[...]),
        total_of(value_conv_grad * d_v[0]),
        total_of(value_conv_grad * d_v[1]),
        total_of(x_g[...] * x_p[...]),
    ]
    lane = lax.broadcasted_iota(jnp.int32, (group, 128), 1)
    place = lax.broadcasted_iota(jnp.int32, (group, 128), 0)
    packed = jnp.zeros((group, 128), F32)
    for index, value in enumerate(sums):
        packed = jnp.where(lane == group * index + place, value, packed)
    packed = scale * jnp.sum(packed, axis=0, keepdims=True)
    out_s[...] = jnp.broadcast_to(packed[None], out_s.shape)
    send_all(out_s, in_s, 6)

    def unpaired(source, first, second):
        both = source[...].astype(F32)
        first[...] = both[:, :group].reshape(rows, width).T.astype(BF16)
        second[...] = both[:, group:].reshape(rows, width).T.astype(BF16)

    arrived(in_gq, 3)
    unpaired(in_gq, go_ref, qg_ref)
    arrived(in_f, 4)
    fg_ref[...] = in_f[...].reshape(rows, width).T
    arrived(in_kv, 5)
    unpaired(in_kv, kg_ref, vg_ref)
    arrived(in_s, 6)
    sums_ref[...] = in_s[...]
    for index, source in enumerate([send_h, send_kv, send_qc, out_gq, out_f, out_kv, out_s]):
        sent(source, index)


def deliver(go, qg, kg, vg, fg, sums, go_out, qg_out, kg_out, vg_out, fg_out, taps_out, gain_out, sem):
    nseq, group = sums.shape[0], gain_out.shape[1] // sums.shape[0]
    pairs = [(go, go_out), (qg, qg_out), (kg, kg_out), (vg, vg_out), (fg, fg_out)]
    copies = [pltpu.make_async_copy(src, dst, sem.at[i]) for i, (src, dst) in enumerate(pairs)]
    for copy in copies:
        copy.start()
    table = sums[...].reshape(nseq, 128)
    turned = jnp.concatenate(
        [table if r == 0 else pltpu.roll(table, 128 - group * r, 1) for r in range(10)], axis=0
    )
    width = gain_out.shape[1]
    channel = lax.broadcasted_iota(jnp.int32, (128, width), 1)
    pick = lax.rem(channel, group) == lax.broadcasted_iota(jnp.int32, (128, width), 0)
    wide = jnp.dot(
        turned,
        pick.astype(F32),
        preferred_element_type=F32,
        precision=lax.Precision.HIGHEST,
    ).reshape(10, nseq, width)
    owner = lax.div(lax.broadcasted_iota(jnp.int32, (nseq, width), 1), group)
    keep = owner == lax.broadcasted_iota(jnp.int32, (nseq, width), 0)
    rows = [jnp.sum(jnp.where(keep, wide[r], 0.0), axis=0, keepdims=True) for r in range(10)]
    for r in range(9):
        taps_out[r // 3, r % 3 : r % 3 + 1, :] = rows[r]
    gain_out[...] = rows[9]
    for copy in copies:
        copy.wait()


def per_device(query_rows, key_rows, value_rows, long_filter, short_taps, skip_gain, cotangent):
    rows, channels = query_rows.shape
    nseq, nchan = lax.axis_size("seq"), lax.axis_size("chan")
    group = channels // nseq
    scale = 1.0 / math.sqrt(rows * nseq)
    tables = [jnp.asarray(t) for t in transform_tables(nseq, rows, group)]
    block = jax.ShapeDtypeStruct((rows, channels), BF16)
    vmem = pl.BlockSpec(memory_space=pltpu.VMEM)
    hbm = pl.BlockSpec(memory_space=pltpu.HBM)
    one, two = (nseq, group, rows), (nseq, 2 * group, rows)
    spec = pltpu.VMEM((2, nseq * group, rows), F32)
    outs = pl.pallas_call(
        functools.partial(kernel, nseq, nchan, group, scale),
        out_shape=(
            block,
            block,
            block,
            block,
            jax.ShapeDtypeStruct((rows, channels), F32),
            jax.ShapeDtypeStruct((nseq, 1, 128), F32),
        ),
        in_specs=[hbm] * 11,
        out_specs=[vmem] * 6,
        scratch_shapes=[pltpu.VMEM((rows, channels), BF16)] * 4
        + [
            pltpu.VMEM((rows, channels), F32),
            pltpu.VMEM((3, 3, group), F32),
            pltpu.VMEM((1, group), F32),
        ]
        + [pltpu.VMEM(t.shape, t.dtype) for t in tables]
        + [
            pltpu.VMEM(one, F32),
            pltpu.VMEM(two, BF16),
            pltpu.VMEM(two, BF16),
            pltpu.VMEM(one, F32),
            pltpu.VMEM(two, BF16),
            pltpu.VMEM(two, BF16),
            pltpu.VMEM((3, 3, group), F32),
            pltpu.VMEM((1, group), F32),
            pltpu.VMEM(two, BF16),
            pltpu.VMEM(one, F32),
            pltpu.VMEM(two, BF16),
            pltpu.VMEM((nseq, 1, 128), F32),
            pltpu.VMEM(two, BF16),
            pltpu.VMEM(one, F32),
            pltpu.VMEM(two, BF16),
            pltpu.VMEM((nseq, 1, 128), F32),
        ]
        + [pltpu.VMEM(one, F32)] * 6
        + [pltpu.VMEM((2,) + one, F32)] * 3
        + [spec] * 3
        + [
            pltpu.SemaphoreType.DMA((7,)),
            pltpu.SemaphoreType.DMA((4,)),
            pltpu.SemaphoreType.DMA((7,)),
            pltpu.SemaphoreType.DMA((7,)),
            pltpu.SemaphoreType.DMA((4,)),
        ],
        compiler_params=pltpu.CompilerParams(
            collective_id=0, has_side_effects=True, vmem_limit_bytes=40 << 20
        ),
        name="hyena",
    )(
        *[
            pltpu.with_memory_space_constraint(x, pltpu.HBM)
            for x in (
                query_rows, key_rows, value_rows, cotangent, long_filter, short_taps,
                skip_gain[None], *tables,
            )
        ]
    )
    moved = pl.pallas_call(
        deliver,
        out_shape=tuple(jax.ShapeDtypeStruct(o.shape, o.dtype) for o in outs[:5])
        + (
            jax.ShapeDtypeStruct((3, 3, channels), F32),
            jax.ShapeDtypeStruct((1, channels), F32),
        ),
        in_specs=[vmem] * 6,
        out_specs=[hbm] * 5 + [vmem] * 2,
        scratch_shapes=[pltpu.SemaphoreType.DMA((5,))],
        compiler_params=pltpu.CompilerParams(vmem_limit_bytes=16 << 20),
        name="deliver",
    )(*outs)
    return tuple(moved[:6]) + (moved[6].reshape(channels),)


def solution(mesh):
    in_specs = (
        P("seq", "chan"),
        P("seq", "chan"),
        P("seq", "chan"),
        P("seq", "chan"),
        P(None, None, ("seq", "chan")),
        P(("seq", "chan")),
        P("seq", "chan"),
    )
    out_specs = (
        P("seq", "chan"),
        P("seq", "chan"),
        P("seq", "chan"),
        P("seq", "chan"),
        P("seq", "chan"),
        P(None, None, "chan"),
        P("chan"),
    )
    return jax.shard_map(
        per_device, mesh=mesh, in_specs=in_specs, out_specs=out_specs, check_vma=False
    )
```

```python
import functools
import math
import types

import jax
import jax.numpy as jnp
import ml_dtypes
import numpy as np
from jax import lax
from jax.experimental import pallas as pl
from jax.experimental.pallas import tpu as pltpu
from jax.sharding import PartitionSpec as P

F32 = jnp.float32
BF16 = jnp.bfloat16
MESH = pl.DeviceIdType.MESH
REACH = 125.0 * math.log(2.0)


def halves(table):
    high = table.astype(np.float32).astype(ml_dtypes.bfloat16)
    low = (table - high.astype(np.float64)).astype(np.float32).astype(ml_dtypes.bfloat16)
    return np.stack([high, low])


def transform_tables(blocks, width, group):
    total = blocks * width
    shifted = np.arange(blocks) - 0.25
    outer = 2.0 * np.pi / blocks * np.outer(shifted, np.arange(blocks))
    eye = np.eye(group)
    left = np.concatenate([np.kron(np.cos(outer), eye), np.kron(-np.sin(outer), eye)], axis=0)
    back = left.T / total
    inner = 2.0 * np.pi / width * (np.outer(np.arange(width), np.arange(width)) % width)
    right = np.stack([halves(np.cos(inner)), halves(np.sin(inner))])
    turn = 2.0 * np.pi / total * np.outer(shifted, np.arange(width))
    twist = np.stack([np.cos(turn), np.sin(turn)]).astype(np.float32)
    twist = np.repeat(twist, group, axis=1)
    return halves(left), halves(back), right, twist


def split(value):
    high = value.astype(BF16)
    return high, (value - high.astype(F32)).astype(BF16)


def dot(left, right):
    return jnp.dot(left, right, preferred_element_type=F32)


def dot3(left, right):
    return dot(left[0], right[0]) + dot(left[0], right[1]) + dot(left[1], right[0])


def delayed(value, steps):
    before = jnp.concatenate([jnp.zeros_like(value[:1]), value[:-1]], axis=0)
    lane = lax.broadcasted_iota(jnp.int32, value.shape, 2)
    return jnp.where(
        lane < steps, pltpu.roll(before, steps, 2), pltpu.roll(value, steps, 2)
    )


def later(value, head, steps):
    return pltpu.roll(jnp.concatenate([head, value], axis=0), steps, 0)[head.shape[0] :]


def block_ends(grad, coeffs):
    half = grad.shape[2] // 2
    low, high = grad[:, :, :half], grad[:, :, half:]
    after = jnp.concatenate([low[1:], jnp.zeros_like(low[:1])], axis=0)
    lane = lax.broadcasted_iota(jnp.int32, high.shape, 2)
    total = coeffs[0] * high
    for steps in (1, 2):
        moved = jnp.where(
            lane < half - steps,
            pltpu.roll(high, half - steps, 2),
            pltpu.roll(after, half - steps, 2),
        )
        total = total + coeffs[steps] * moved
    return [
        jnp.sum(jnp.where(lane == half - back, total, 0.0), axis=2, keepdims=True)
        for back in (2, 1)
    ]


def total_of(value):
    return jnp.sum(jnp.sum(value, axis=0), axis=1, keepdims=True)


def encode(value):
    peak = jnp.maximum(jnp.max(jnp.abs(value), axis=2, keepdims=True), 1e-30)
    code = jnp.exp(jnp.abs(value) * (2.0 * REACH / peak) - REACH)
    code = jnp.where(value < 0.0, -code, code)
    half = value.shape[2] // 2
    return jnp.concatenate([code[:, :, :half], code[:, :, half:]], axis=1).astype(BF16), peak


def decode(code, peak):
    group = code.shape[1] // 2
    code = code.astype(F32)
    code = jnp.concatenate([code[:, :group], code[:, group:]], axis=2)
    size = (jnp.log(jnp.abs(code)) + REACH) * (peak * (0.5 / REACH))
    return jnp.where(code < 0.0, -size, size)


def field_mask(group, field):
    lane = lax.broadcasted_iota(jnp.int32, (1, group, 128), 2)
    return lane == group * field + lax.broadcasted_iota(jnp.int32, (1, group, 128), 1)


def packed_rows(count, group, fields):
    wide = jnp.zeros((count, group, 128), F32)
    for field, value in fields.items():
        wide = jnp.where(field_mask(group, field), value, wide)
    return jnp.sum(wide, axis=1, keepdims=True)


def unpacked(rows, group, field):
    wide = jnp.broadcast_to(rows, (rows.shape[0], group, 128))
    return jnp.sum(jnp.where(field_mask(group, field), wide, 0.0), axis=2, keepdims=True)


def channel_rows(table, count, group):
    owners = table.shape[0]
    width = owners * group
    turned = jnp.concatenate(
        [table if f == 0 else pltpu.roll(table, 128 - group * f, 1) for f in range(count)],
        axis=0,
    )
    channel = lax.broadcasted_iota(jnp.int32, (128, width), 1)
    pick = lax.rem(channel, group) == lax.broadcasted_iota(jnp.int32, (128, width), 0)
    wide = jnp.dot(
        turned,
        pick.astype(F32),
        preferred_element_type=F32,
        precision=lax.Precision.HIGHEST,
    ).reshape(count, owners, width)
    owner = lax.div(lax.broadcasted_iota(jnp.int32, (owners, width), 1), group)
    keep = owner == lax.broadcasted_iota(jnp.int32, (owners, width), 0)
    return [jnp.sum(jnp.where(keep, wide[f], 0.0), axis=0, keepdims=True) for f in range(count)]


HALO = 16
MESSAGES = ("kv", "h", "hs", "qc", "t", "m", "ms", "p", "ps", "f", "fs", "s")


def kernel(names, nseq, nchan, group, scale, *refs):
    r = types.SimpleNamespace(**dict(zip(names, refs, strict=True)))
    me = lax.axis_index("seq")
    mine = lax.axis_index("chan")
    rows, width = r.q_hbm.shape
    number = {name: i for i, name in enumerate(MESSAGES)}

    fetched = {}
    pairs = [("k", "k"), ("v", "v"), ("h", "h"), ("q", "q"), ("c", "c"), ("taps", "taps_own")]
    pairs += [("gain", "gain_own"), ("left", "left"), ("twist", "twist")]
    pairs += [("right", "right"), ("back", "back")]
    for i, (src, dst) in enumerate(pairs):
        fetched[src] = pltpu.make_async_copy(
            getattr(r, src + "_hbm"), getattr(r, dst), r.fetch_sem.at[i]
        )
        fetched[src].start()

    per = nseq // nchan
    to_seq = nchan * lax.rem(me, per) + mine
    to_chan = lax.div(me, per)
    from_seq = per * mine + lax.div(me, nchan)
    from_chan = lax.rem(me, nchan)
    stays = jnp.logical_and(to_seq == me, to_chan == mine)

    barrier = pltpu.get_barrier_semaphore()

    def greet(step, carry):
        peer = lax.rem(me + step, nseq)
        pl.semaphore_signal(barrier, inc=1, device_id=(peer, mine), device_id_type=MESH)
        return carry

    lax.fori_loop(1, nseq, greet, 0)

    @pl.when(jnp.logical_not(stays))
    def _():
        pl.semaphore_signal(
            barrier, inc=1, device_id=(from_seq, from_chan), device_id_type=MESH
        )

    shape = (nseq, group, width)

    def paired(first, second):
        one = first[...].astype(F32).T.reshape(shape)
        two = second[...].astype(F32).T.reshape(shape)
        return jnp.concatenate([one, two], axis=1).astype(BF16)

    fetched["k"].wait()
    fetched["v"].wait()
    r.send_kv[...] = paired(r.k, r.v)

    @pl.when(stays)
    def _():
        pl.semaphore_wait(barrier, nseq - 1)

    @pl.when(jnp.logical_not(stays))
    def _():
        pl.semaphore_wait(barrier, nseq)

    def send_all(name):
        source, target = getattr(r, "send_" + name), getattr(r, "got_" + name)
        index = number[name]

        def body(step, carry):
            peer = lax.rem(me + step, nseq)
            pltpu.make_async_remote_copy(
                src_ref=source.at[peer],
                dst_ref=target.at[me],
                send_sem=r.send_sem.at[index],
                recv_sem=r.recv_sem.at[index],
                device_id=(peer, mine),
                device_id_type=MESH,
            ).start()
            return carry

        lax.fori_loop(1, nseq, body, 0)
        target[me] = source[me]

    def arrived(name):
        part = getattr(r, "got_" + name).at[pl.ds(0, nseq - 1)]
        pltpu.make_async_copy(part, part, r.recv_sem.at[number[name]]).wait()

    def sent(name):
        part = getattr(r, "send_" + name).at[pl.ds(0, nseq - 1)]
        pltpu.make_async_copy(part, part, r.send_sem.at[number[name]]).wait()

    send_all("kv")

    side_copies = [
        pltpu.make_async_remote_copy(
            src_ref=src,
            dst_ref=dst,
            send_sem=r.side_sem.at[i],
            recv_sem=r.side_sem.at[2 + i],
            device_id=(to_seq, to_chan),
            device_id_type=MESH,
        )
        for i, (src, dst) in enumerate([(r.taps_own, r.taps), (r.gain_own, r.gain)])
    ]
    fetched["taps"].wait()
    fetched["gain"].wait()

    @pl.when(jnp.logical_not(stays))
    def _():
        for copy in side_copies:
            copy.start()

    @pl.when(stays)
    def _():
        r.taps[...] = r.taps_own[...]
        r.gain[...] = r.gain_own[...]

    fetched["h"].wait()
    r.send_h[...], peak = encode(r.h[...].T.reshape(shape))
    r.send_hs[...] = packed_rows(nseq, group, {0: peak})
    send_all("h")
    send_all("hs")

    fetched["q"].wait()
    fetched["c"].wait()
    r.send_qc[...] = paired(r.q, r.c)
    send_all("qc")

    halo_copies = [
        pltpu.make_async_remote_copy(
            src_ref=src.at[pl.ds(rows - HALO, HALO)],
            dst_ref=r.halo.at[i],
            send_sem=r.halo_sem.at[i],
            recv_sem=r.halo_sem.at[3 + i],
            device_id=(lax.rem(me + 1, nseq), mine),
            device_id_type=MESH,
        )
        for i, src in enumerate([r.q, r.k, r.v])
    ]

    @pl.when(me < nseq - 1)
    def _():
        for copy in halo_copies:
            copy.start()

    @pl.when(me == 0)
    def _():
        r.halo[...] = jnp.zeros(r.halo.shape, BF16)

    @pl.when(jnp.logical_not(stays))
    def _():
        for copy in side_copies:
            copy.wait()

    diagonal = field_mask(group, 0)[0, :, :group]

    def column(row):
        spread_out = jnp.broadcast_to(row, (group, group))
        return jnp.sum(jnp.where(diagonal, spread_out, 0.0), axis=1, keepdims=True)

    taps = [[column(r.taps[s, i : i + 1, :]) for i in range(3)] for s in range(3)]
    gain = column(r.gain[...])
    r.send_t[...] = jnp.broadcast_to(
        packed_rows(1, group, {3 * s + i: taps[s][i] for s in range(3) for i in range(3)}),
        r.send_t.shape,
    )
    send_all("t")

    for name in ("left", "twist", "right", "back"):
        fetched[name].wait()

    def forward(signal, spec):
        parts = split(signal.reshape(rows, width))
        wave = dot3((r.left[0], r.left[1]), parts)
        real, imag = wave[:rows], wave[rows:]
        cosine, sine = r.twist[0], r.twist[1]
        turned_real = split(real * cosine + imag * sine)
        turned_imag = split(imag * cosine - real * sine)
        cos_parts = (r.right[0, 0], r.right[0, 1])
        sin_parts = (r.right[1, 0], r.right[1, 1])
        spec[0] = dot3(turned_real, cos_parts) + dot3(turned_imag, sin_parts)
        spec[1] = dot3(turned_imag, cos_parts) - dot3(turned_real, sin_parts)

    def inverse(left_spec, right_spec, conjugate):
        a_re, a_im, b_re, b_im = left_spec[0], left_spec[1], right_spec[0], right_spec[1]
        if conjugate:
            real, imag = a_re * b_re + a_im * b_im, a_re * b_im - a_im * b_re
        else:
            real, imag = a_re * b_re - a_im * b_im, a_re * b_im + a_im * b_re
        real, imag = split(real), split(imag)
        cos_parts = (r.right[0, 0], r.right[0, 1])
        sin_parts = (r.right[1, 0], r.right[1, 1])
        wave_real = dot3(real, cos_parts) - dot3(imag, sin_parts)
        wave_imag = dot3(imag, cos_parts) + dot3(real, sin_parts)
        cosine, sine = r.twist[0], r.twist[1]
        turned_real = split(wave_real * cosine - wave_imag * sine)
        turned_imag = split(wave_imag * cosine + wave_real * sine)
        signal = dot3((r.back[0, :, :rows], r.back[1, :, :rows]), turned_real)
        signal = signal + dot3((r.back[0, :, rows:], r.back[1, :, rows:]), turned_imag)
        return signal.reshape(shape)

    def short(value, keep, coeffs):
        one, two = delayed(value, 1), delayed(value, 2)
        keep[0] = one
        keep[1] = two
        return coeffs[0] * value + coeffs[1] * one + coeffs[2] * two

    arrived("kv")
    both = r.got_kv[...].astype(F32)
    r.x_k[...] = both[:, :group]
    r.x_v[...] = both[:, group:]
    r.key_conv[...] = short(r.x_k[...], r.d_k, taps[1])
    r.value_conv[...] = short(r.x_v[...], r.d_v, taps[2])
    r.x_p[...] = r.key_conv[...] * r.value_conv[...]
    forward(r.x_p[...], r.spec_p)

    arrived("h")
    arrived("hs")
    forward(decode(r.got_h[...], unpacked(r.got_hs[...], group, 0)), r.spec_h)
    r.x_m[...] = inverse(r.spec_h, r.spec_p, False) + gain * r.x_p[...]
    r.send_m[...], peak = encode(r.x_m[...])
    r.send_ms[...] = packed_rows(nseq, group, {0: peak})
    send_all("m")
    send_all("ms")

    arrived("t")
    for i, row in enumerate(channel_rows(r.got_t[...].reshape(nseq, 128), 9, group)):
        r.taps_row[i : i + 1, :] = row

    @pl.when(me > 0)
    def _():
        for copy in halo_copies:
            copy.wait_recv()

    def tap_row(s, i):
        return r.taps_row[3 * s + i : 3 * s + i + 1, :]

    for s, src in enumerate([r.q, r.k, r.v]):
        own = src[...].astype(F32)
        above = r.halo[s].astype(F32)
        r.conv_rows[s] = (
            tap_row(s, 0) * own
            + tap_row(s, 1) * later(own, above, 1)
            + tap_row(s, 2) * later(own, above, 2)
        )

    arrived("qc")
    both = r.got_qc[...].astype(F32)
    r.x_q[...] = both[:, :group]
    r.x_c[...] = both[:, group:]
    r.x_g[...] = r.x_c[...] * short(r.x_q[...], r.d_q, taps[0])
    forward(r.x_g[...], r.spec_g)
    r.x_pg[...] = inverse(r.spec_h, r.spec_g, True) + gain * r.x_g[...]
    r.send_p[...], peak = encode(r.x_pg[...])
    r.send_ps[...] = packed_rows(nseq, group, {0: peak})
    send_all("p")
    send_all("ps")
    r.send_f[...], peak = encode(scale * inverse(r.spec_p, r.spec_g, True))
    r.send_fs[...] = packed_rows(nseq, group, {0: peak})
    send_all("f")
    send_all("fs")

    grads = [
        (r.x_c[...] * r.x_m[...], r.x_q, r.d_q),
        (r.x_pg[...] * r.value_conv[...], r.x_k, r.d_k),
        (r.x_pg[...] * r.key_conv[...], r.x_v, r.d_v),
    ]
    fields = {9: scale * total_of(r.x_g[...] * r.x_p[...])}
    for s, (grad, stream, moved) in enumerate(grads):
        fields[3 * s] = scale * total_of(grad * stream[...])
        fields[3 * s + 1] = scale * total_of(grad * moved[0])
        fields[3 * s + 2] = scale * total_of(grad * moved[1])
        fields[10 + 2 * s], fields[11 + 2 * s] = block_ends(grad, taps[s])
    r.send_s[...] = packed_rows(nseq, group, fields)
    send_all("s")

    def spread(grad, s):
        return (
            tap_row(s, 0) * grad
            + tap_row(s, 1) * pltpu.roll(grad, rows - 1, 0)
            + tap_row(s, 2) * pltpu.roll(grad, rows - 2, 0)
        ).astype(BF16)

    def in_rows(name):
        peaks = unpacked(getattr(r, "got_" + name + "s")[...], group, 0)
        return decode(getattr(r, "got_" + name)[...], peaks).reshape(rows, width).T

    arrived("m")
    arrived("ms")
    mixed = in_rows("m")
    r.go[...] = (r.conv_rows[0] * mixed).astype(BF16)
    r.qg[...] = spread(r.c[...].astype(F32) * mixed, 0)
    arrived("p")
    arrived("ps")
    product_grad = in_rows("p")
    r.kg[...] = spread(product_grad * r.conv_rows[2], 1)
    r.vg[...] = spread(product_grad * r.conv_rows[1], 2)
    arrived("f")
    arrived("fs")
    r.fg[...] = in_rows("f")
    arrived("s")
    r.sums[...] = r.got_s[...]

    for name in MESSAGES:
        sent(name)

    @pl.when(me < nseq - 1)
    def _():
        for copy in halo_copies:
            copy.wait_send()


def deliver(go, qg, kg, vg, fg, sums, go_out, qg_out, kg_out, vg_out, fg_out, taps_out, gain_out, ends, sem):
    nseq, group = sums.shape[0], gain_out.shape[1] // sums.shape[0]
    top = pl.ds(0, qg.shape[0] - HALO)
    low = pl.ds(qg.shape[0] - HALO, HALO)
    copies = [
        pltpu.make_async_copy(go, go_out, sem.at[0]),
        pltpu.make_async_copy(fg, fg_out, sem.at[1]),
    ]
    streams = [(qg, qg_out), (kg, kg_out), (vg, vg_out)]
    for i, (src, dst) in enumerate(streams):
        copies.append(pltpu.make_async_copy(src.at[top], dst.at[top], sem.at[2 + i]))
    for copy in copies:
        copy.start()
    rows = channel_rows(sums[...].reshape(nseq, 128), 16, group)
    place = lax.broadcasted_iota(jnp.int32, (HALO, qg.shape[1]), 0)
    for i, (src, dst) in enumerate(streams):
        last = src[low, :].astype(F32)
        last = jnp.where(place == HALO - 2, rows[10 + 2 * i], last)
        last = jnp.where(place == HALO - 1, rows[11 + 2 * i], last)
        ends[i] = last.astype(BF16)
        copy = pltpu.make_async_copy(ends.at[i], dst.at[low], sem.at[5 + i])
        copy.start()
        copies.append(copy)
    for i in range(9):
        taps_out[i // 3, i % 3 : i % 3 + 1, :] = rows[i]
    gain_out[...] = rows[9]
    for copy in copies:
        copy.wait()


def per_device(query_rows, key_rows, value_rows, long_filter, short_taps, skip_gain, cotangent):
    rows, channels = query_rows.shape
    nseq, nchan = lax.axis_size("seq"), lax.axis_size("chan")
    group = channels // nseq
    scale = 1.0 / math.sqrt(rows * nseq)
    tables = [jnp.asarray(t) for t in transform_tables(nseq, rows, group)]
    vmem = pl.BlockSpec(memory_space=pltpu.VMEM)
    hbm = pl.BlockSpec(memory_space=pltpu.HBM)
    inputs = {
        "q_hbm": query_rows,
        "k_hbm": key_rows,
        "v_hbm": value_rows,
        "c_hbm": cotangent,
        "h_hbm": long_filter,
        "taps_hbm": short_taps,
        "gain_hbm": skip_gain[None],
        "left_hbm": tables[0],
        "back_hbm": tables[1],
        "right_hbm": tables[2],
        "twist_hbm": tables[3],
    }
    block = jax.ShapeDtypeStruct((rows, channels), BF16)
    results = {
        "go": block,
        "qg": block,
        "kg": block,
        "vg": block,
        "fg": jax.ShapeDtypeStruct((rows, channels), F32),
        "sums": jax.ShapeDtypeStruct((nseq, 1, 128), F32),
    }
    local = pltpu.VMEM((rows, channels), BF16)
    taps, gain = pltpu.VMEM((3, 3, group), F32), pltpu.VMEM((1, group), F32)
    scratch = dict(
        q=local,
        k=local,
        v=local,
        c=local,
        h=pltpu.VMEM((rows, channels), F32),
        taps_own=taps,
        gain_own=gain,
        taps=taps,
        gain=gain,
        halo=pltpu.VMEM((3, HALO, channels), BF16),
        taps_row=pltpu.VMEM((16, channels), F32),
        conv_rows=pltpu.VMEM((3, rows, channels), F32),
    )
    for name, table in zip(("left", "back", "right", "twist"), tables):
        scratch[name] = pltpu.VMEM(table.shape, table.dtype)
    for name in MESSAGES:
        if name in ("kv", "qc"):
            kind = pltpu.VMEM((nseq, 2 * group, rows), BF16)
        elif name in ("h", "m", "p", "f"):
            kind = pltpu.VMEM((nseq, 2 * group, rows // 2), BF16)
        else:
            kind = pltpu.VMEM((nseq, 1, 128), F32)
        scratch["send_" + name] = scratch["got_" + name] = kind
    for name in ("x_q", "x_k", "x_v", "x_c", "x_p", "x_g", "x_m", "x_pg", "key_conv", "value_conv"):
        scratch[name] = pltpu.VMEM((nseq, group, rows), F32)
    for name in ("d_q", "d_k", "d_v"):
        scratch[name] = pltpu.VMEM((2, nseq, group, rows), F32)
    for name in ("spec_h", "spec_p", "spec_g"):
        scratch[name] = pltpu.VMEM((2, nseq * group, rows), F32)
    scratch["fetch_sem"] = pltpu.SemaphoreType.DMA((11,))
    scratch["send_sem"] = pltpu.SemaphoreType.DMA((len(MESSAGES),))
    scratch["recv_sem"] = pltpu.SemaphoreType.DMA((len(MESSAGES),))
    scratch["side_sem"] = pltpu.SemaphoreType.DMA((4,))
    scratch["halo_sem"] = pltpu.SemaphoreType.DMA((6,))
    names = tuple(inputs) + tuple(results) + tuple(scratch)
    outs = pl.pallas_call(
        functools.partial(kernel, names, nseq, nchan, group, scale),
        out_shape=tuple(results.values()),
        in_specs=[hbm] * len(inputs),
        out_specs=[vmem] * len(results),
        scratch_shapes=list(scratch.values()),
        compiler_params=pltpu.CompilerParams(
            collective_id=0, has_side_effects=True, vmem_limit_bytes=44 << 20
        ),
        name="hyena",
    )(*[pltpu.with_memory_space_constraint(x, pltpu.HBM) for x in inputs.values()])
    moved = pl.pallas_call(
        deliver,
        out_shape=tuple(jax.ShapeDtypeStruct(o.shape, o.dtype) for o in outs[:5])
        + (
            jax.ShapeDtypeStruct((3, 3, channels), F32),
            jax.ShapeDtypeStruct((1, channels), F32),
        ),
        in_specs=[vmem] * 6,
        out_specs=[hbm] * 5 + [vmem] * 2,
        scratch_shapes=[pltpu.VMEM((3, HALO, channels), BF16), pltpu.SemaphoreType.DMA((8,))],
        compiler_params=pltpu.CompilerParams(vmem_limit_bytes=16 << 20),
        name="deliver",
    )(*outs)
    return tuple(moved[:6]) + (moved[6].reshape(channels),)


def solution(mesh):
    in_specs = (
        P("seq", "chan"),
        P("seq", "chan"),
        P("seq", "chan"),
        P("seq", "chan"),
        P(None, None, ("seq", "chan")),
        P(("seq", "chan")),
        P("seq", "chan"),
    )
    out_specs = (
        P("seq", "chan"),
        P("seq", "chan"),
        P("seq", "chan"),
        P("seq", "chan"),
        P("seq", "chan"),
        P(None, None, "chan"),
        P("chan"),
    )
    return jax.shard_map(
        per_device, mesh=mesh, in_specs=in_specs, out_specs=out_specs, check_vma=False
    )
```

```python
import functools
import math
import types

import jax
import jax.numpy as jnp
import ml_dtypes
import numpy as np
from jax import lax
from jax.experimental import pallas as pl
from jax.experimental.pallas import tpu as pltpu
from jax.sharding import PartitionSpec as P

F32 = jnp.float32
BF16 = jnp.bfloat16
MESH = pl.DeviceIdType.MESH
REACH = 125.0 * math.log(2.0)


def halves(table):
    high = table.astype(np.float32).astype(ml_dtypes.bfloat16)
    low = (table - high.astype(np.float64)).astype(np.float32).astype(ml_dtypes.bfloat16)
    return np.stack([high, low])


def transform_tables(blocks, width, group):
    total = blocks * width
    shifted = np.arange(blocks) - 0.25
    outer = 2.0 * np.pi / blocks * np.outer(shifted, np.arange(blocks))
    eye = np.eye(group)
    left = np.concatenate([np.kron(np.cos(outer), eye), np.kron(-np.sin(outer), eye)], axis=0)
    back = left.T / total
    inner = 2.0 * np.pi / width * (np.outer(np.arange(width), np.arange(width)) % width)
    right = np.stack([halves(np.cos(inner)), halves(np.sin(inner))])
    turn = 2.0 * np.pi / total * np.outer(shifted, np.arange(width))
    twist = np.stack([np.cos(turn), np.sin(turn)]).astype(np.float32)
    twist = np.repeat(twist, group, axis=1)
    left, back = halves(left), halves(back)
    left = np.concatenate([left[0], left[0], left[1]], axis=1)
    back = np.concatenate([back[0], back[0], back[1]], axis=1)
    return left, back, right, twist


def split(value):
    high = value.astype(BF16)
    return high, (value - high.astype(F32)).astype(BF16)


def dot(left, right):
    return jnp.dot(left, right, preferred_element_type=F32)


def delayed(value, steps):
    before = jnp.concatenate([jnp.zeros_like(value[:1]), value[:-1]], axis=0)
    lane = lax.broadcasted_iota(jnp.int32, value.shape, 2)
    return jnp.where(
        lane < steps, pltpu.roll(before, steps, 2), pltpu.roll(value, steps, 2)
    )


def later(value, head, steps):
    return pltpu.roll(jnp.concatenate([head, value], axis=0), steps, 0)[head.shape[0] :]


def block_ends(grad, coeffs):
    half = grad.shape[2] // 2
    low, high = grad[:, :, :half], grad[:, :, half:]
    after = jnp.concatenate([low[1:], jnp.zeros_like(low[:1])], axis=0)
    lane = lax.broadcasted_iota(jnp.int32, high.shape, 2)
    total = coeffs[0] * high
    for steps in (1, 2):
        moved = jnp.where(
            lane < half - steps,
            pltpu.roll(high, half - steps, 2),
            pltpu.roll(after, half - steps, 2),
        )
        total = total + coeffs[steps] * moved
    return [
        jnp.sum(jnp.where(lane == half - back, total, 0.0), axis=2, keepdims=True)
        for back in (2, 1)
    ]


def total_of(value):
    return jnp.sum(jnp.sum(value, axis=0), axis=1, keepdims=True)


def encode(value):
    peak = jnp.maximum(jnp.max(jnp.abs(value), axis=2, keepdims=True), 1e-30)
    code = jnp.exp(jnp.abs(value) * (2.0 * REACH / peak) - REACH)
    code = jnp.where(value < 0.0, -code, code)
    half = value.shape[2] // 2
    return jnp.concatenate([code[:, :, :half], code[:, :, half:]], axis=1).astype(BF16), peak


def decode(code, peak):
    group = code.shape[1] // 2
    code = code.astype(F32)
    code = jnp.concatenate([code[:, :group], code[:, group:]], axis=2)
    size = (jnp.log(jnp.abs(code)) + REACH) * (peak * (0.5 / REACH))
    return jnp.where(code < 0.0, -size, size)


def field_mask(group, field):
    lane = lax.broadcasted_iota(jnp.int32, (1, group, 128), 2)
    return lane == group * field + lax.broadcasted_iota(jnp.int32, (1, group, 128), 1)


def packed_rows(count, group, fields):
    wide = jnp.zeros((count, group, 128), F32)
    for field, value in fields.items():
        wide = jnp.where(field_mask(group, field), value, wide)
    return jnp.sum(wide, axis=1, keepdims=True)


def unpacked(rows, group, field):
    wide = jnp.broadcast_to(rows, (rows.shape[0], group, 128))
    return jnp.sum(jnp.where(field_mask(group, field), wide, 0.0), axis=2, keepdims=True)


def channel_rows(table, count, group):
    owners = table.shape[0]
    width = owners * group
    turned = jnp.concatenate(
        [table if f == 0 else pltpu.roll(table, 128 - group * f, 1) for f in range(count)],
        axis=0,
    )
    channel = lax.broadcasted_iota(jnp.int32, (128, width), 1)
    pick = lax.rem(channel, group) == lax.broadcasted_iota(jnp.int32, (128, width), 0)
    pick = pick.astype(F32).astype(BF16)
    high, low = split(turned)
    wide = (dot(high, pick) + dot(low, pick)).reshape(count, owners, width)
    owner = lax.div(lax.broadcasted_iota(jnp.int32, (owners, width), 1), group)
    keep = owner == lax.broadcasted_iota(jnp.int32, (owners, width), 0)
    return [jnp.sum(jnp.where(keep, wide[f], 0.0), axis=0, keepdims=True) for f in range(count)]


HALO = 16
DEPTH = 8


def farthest(step, length):
    away_by = lax.div(step + 1, 2)
    return jnp.where(lax.rem(step, 2) == 1, length // 2 - away_by, length // 2 + away_by)


def away(me, step, count):
    planes = count // DEPTH
    across = farthest(lax.div(step - 1, DEPTH), planes)
    along = farthest(lax.rem(step - 1, DEPTH), DEPTH)
    plane = lax.rem(lax.div(me, DEPTH) + across, planes)
    return DEPTH * plane + lax.rem(lax.rem(me, DEPTH) + along, DEPTH)


MESSAGES = ("kv", "h", "hs", "qc", "m", "ms", "p", "f", "pfs", "s")


def kernel(names, nseq, nchan, group, scale, *refs):
    r = types.SimpleNamespace(**dict(zip(names, refs, strict=True)))
    me = lax.axis_index("seq")
    mine = lax.axis_index("chan")
    rows, width = r.q_hbm.shape
    number = {name: i for i, name in enumerate(MESSAGES)}

    fetched = {}
    pairs = [("k", "k"), ("v", "v"), ("h", "h"), ("q", "q"), ("c", "c"), ("taps", "taps_own")]
    pairs += [("gain", "gain_own"), ("left", "left"), ("twist", "twist")]
    pairs += [("right", "right"), ("back", "back")]
    for i, (src, dst) in enumerate(pairs):
        fetched[src] = pltpu.make_async_copy(
            getattr(r, src + "_hbm"), getattr(r, dst), r.fetch_sem.at[i]
        )
        fetched[src].start()

    per = nseq // nchan
    to_seq = nchan * lax.rem(me, per) + mine
    to_chan = lax.div(me, per)
    from_seq = per * mine + lax.div(me, nchan)
    from_chan = lax.rem(me, nchan)
    stays = jnp.logical_and(to_seq == me, to_chan == mine)

    barrier = pltpu.get_barrier_semaphore()

    def greet(step, carry):
        peer = lax.rem(me + step, nseq)
        pl.semaphore_signal(barrier, inc=1, device_id=(peer, mine), device_id_type=MESH)
        return carry

    lax.fori_loop(1, nseq, greet, 0)

    @pl.when(jnp.logical_not(stays))
    def _():
        pl.semaphore_signal(
            barrier, inc=1, device_id=(from_seq, from_chan), device_id_type=MESH
        )

    shape = (nseq, group, width)

    def paired(first, second):
        one = first[...].astype(F32).T.reshape(shape)
        two = second[...].astype(F32).T.reshape(shape)
        return jnp.concatenate([one, two], axis=1).astype(BF16)

    fetched["k"].wait()
    fetched["v"].wait()
    r.send_kv[...] = paired(r.k, r.v)

    @pl.when(stays)
    def _():
        pl.semaphore_wait(barrier, nseq - 1)

    @pl.when(jnp.logical_not(stays))
    def _():
        pl.semaphore_wait(barrier, nseq)

    def send_all(name):
        source, target = getattr(r, "send_" + name), getattr(r, "got_" + name)
        index = number[name]

        def body(step, carry):
            peer = away(me, step, nseq)
            pltpu.make_async_remote_copy(
                src_ref=source.at[peer],
                dst_ref=target.at[me],
                send_sem=r.send_sem.at[index],
                recv_sem=r.recv_sem.at[index],
                device_id=(peer, mine),
                device_id_type=MESH,
            ).start()
            return carry

        lax.fori_loop(1, nseq, body, 0)
        target[me] = source[me]

    def arrived(name):
        part = getattr(r, "got_" + name).at[pl.ds(0, nseq - 1)]
        pltpu.make_async_copy(part, part, r.recv_sem.at[number[name]]).wait()

    def sent(name):
        part = getattr(r, "send_" + name).at[pl.ds(0, nseq - 1)]
        pltpu.make_async_copy(part, part, r.send_sem.at[number[name]]).wait()

    send_all("kv")

    side_copies = [
        pltpu.make_async_remote_copy(
            src_ref=src,
            dst_ref=dst,
            send_sem=r.side_sem.at[i],
            recv_sem=r.side_sem.at[2 + i],
            device_id=(to_seq, to_chan),
            device_id_type=MESH,
        )
        for i, (src, dst) in enumerate([(r.taps_own, r.taps), (r.gain_own, r.gain)])
    ]
    fetched["taps"].wait()
    fetched["gain"].wait()

    @pl.when(jnp.logical_not(stays))
    def _():
        for copy in side_copies:
            copy.start()

    @pl.when(stays)
    def _():
        r.taps[...] = r.taps_own[...]
        r.gain[...] = r.gain_own[...]

    fetched["h"].wait()
    r.send_h[...], peak = encode(r.h[...].T.reshape(shape))
    r.send_hs[...] = packed_rows(nseq, group, {0: peak})
    send_all("h")
    send_all("hs")

    fetched["q"].wait()
    fetched["c"].wait()
    r.send_qc[...] = paired(r.q, r.c)
    send_all("qc")

    halo_copies = [
        pltpu.make_async_remote_copy(
            src_ref=src.at[pl.ds(rows - HALO, HALO)],
            dst_ref=r.halo.at[i],
            send_sem=r.halo_sem.at[i],
            recv_sem=r.halo_sem.at[3 + i],
            device_id=(lax.rem(me + 1, nseq), mine),
            device_id_type=MESH,
        )
        for i, src in enumerate([r.q, r.k, r.v])
    ]

    @pl.when(me < nseq - 1)
    def _():
        for copy in halo_copies:
            copy.start()

    @pl.when(me == 0)
    def _():
        r.halo[...] = jnp.zeros(r.halo.shape, BF16)

    @pl.when(jnp.logical_not(stays))
    def _():
        for copy in side_copies:
            copy.wait()

    diagonal = field_mask(group, 0)[0, :, :group]

    def column(row):
        spread_out = jnp.broadcast_to(row, (group, group))
        return jnp.sum(jnp.where(diagonal, spread_out, 0.0), axis=1, keepdims=True)

    taps = [[column(r.taps[s, i : i + 1, :]) for i in range(3)] for s in range(3)]
    gain = column(r.gain[...])
    for name in ("left", "twist", "right", "back"):
        fetched[name].wait()

    high_cos, low_cos = r.right[0, 0], r.right[0, 1]
    high_sin, low_sin = r.right[1, 0], r.right[1, 1]
    for i, (cos_part, sin_part) in enumerate(
        [(high_cos, high_sin), (high_cos, high_sin), (low_cos, low_sin)]
    ):
        top, bottom = pl.ds(i * width, width), pl.ds((3 + i) * width, width)
        r.turn[top, :width] = cos_part
        r.turn[bottom, :width] = sin_part
        r.turn[top, width:] = -sin_part
        r.turn[bottom, width:] = cos_part

    def over_lanes(real, imag):
        for i, value in enumerate([real, imag]):
            high, low = split(value)
            for k, part in enumerate([high, low, high]):
                start = (3 * i + k) * width
                r.lanes[:, start : start + width] = part
        both = dot(r.lanes[...], r.turn[...])
        return both[:, :width], both[:, width:]

    def forward(signal, spec):
        high, low = split(signal.reshape(rows, width))
        for i, part in enumerate([high, low, high]):
            r.stack[i * rows : (i + 1) * rows, :] = part
        wave = dot(r.left[...], r.stack[: 3 * rows, :])
        real, imag = wave[:rows], wave[rows:]
        cosine, sine = r.twist[0], r.twist[1]
        spec[0], spec[1] = over_lanes(
            real * cosine + imag * sine, imag * cosine - real * sine
        )

    def inverse(left_spec, right_spec, conjugate):
        a_re, a_im, b_re, b_im = left_spec[0], left_spec[1], right_spec[0], right_spec[1]
        if conjugate:
            real, imag = a_re * b_re + a_im * b_im, a_im * b_re - a_re * b_im
        else:
            real, imag = a_re * b_re - a_im * b_im, -(a_re * b_im + a_im * b_re)
        wave_real, wave_imag = over_lanes(real, imag)
        cosine, sine = r.twist[0], r.twist[1]
        high_real, low_real = split(wave_real * cosine + wave_imag * sine)
        high_imag, low_imag = split(wave_real * sine - wave_imag * cosine)
        parts = [high_real, high_imag, low_real, low_imag, high_real, high_imag]
        for i, part in enumerate(parts):
            r.stack[i * rows : (i + 1) * rows, :] = part
        return dot(r.back[...], r.stack[...]).reshape(shape)

    def short(value, keep, coeffs):
        one, two = delayed(value, 1), delayed(value, 2)
        keep[0] = one
        keep[1] = two
        return coeffs[0] * value + coeffs[1] * one + coeffs[2] * two

    arrived("kv")
    both = r.got_kv[...].astype(F32)
    r.x_k[...] = both[:, :group]
    r.x_v[...] = both[:, group:]
    r.key_conv[...] = short(r.x_k[...], r.d_k, taps[1])
    r.value_conv[...] = short(r.x_v[...], r.d_v, taps[2])
    r.x_p[...] = r.key_conv[...] * r.value_conv[...]
    forward(r.x_p[...], r.spec_p)

    arrived("h")
    arrived("hs")
    forward(decode(r.got_h[...], unpacked(r.got_hs[...], group, 0)), r.spec_h)
    r.x_m[...] = inverse(r.spec_h, r.spec_p, False) + gain * r.x_p[...]
    r.send_m[...], peak = encode(r.x_m[...])
    fields = {3 * s + i: taps[s][i] for s in range(3) for i in range(3)}
    r.send_ms[...] = packed_rows(nseq, group, {**fields, 9: peak})
    send_all("m")
    send_all("ms")

    arrived("qc")
    both = r.got_qc[...].astype(F32)
    r.x_q[...] = both[:, :group]
    r.x_c[...] = both[:, group:]
    r.x_g[...] = r.x_c[...] * short(r.x_q[...], r.d_q, taps[0])
    forward(r.x_g[...], r.spec_g)
    r.x_pg[...] = inverse(r.spec_h, r.spec_g, True) + gain * r.x_g[...]
    r.send_p[...], peak = encode(r.x_pg[...])
    send_all("p")
    r.send_f[...], other = encode(scale * inverse(r.spec_p, r.spec_g, True))
    send_all("f")
    r.send_pfs[...] = packed_rows(nseq, group, {0: peak, 1: other})
    send_all("pfs")

    grads = [
        (r.x_c[...] * r.x_m[...], r.x_q, r.d_q),
        (r.x_pg[...] * r.value_conv[...], r.x_k, r.d_k),
        (r.x_pg[...] * r.key_conv[...], r.x_v, r.d_v),
    ]
    fields = {9: scale * total_of(r.x_g[...] * r.x_p[...])}
    for s, (grad, stream, moved) in enumerate(grads):
        fields[3 * s] = scale * total_of(grad * stream[...])
        fields[3 * s + 1] = scale * total_of(grad * moved[0])
        fields[3 * s + 2] = scale * total_of(grad * moved[1])
        fields[10 + 2 * s], fields[11 + 2 * s] = block_ends(grad, taps[s])
    r.send_s[...] = packed_rows(nseq, group, fields)
    send_all("s")

    def spread(grad, s):
        return (
            tap_row(s, 0) * grad
            + tap_row(s, 1) * pltpu.roll(grad, rows - 1, 0)
            + tap_row(s, 2) * pltpu.roll(grad, rows - 2, 0)
        ).astype(BF16)

    def in_rows(name, side, field):
        peaks = unpacked(getattr(r, "got_" + side)[...], group, field)
        return decode(getattr(r, "got_" + name)[...], peaks).reshape(rows, width).T

    arrived("ms")
    for i, row in enumerate(channel_rows(r.got_ms[...].reshape(nseq, 128), 9, group)):
        r.taps_row[i : i + 1, :] = row

    @pl.when(me > 0)
    def _():
        for copy in halo_copies:
            copy.wait_recv()

    def tap_row(s, i):
        return r.taps_row[3 * s + i : 3 * s + i + 1, :]

    for s, src in enumerate([r.q, r.k, r.v]):
        own = src[...].astype(F32)
        above = r.halo[s].astype(F32)
        r.conv_rows[s] = (
            tap_row(s, 0) * own
            + tap_row(s, 1) * later(own, above, 1)
            + tap_row(s, 2) * later(own, above, 2)
        )

    arrived("m")
    mixed = in_rows("m", "ms", 9)
    r.go[...] = (r.conv_rows[0] * mixed).astype(BF16)
    r.qg[...] = spread(r.c[...].astype(F32) * mixed, 0)
    arrived("p")
    arrived("pfs")
    product_grad = in_rows("p", "pfs", 0)
    r.kg[...] = spread(product_grad * r.conv_rows[2], 1)
    r.vg[...] = spread(product_grad * r.conv_rows[1], 2)
    arrived("f")
    r.fg[...] = in_rows("f", "pfs", 1)
    arrived("s")
    r.sums[...] = r.got_s[...]

    for name in MESSAGES:
        sent(name)

    @pl.when(me < nseq - 1)
    def _():
        for copy in halo_copies:
            copy.wait_send()


def deliver(go, qg, kg, vg, fg, sums, go_out, qg_out, kg_out, vg_out, fg_out, taps_out, gain_out, ends, sem):
    nseq, group = sums.shape[0], gain_out.shape[1] // sums.shape[0]
    top = pl.ds(0, qg.shape[0] - HALO)
    low = pl.ds(qg.shape[0] - HALO, HALO)
    copies = [
        pltpu.make_async_copy(go, go_out, sem.at[0]),
        pltpu.make_async_copy(fg, fg_out, sem.at[1]),
    ]
    streams = [(qg, qg_out), (kg, kg_out), (vg, vg_out)]
    for i, (src, dst) in enumerate(streams):
        copies.append(pltpu.make_async_copy(src.at[top], dst.at[top], sem.at[2 + i]))
    for copy in copies:
        copy.start()
    rows = channel_rows(sums[...].reshape(nseq, 128), 16, group)
    place = lax.broadcasted_iota(jnp.int32, (HALO, qg.shape[1]), 0)
    for i, (src, dst) in enumerate(streams):
        last = src[low, :].astype(F32)
        last = jnp.where(place == HALO - 2, rows[10 + 2 * i], last)
        last = jnp.where(place == HALO - 1, rows[11 + 2 * i], last)
        ends[i] = last.astype(BF16)
        copy = pltpu.make_async_copy(ends.at[i], dst.at[low], sem.at[5 + i])
        copy.start()
        copies.append(copy)
    for i in range(9):
        taps_out[i // 3, i % 3 : i % 3 + 1, :] = rows[i]
    gain_out[...] = rows[9]
    for copy in copies:
        copy.wait()


def per_device(query_rows, key_rows, value_rows, long_filter, short_taps, skip_gain, cotangent):
    rows, channels = query_rows.shape
    nseq, nchan = lax.axis_size("seq"), lax.axis_size("chan")
    group = channels // nseq
    scale = 1.0 / math.sqrt(rows * nseq)
    tables = [jnp.asarray(t) for t in transform_tables(nseq, rows, group)]
    vmem = pl.BlockSpec(memory_space=pltpu.VMEM)
    hbm = pl.BlockSpec(memory_space=pltpu.HBM)
    inputs = {
        "q_hbm": query_rows,
        "k_hbm": key_rows,
        "v_hbm": value_rows,
        "c_hbm": cotangent,
        "h_hbm": long_filter,
        "taps_hbm": short_taps,
        "gain_hbm": skip_gain[None],
        "left_hbm": tables[0],
        "back_hbm": tables[1],
        "right_hbm": tables[2],
        "twist_hbm": tables[3],
    }
    block = jax.ShapeDtypeStruct((rows, channels), BF16)
    results = {
        "go": block,
        "qg": block,
        "kg": block,
        "vg": block,
        "fg": jax.ShapeDtypeStruct((rows, channels), F32),
        "sums": jax.ShapeDtypeStruct((nseq, 1, 128), F32),
    }
    local = pltpu.VMEM((rows, channels), BF16)
    taps, gain = pltpu.VMEM((3, 3, group), F32), pltpu.VMEM((1, group), F32)
    scratch = dict(
        q=local,
        k=local,
        v=local,
        c=local,
        h=pltpu.VMEM((rows, channels), F32),
        taps_own=taps,
        gain_own=gain,
        taps=taps,
        gain=gain,
        halo=pltpu.VMEM((3, HALO, channels), BF16),
        taps_row=pltpu.VMEM((16, channels), F32),
        conv_rows=pltpu.VMEM((3, rows, channels), F32),
    )
    for name, table in zip(("left", "back", "right", "twist"), tables):
        scratch[name] = pltpu.VMEM(table.shape, table.dtype)
    for name in MESSAGES:
        if name in ("kv", "qc"):
            kind = pltpu.VMEM((nseq, 2 * group, rows), BF16)
        elif name in ("h", "m", "p", "f"):
            kind = pltpu.VMEM((nseq, 2 * group, rows // 2), BF16)
        else:
            kind = pltpu.VMEM((nseq, 1, 128), F32)
        scratch["send_" + name] = scratch["got_" + name] = kind
    for name in ("x_q", "x_k", "x_v", "x_c", "x_p", "x_g", "x_m", "x_pg", "key_conv", "value_conv"):
        scratch[name] = pltpu.VMEM((nseq, group, rows), F32)
    for name in ("d_q", "d_k", "d_v"):
        scratch[name] = pltpu.VMEM((2, nseq, group, rows), F32)
    for name in ("spec_h", "spec_p", "spec_g"):
        scratch[name] = pltpu.VMEM((2, nseq * group, rows), F32)
    scratch["turn"] = pltpu.VMEM((6 * rows, 2 * rows), BF16)
    scratch["lanes"] = pltpu.VMEM((nseq * group, 6 * rows), BF16)
    scratch["stack"] = pltpu.VMEM((6 * nseq * group, rows), BF16)
    scratch["fetch_sem"] = pltpu.SemaphoreType.DMA((11,))
    scratch["send_sem"] = pltpu.SemaphoreType.DMA((len(MESSAGES),))
    scratch["recv_sem"] = pltpu.SemaphoreType.DMA((len(MESSAGES),))
    scratch["side_sem"] = pltpu.SemaphoreType.DMA((4,))
    scratch["halo_sem"] = pltpu.SemaphoreType.DMA((6,))
    names = tuple(inputs) + tuple(results) + tuple(scratch)
    outs = pl.pallas_call(
        functools.partial(kernel, names, nseq, nchan, group, scale),
        out_shape=tuple(results.values()),
        in_specs=[hbm] * len(inputs),
        out_specs=[vmem] * len(results),
        scratch_shapes=list(scratch.values()),
        compiler_params=pltpu.CompilerParams(
            collective_id=0, has_side_effects=True, vmem_limit_bytes=44 << 20
        ),
        name="hyena",
    )(*[pltpu.with_memory_space_constraint(x, pltpu.HBM) for x in inputs.values()])
    moved = pl.pallas_call(
        deliver,
        out_shape=tuple(jax.ShapeDtypeStruct(o.shape, o.dtype) for o in outs[:5])
        + (
            jax.ShapeDtypeStruct((3, 3, channels), F32),
            jax.ShapeDtypeStruct((1, channels), F32),
        ),
        in_specs=[vmem] * 6,
        out_specs=[hbm] * 5 + [vmem] * 2,
        scratch_shapes=[pltpu.VMEM((3, HALO, channels), BF16), pltpu.SemaphoreType.DMA((8,))],
        compiler_params=pltpu.CompilerParams(vmem_limit_bytes=16 << 20),
        name="deliver",
    )(*outs)
    return tuple(moved[:6]) + (moved[6].reshape(channels),)


def solution(mesh):
    in_specs = (
        P("seq", "chan"),
        P("seq", "chan"),
        P("seq", "chan"),
        P("seq", "chan"),
        P(None, None, ("seq", "chan")),
        P(("seq", "chan")),
        P("seq", "chan"),
    )
    out_specs = (
        P("seq", "chan"),
        P("seq", "chan"),
        P("seq", "chan"),
        P("seq", "chan"),
        P("seq", "chan"),
        P(None, None, "chan"),
        P("chan"),
    )
    return jax.shard_map(
        per_device, mesh=mesh, in_specs=in_specs, out_specs=out_specs, check_vma=False
    )
```

```python
import functools
import math
import types

import jax
import jax.numpy as jnp
import ml_dtypes
import numpy as np
from jax import lax
from jax.experimental import pallas as pl
from jax.experimental.pallas import tpu as pltpu
from jax.sharding import PartitionSpec as P

F32 = jnp.float32
BF16 = jnp.bfloat16
MESH = pl.DeviceIdType.MESH
REACH = 125.0 * math.log(2.0)


def halves(table):
    high = table.astype(np.float32).astype(ml_dtypes.bfloat16)
    low = (table - high.astype(np.float64)).astype(np.float32).astype(ml_dtypes.bfloat16)
    return np.stack([high, low])


def transform_tables(blocks, width, group):
    total = blocks * width
    shifted = np.arange(blocks) - 0.25
    outer = 2.0 * np.pi / blocks * np.outer(shifted, np.arange(blocks))
    eye = np.eye(group)
    left = np.concatenate([np.kron(np.cos(outer), eye), np.kron(-np.sin(outer), eye)], axis=0)
    back = left.T / total
    half = width // 2
    inner = 2.0 * np.pi / half * (np.outer(np.arange(half), np.arange(half)) % half)
    cosine, sine = halves(np.cos(inner)), halves(np.sin(inner))
    right = np.concatenate(
        [np.block([[cosine[i], -sine[i]], [sine[i], cosine[i]]]) for i in (0, 0, 1)]
    )
    step = 2.0 * np.pi / width * np.arange(half)
    swing = np.stack([np.tile(f(step), (8, 1)) for f in (np.cos, np.sin)]).astype(np.float32)
    turn = 2.0 * np.pi / total * np.outer(shifted, np.arange(width))
    twist = np.stack([np.cos(turn), np.sin(turn)]).astype(np.float32)
    twist = np.repeat(twist, group, axis=1)
    left, back = halves(left), halves(back)
    left = np.concatenate([left[0], left[0], left[1]], axis=1)
    back = np.concatenate([back[0], back[0], back[1]], axis=1)
    return left, back, right, twist, swing


def split(value):
    high = value.astype(BF16)
    return high, (value - high.astype(F32)).astype(BF16)


def dot(left, right):
    return jnp.dot(left, right, preferred_element_type=F32)


def delayed(value, steps):
    before = jnp.concatenate([jnp.zeros_like(value[:1]), value[:-1]], axis=0)
    lane = lax.broadcasted_iota(jnp.int32, value.shape, 2)
    return jnp.where(
        lane < steps, pltpu.roll(before, steps, 2), pltpu.roll(value, steps, 2)
    )


def later(value, head, steps):
    return pltpu.roll(jnp.concatenate([head, value], axis=0), steps, 0)[head.shape[0] :]


def block_ends(grad, coeffs):
    half = grad.shape[2] // 2
    low, high = grad[:, :, :half], grad[:, :, half:]
    after = jnp.concatenate([low[1:], jnp.zeros_like(low[:1])], axis=0)
    lane = lax.broadcasted_iota(jnp.int32, high.shape, 2)
    total = coeffs[0] * high
    for steps in (1, 2):
        moved = jnp.where(
            lane < half - steps,
            pltpu.roll(high, half - steps, 2),
            pltpu.roll(after, half - steps, 2),
        )
        total = total + coeffs[steps] * moved
    return [
        jnp.sum(jnp.where(lane == half - back, total, 0.0), axis=2, keepdims=True)
        for back in (2, 1)
    ]


def total_of(value):
    return jnp.sum(jnp.sum(value, axis=0), axis=1, keepdims=True)


def encode(value):
    peak = jnp.maximum(jnp.max(jnp.abs(value), axis=2, keepdims=True), 1e-30)
    code = jnp.exp(jnp.abs(value) * (2.0 * REACH / peak) - REACH)
    code = jnp.where(value < 0.0, -code, code)
    half = value.shape[2] // 2
    return jnp.concatenate([code[:, :, :half], code[:, :, half:]], axis=1).astype(BF16), peak


def decode(code, peak):
    group = code.shape[1] // 2
    code = code.astype(F32)
    code = jnp.concatenate([code[:, :group], code[:, group:]], axis=2)
    size = (jnp.log(jnp.abs(code)) + REACH) * (peak * (0.5 / REACH))
    return jnp.where(code < 0.0, -size, size)


def field_mask(group, field):
    lane = lax.broadcasted_iota(jnp.int32, (1, group, 128), 2)
    return lane == group * field + lax.broadcasted_iota(jnp.int32, (1, group, 128), 1)


def packed_rows(count, group, fields):
    wide = jnp.zeros((count, group, 128), F32)
    for field, value in fields.items():
        wide = jnp.where(field_mask(group, field), value, wide)
    return jnp.sum(wide, axis=1, keepdims=True)


def unpacked(rows, group, field):
    wide = jnp.broadcast_to(rows, (rows.shape[0], group, 128))
    return jnp.sum(jnp.where(field_mask(group, field), wide, 0.0), axis=2, keepdims=True)


def channel_rows(table, count, group):
    owners = table.shape[0]
    width = owners * group
    turned = jnp.concatenate(
        [table if f == 0 else pltpu.roll(table, 128 - group * f, 1) for f in range(count)],
        axis=0,
    )
    channel = lax.broadcasted_iota(jnp.int32, (128, width), 1)
    pick = lax.rem(channel, group) == lax.broadcasted_iota(jnp.int32, (128, width), 0)
    pick = pick.astype(F32).astype(BF16)
    high, low = split(turned)
    wide = (dot(high, pick) + dot(low, pick)).reshape(count, owners, width)
    owner = lax.div(lax.broadcasted_iota(jnp.int32, (owners, width), 1), group)
    keep = owner == lax.broadcasted_iota(jnp.int32, (owners, width), 0)
    return [jnp.sum(jnp.where(keep, wide[f], 0.0), axis=0, keepdims=True) for f in range(count)]


HALO = 16
DEPTH = 8


def farthest(step, length):
    away_by = lax.div(step + 1, 2)
    return jnp.where(lax.rem(step, 2) == 1, length // 2 - away_by, length // 2 + away_by)


def away(me, step, count):
    planes = count // DEPTH
    across = farthest(lax.div(step - 1, DEPTH), planes)
    along = farthest(lax.rem(step - 1, DEPTH), DEPTH)
    plane = lax.rem(lax.div(me, DEPTH) + across, planes)
    return DEPTH * plane + lax.rem(lax.rem(me, DEPTH) + along, DEPTH)


MESSAGES = ("kv", "h", "hs", "qc", "m", "ms", "p", "s", "f", "fs")


def kernel(names, nseq, nchan, group, scale, *refs):
    r = types.SimpleNamespace(**dict(zip(names, refs, strict=True)))
    me = lax.axis_index("seq")
    mine = lax.axis_index("chan")
    rows, width = r.q_hbm.shape
    number = {name: i for i, name in enumerate(MESSAGES)}

    fetched = {}
    pairs = [("k", "k"), ("v", "v"), ("h", "h"), ("q", "q"), ("c", "c"), ("taps", "taps_own")]
    pairs += [("gain", "gain_own"), ("left", "left"), ("twist", "twist")]
    pairs += [("right", "right"), ("back", "back"), ("swing", "swing")]
    for i, (src, dst) in enumerate(pairs):
        fetched[src] = pltpu.make_async_copy(
            getattr(r, src + "_hbm"), getattr(r, dst), r.fetch_sem.at[i]
        )
        fetched[src].start()

    per = nseq // nchan
    to_seq = nchan * lax.rem(me, per) + mine
    to_chan = lax.div(me, per)
    from_seq = per * mine + lax.div(me, nchan)
    from_chan = lax.rem(me, nchan)
    stays = jnp.logical_and(to_seq == me, to_chan == mine)

    barrier = pltpu.get_barrier_semaphore()

    def greet(step, carry):
        peer = lax.rem(me + step, nseq)
        pl.semaphore_signal(barrier, inc=1, device_id=(peer, mine), device_id_type=MESH)
        return carry

    lax.fori_loop(1, nseq, greet, 0)

    @pl.when(jnp.logical_not(stays))
    def _():
        pl.semaphore_signal(
            barrier, inc=1, device_id=(from_seq, from_chan), device_id_type=MESH
        )

    shape = (nseq, group, width)

    def paired(first, second):
        one = first[...].astype(F32).T.reshape(shape)
        two = second[...].astype(F32).T.reshape(shape)
        return jnp.concatenate([one, two], axis=1).astype(BF16)

    fetched["k"].wait()
    fetched["v"].wait()
    r.send_kv[...] = paired(r.k, r.v)

    @pl.when(stays)
    def _():
        pl.semaphore_wait(barrier, nseq - 1)

    @pl.when(jnp.logical_not(stays))
    def _():
        pl.semaphore_wait(barrier, nseq)

    def send_all(name):
        source, target = getattr(r, "send_" + name), getattr(r, "got_" + name)
        index = number[name]

        def body(step, carry):
            peer = away(me, step, nseq)
            pltpu.make_async_remote_copy(
                src_ref=source.at[peer],
                dst_ref=target.at[me],
                send_sem=r.send_sem.at[index],
                recv_sem=r.recv_sem.at[index],
                device_id=(peer, mine),
                device_id_type=MESH,
            ).start()
            return carry

        lax.fori_loop(1, nseq, body, 0)
        target[me] = source[me]

    def arrived(name):
        part = getattr(r, "got_" + name).at[pl.ds(0, nseq - 1)]
        pltpu.make_async_copy(part, part, r.recv_sem.at[number[name]]).wait()

    def sent(name):
        part = getattr(r, "send_" + name).at[pl.ds(0, nseq - 1)]
        pltpu.make_async_copy(part, part, r.send_sem.at[number[name]]).wait()

    send_all("kv")

    side_copies = [
        pltpu.make_async_remote_copy(
            src_ref=src,
            dst_ref=dst,
            send_sem=r.side_sem.at[i],
            recv_sem=r.side_sem.at[2 + i],
            device_id=(to_seq, to_chan),
            device_id_type=MESH,
        )
        for i, (src, dst) in enumerate([(r.taps_own, r.taps), (r.gain_own, r.gain)])
    ]
    fetched["taps"].wait()
    fetched["gain"].wait()

    @pl.when(jnp.logical_not(stays))
    def _():
        for copy in side_copies:
            copy.start()

    @pl.when(stays)
    def _():
        r.taps[...] = r.taps_own[...]
        r.gain[...] = r.gain_own[...]

    fetched["h"].wait()
    r.send_h[...], peak = encode(r.h[...].T.reshape(shape))
    r.send_hs[...] = packed_rows(nseq, group, {0: peak})
    send_all("h")
    send_all("hs")

    fetched["q"].wait()
    fetched["c"].wait()
    r.send_qc[...] = paired(r.q, r.c)
    send_all("qc")

    halo_copies = [
        pltpu.make_async_remote_copy(
            src_ref=src.at[pl.ds(rows - HALO, HALO)],
            dst_ref=r.halo.at[i],
            send_sem=r.halo_sem.at[i],
            recv_sem=r.halo_sem.at[3 + i],
            device_id=(lax.rem(me + 1, nseq), mine),
            device_id_type=MESH,
        )
        for i, src in enumerate([r.q, r.k, r.v])
    ]

    @pl.when(me < nseq - 1)
    def _():
        for copy in halo_copies:
            copy.start()

    @pl.when(me == 0)
    def _():
        r.halo[...] = jnp.zeros(r.halo.shape, BF16)

    @pl.when(jnp.logical_not(stays))
    def _():
        for copy in side_copies:
            copy.wait()

    diagonal = field_mask(group, 0)[0, :, :group]

    def column(row):
        spread_out = jnp.broadcast_to(row, (group, group))
        return jnp.sum(jnp.where(diagonal, spread_out, 0.0), axis=1, keepdims=True)

    taps = [[column(r.taps[s, i : i + 1, :]) for i in range(3)] for s in range(3)]
    gain = column(r.gain[...])
    for name in ("left", "twist", "right", "back", "swing"):
        fetched[name].wait()

    half = width // 2
    swing = [r.swing[i, :1, :] for i in range(2)]

    def over_lanes(real, imag):
        high_real, low_real = split(real)
        high_imag, low_imag = split(imag)
        parts = [high_real, high_imag, low_real, low_imag, high_real, high_imag]
        for i, part in enumerate(parts):
            r.lanes[:, i * half : (i + 1) * half] = part
        return dot(r.lanes[...], r.right[...])

    def forward(signal, spec):
        high, low = split(signal.reshape(rows, width))
        for i, part in enumerate([high, low, high]):
            r.stack[i * rows : (i + 1) * rows, :] = part
        wave = dot(r.left[...], r.stack[: 3 * rows, :])
        real, imag = wave[:rows], wave[rows:]
        cosine, sine = r.twist[0], r.twist[1]
        real, imag = real * cosine + imag * sine, imag * cosine - real * sine
        gap_real, gap_imag = real[:, :half] - real[:, half:], imag[:, :half] - imag[:, half:]
        spec[...] = over_lanes(
            jnp.concatenate(
                [
                    real[:, :half] + real[:, half:],
                    gap_real * swing[0] + gap_imag * swing[1],
                ],
                axis=0,
            ),
            jnp.concatenate(
                [
                    imag[:, :half] + imag[:, half:],
                    gap_imag * swing[0] - gap_real * swing[1],
                ],
                axis=0,
            ),
        )

    def inverse(left_spec, right_spec, conjugate):
        a_re, a_im = left_spec[:, :half], left_spec[:, half:]
        b_re, b_im = right_spec[:, :half], right_spec[:, half:]
        if conjugate:
            real, imag = a_re * b_re + a_im * b_im, a_im * b_re - a_re * b_im
        else:
            real, imag = a_re * b_re - a_im * b_im, -(a_re * b_im + a_im * b_re)
        wave = over_lanes(real, imag)
        even_real, even_imag = wave[:rows, :half], wave[:rows, half:]
        odd_real, odd_imag = wave[rows:, :half], wave[rows:, half:]
        odd_real, odd_imag = (
            odd_real * swing[0] + odd_imag * swing[1],
            odd_imag * swing[0] - odd_real * swing[1],
        )
        wave_real = jnp.concatenate([even_real + odd_real, even_real - odd_real], axis=1)
        wave_imag = jnp.concatenate([even_imag + odd_imag, even_imag - odd_imag], axis=1)
        cosine, sine = r.twist[0], r.twist[1]
        high_real, low_real = split(wave_real * cosine + wave_imag * sine)
        high_imag, low_imag = split(wave_real * sine - wave_imag * cosine)
        parts = [high_real, high_imag, low_real, low_imag, high_real, high_imag]
        for i, part in enumerate(parts):
            r.stack[i * rows : (i + 1) * rows, :] = part
        return dot(r.back[...], r.stack[...]).reshape(shape)

    def short(value, keep, coeffs):
        one, two = delayed(value, 1), delayed(value, 2)
        keep[0] = one
        keep[1] = two
        return coeffs[0] * value + coeffs[1] * one + coeffs[2] * two

    arrived("kv")
    both = r.got_kv[...].astype(F32)
    r.x_k[...] = both[:, :group]
    r.x_v[...] = both[:, group:]
    r.key_conv[...] = short(r.x_k[...], r.d_k, taps[1])
    r.value_conv[...] = short(r.x_v[...], r.d_v, taps[2])
    r.x_p[...] = r.key_conv[...] * r.value_conv[...]
    forward(r.x_p[...], r.spec_p)

    arrived("h")
    arrived("hs")
    forward(decode(r.got_h[...], unpacked(r.got_hs[...], group, 0)), r.spec_h)
    r.x_m[...] = inverse(r.spec_h, r.spec_p, False) + gain * r.x_p[...]
    r.send_m[...], peak = encode(r.x_m[...])
    fields = {3 * s + i: taps[s][i] for s in range(3) for i in range(3)}
    r.send_ms[...] = packed_rows(nseq, group, {**fields, 9: peak})
    send_all("m")
    send_all("ms")

    arrived("qc")
    both = r.got_qc[...].astype(F32)
    r.x_q[...] = both[:, :group]
    r.x_c[...] = both[:, group:]
    r.x_g[...] = r.x_c[...] * short(r.x_q[...], r.d_q, taps[0])
    forward(r.x_g[...], r.spec_g)
    r.x_pg[...] = inverse(r.spec_h, r.spec_g, True) + gain * r.x_g[...]
    r.send_p[...], peak = encode(r.x_pg[...])
    send_all("p")

    grads = [
        (r.x_c[...] * r.x_m[...], r.x_q, r.d_q),
        (r.x_pg[...] * r.value_conv[...], r.x_k, r.d_k),
        (r.x_pg[...] * r.key_conv[...], r.x_v, r.d_v),
    ]
    fields = {9: scale * total_of(r.x_g[...] * r.x_p[...])}
    for s, (grad, stream, moved) in enumerate(grads):
        fields[3 * s] = scale * total_of(grad * stream[...])
        fields[3 * s + 1] = scale * total_of(grad * moved[0])
        fields[3 * s + 2] = scale * total_of(grad * moved[1])
        fields[10 + 2 * s], fields[11 + 2 * s] = block_ends(grad, taps[s])
    r.send_s[:, :, :128] = packed_rows(nseq, group, fields)
    r.send_s[:, :, 128:] = packed_rows(nseq, group, {0: peak})
    send_all("s")
    r.send_f[...], peak = encode(scale * inverse(r.spec_p, r.spec_g, True))
    send_all("f")
    r.send_fs[...] = packed_rows(nseq, group, {0: peak})
    send_all("fs")

    def spread(grad, s):
        return (
            tap_row(s, 0) * grad
            + tap_row(s, 1) * pltpu.roll(grad, rows - 1, 0)
            + tap_row(s, 2) * pltpu.roll(grad, rows - 2, 0)
        ).astype(BF16)

    def in_rows(name, side, field):
        return decode(getattr(r, "got_" + name)[...], unpacked(side, group, field)).reshape(
            rows, width
        ).T

    arrived("ms")
    for i, row in enumerate(channel_rows(r.got_ms[...].reshape(nseq, 128), 9, group)):
        r.taps_row[i : i + 1, :] = row

    @pl.when(me > 0)
    def _():
        for copy in halo_copies:
            copy.wait_recv()

    def tap_row(s, i):
        return r.taps_row[3 * s + i : 3 * s + i + 1, :]

    for s, src in enumerate([r.q, r.k, r.v]):
        own = src[...].astype(F32)
        above = r.halo[s].astype(F32)
        r.conv_rows[s] = (
            tap_row(s, 0) * own
            + tap_row(s, 1) * later(own, above, 1)
            + tap_row(s, 2) * later(own, above, 2)
        )

    arrived("m")
    mixed = in_rows("m", r.got_ms[...], 9)
    r.go[...] = (r.conv_rows[0] * mixed).astype(BF16)
    r.qg[...] = spread(r.c[...].astype(F32) * mixed, 0)
    arrived("p")
    arrived("s")
    product_grad = in_rows("p", r.got_s[:, :, 128:], 0)
    r.kg[...] = spread(product_grad * r.conv_rows[2], 1)
    r.vg[...] = spread(product_grad * r.conv_rows[1], 2)
    finals = channel_rows(r.got_s[:, :, :128].reshape(nseq, 128), 16, group)
    place = lax.broadcasted_iota(jnp.int32, (HALO, width), 0)
    for i, grad in enumerate([r.qg, r.kg, r.vg]):
        last = grad[rows - HALO :, :].astype(F32)
        last = jnp.where(place == HALO - 2, finals[10 + 2 * i], last)
        last = jnp.where(place == HALO - 1, finals[11 + 2 * i], last)
        grad[rows - HALO :, :] = last.astype(BF16)
    for i in range(9):
        r.taps_grad[i // 3, i % 3 : i % 3 + 1, :] = finals[i]
    r.gain_grad[...] = finals[9]
    arrived("f")
    arrived("fs")
    r.fg[...] = in_rows("f", r.got_fs[...], 0)

    for name in MESSAGES:
        sent(name)

    @pl.when(me < nseq - 1)
    def _():
        for copy in halo_copies:
            copy.wait_send()


def deliver(*refs):
    count = len(refs) // 2
    copies = [
        pltpu.make_async_copy(refs[i], refs[count + i], refs[-1].at[i]) for i in range(count)
    ]
    for copy in copies:
        copy.start()
    for copy in copies:
        copy.wait()


def per_device(query_rows, key_rows, value_rows, long_filter, short_taps, skip_gain, cotangent):
    rows, channels = query_rows.shape
    nseq, nchan = lax.axis_size("seq"), lax.axis_size("chan")
    group = channels // nseq
    scale = 1.0 / math.sqrt(rows * nseq)
    tables = [jnp.asarray(t) for t in transform_tables(nseq, rows, group)]
    vmem = pl.BlockSpec(memory_space=pltpu.VMEM)
    hbm = pl.BlockSpec(memory_space=pltpu.HBM)
    inputs = {
        "q_hbm": query_rows,
        "k_hbm": key_rows,
        "v_hbm": value_rows,
        "c_hbm": cotangent,
        "h_hbm": long_filter,
        "taps_hbm": short_taps,
        "gain_hbm": skip_gain[None],
        "left_hbm": tables[0],
        "back_hbm": tables[1],
        "right_hbm": tables[2],
        "twist_hbm": tables[3],
        "swing_hbm": tables[4],
    }
    block = jax.ShapeDtypeStruct((rows, channels), BF16)
    results = {
        "go": block,
        "qg": block,
        "kg": block,
        "vg": block,
        "fg": jax.ShapeDtypeStruct((rows, channels), F32),
        "taps_grad": jax.ShapeDtypeStruct((3, 3, channels), F32),
        "gain_grad": jax.ShapeDtypeStruct((1, channels), F32),
    }
    local = pltpu.VMEM((rows, channels), BF16)
    taps, gain = pltpu.VMEM((3, 3, group), F32), pltpu.VMEM((1, group), F32)
    scratch = dict(
        q=local,
        k=local,
        v=local,
        c=local,
        h=pltpu.VMEM((rows, channels), F32),
        taps_own=taps,
        gain_own=gain,
        taps=taps,
        gain=gain,
        halo=pltpu.VMEM((3, HALO, channels), BF16),
        taps_row=pltpu.VMEM((16, channels), F32),
        conv_rows=pltpu.VMEM((3, rows, channels), F32),
    )
    for name, table in zip(("left", "back", "right", "twist", "swing"), tables):
        scratch[name] = pltpu.VMEM(table.shape, table.dtype)
    for name in MESSAGES:
        if name in ("kv", "qc"):
            kind = pltpu.VMEM((nseq, 2 * group, rows), BF16)
        elif name in ("h", "m", "p", "f"):
            kind = pltpu.VMEM((nseq, 2 * group, rows // 2), BF16)
        else:
            kind = pltpu.VMEM((nseq, 1, 256 if name == "s" else 128), F32)
        scratch["send_" + name] = scratch["got_" + name] = kind
    for name in ("x_q", "x_k", "x_v", "x_c", "x_p", "x_g", "x_m", "x_pg", "key_conv", "value_conv"):
        scratch[name] = pltpu.VMEM((nseq, group, rows), F32)
    for name in ("d_q", "d_k", "d_v"):
        scratch[name] = pltpu.VMEM((2, nseq, group, rows), F32)
    for name in ("spec_h", "spec_p", "spec_g"):
        scratch[name] = pltpu.VMEM((2 * nseq * group, rows), F32)
    scratch["lanes"] = pltpu.VMEM((2 * nseq * group, 3 * rows), BF16)
    scratch["stack"] = pltpu.VMEM((6 * nseq * group, rows), BF16)
    scratch["fetch_sem"] = pltpu.SemaphoreType.DMA((12,))
    scratch["send_sem"] = pltpu.SemaphoreType.DMA((len(MESSAGES),))
    scratch["recv_sem"] = pltpu.SemaphoreType.DMA((len(MESSAGES),))
    scratch["side_sem"] = pltpu.SemaphoreType.DMA((4,))
    scratch["halo_sem"] = pltpu.SemaphoreType.DMA((6,))
    names = tuple(inputs) + tuple(results) + tuple(scratch)
    outs = pl.pallas_call(
        functools.partial(kernel, names, nseq, nchan, group, scale),
        out_shape=tuple(results.values()),
        in_specs=[hbm] * len(inputs),
        out_specs=[vmem] * len(results),
        scratch_shapes=list(scratch.values()),
        compiler_params=pltpu.CompilerParams(
            collective_id=0, has_side_effects=True, vmem_limit_bytes=44 << 20
        ),
        name="hyena",
    )(*[pltpu.with_memory_space_constraint(x, pltpu.HBM) for x in inputs.values()])
    moved = pl.pallas_call(
        deliver,
        out_shape=tuple(results.values()),
        in_specs=[vmem] * len(results),
        out_specs=[hbm] * len(results),
        scratch_shapes=[pltpu.SemaphoreType.DMA((len(results),))],
        compiler_params=pltpu.CompilerParams(vmem_limit_bytes=16 << 20),
        name="deliver",
    )(*outs)
    return tuple(moved[:6]) + (moved[6].reshape(channels),)


def solution(mesh):
    in_specs = (
        P("seq", "chan"),
        P("seq", "chan"),
        P("seq", "chan"),
        P("seq", "chan"),
        P(None, None, ("seq", "chan")),
        P(("seq", "chan")),
        P("seq", "chan"),
    )
    out_specs = (
        P("seq", "chan"),
        P("seq", "chan"),
        P("seq", "chan"),
        P("seq", "chan"),
        P("seq", "chan"),
        P(None, None, "chan"),
        P("chan"),
    )
    return jax.shard_map(
        per_device, mesh=mesh, in_specs=in_specs, out_specs=out_specs, check_vma=False
    )
```

```python
import functools
import math
import types

import jax
import jax.numpy as jnp
import ml_dtypes
import numpy as np
from jax import lax
from jax.experimental import pallas as pl
from jax.experimental.pallas import tpu as pltpu
from jax.sharding import PartitionSpec as P

F32 = jnp.float32
BF16 = jnp.bfloat16
MESH = pl.DeviceIdType.MESH
REACH = 125.0 * math.log(2.0)


def halves(table):
    high = table.astype(np.float32).astype(ml_dtypes.bfloat16)
    low = (table - high.astype(np.float64)).astype(np.float32).astype(ml_dtypes.bfloat16)
    return np.stack([high, low])


def transform_tables(blocks, width, group):
    total = blocks * width
    shifted = np.arange(blocks) - 0.25
    outer = 2.0 * np.pi / blocks * np.outer(shifted, np.arange(blocks))
    eye = np.eye(group)
    left = np.concatenate([np.kron(np.cos(outer), eye), np.kron(-np.sin(outer), eye)], axis=0)
    back = left.T / total
    half = width // 2
    inner = 2.0 * np.pi / half * (np.outer(np.arange(half), np.arange(half)) % half)
    cosine, sine = halves(np.cos(inner)), halves(np.sin(inner))
    right = np.concatenate(
        [np.block([[cosine[i], -sine[i]], [sine[i], cosine[i]]]) for i in (0, 0, 1)]
    )
    step = 2.0 * np.pi / width * np.arange(half)
    swing = np.stack([np.tile(f(step), (8, 1)) for f in (np.cos, np.sin)]).astype(np.float32)
    turn = 2.0 * np.pi / total * np.outer(shifted, np.arange(width))
    twist = np.stack([np.cos(turn), np.sin(turn)]).astype(np.float32)
    twist = np.repeat(twist, group, axis=1)
    left, back = halves(left), halves(back)
    left = np.concatenate([left[0], left[0], left[1]], axis=1)
    left = left.reshape(2, 2, -1, left.shape[1]).swapaxes(0, 1).reshape(left.shape)
    back = np.concatenate([back[0], back[0], back[1]], axis=1)
    return left, back, right, twist, swing


def split(value):
    high = value.astype(BF16)
    return high, (value - high.astype(F32)).astype(BF16)


def dot(left, right):
    return jnp.dot(left, right, preferred_element_type=F32)


def delayed(value, steps):
    before = jnp.concatenate([jnp.zeros_like(value[:1]), value[:-1]], axis=0)
    lane = lax.broadcasted_iota(jnp.int32, value.shape, 2)
    return jnp.where(
        lane < steps, pltpu.roll(before, steps, 2), pltpu.roll(value, steps, 2)
    )


def later(value, head, steps):
    return pltpu.roll(jnp.concatenate([head, value], axis=0), steps, 0)[head.shape[0] :]


def block_ends(grad, coeffs):
    half = grad.shape[2] // 2
    low, high = grad[:, :, :half], grad[:, :, half:]
    after = jnp.concatenate([low[1:], jnp.zeros_like(low[:1])], axis=0)
    lane = lax.broadcasted_iota(jnp.int32, high.shape, 2)
    total = coeffs[0] * high
    for steps in (1, 2):
        moved = jnp.where(
            lane < half - steps,
            pltpu.roll(high, half - steps, 2),
            pltpu.roll(after, half - steps, 2),
        )
        total = total + coeffs[steps] * moved
    return [
        jnp.sum(jnp.where(lane == half - back, total, 0.0), axis=2, keepdims=True)
        for back in (2, 1)
    ]


def total_of(value):
    return jnp.sum(jnp.sum(value, axis=0), axis=1, keepdims=True)


def encode(value):
    peak = jnp.maximum(jnp.max(jnp.abs(value), axis=2, keepdims=True), 1e-30)
    code = jnp.exp(jnp.abs(value) * (2.0 * REACH / peak) - REACH)
    code = jnp.where(value < 0.0, -code, code)
    half = value.shape[2] // 2
    return jnp.concatenate([code[:, :, :half], code[:, :, half:]], axis=1).astype(BF16), peak


def decode(code, peak):
    group = code.shape[1] // 2
    code = code.astype(F32)
    code = jnp.concatenate([code[:, :group], code[:, group:]], axis=2)
    size = (jnp.log(jnp.abs(code)) + REACH) * (peak * (0.5 / REACH))
    return jnp.where(code < 0.0, -size, size)


def field_mask(group, field):
    lane = lax.broadcasted_iota(jnp.int32, (1, group, 128), 2)
    return lane == group * field + lax.broadcasted_iota(jnp.int32, (1, group, 128), 1)


def packed_rows(count, group, fields):
    wide = jnp.zeros((count, group, 128), F32)
    for field, value in fields.items():
        wide = jnp.where(field_mask(group, field), value, wide)
    return jnp.sum(wide, axis=1, keepdims=True)


def unpacked(rows, group, field):
    wide = jnp.broadcast_to(rows, (rows.shape[0], group, 128))
    return jnp.sum(jnp.where(field_mask(group, field), wide, 0.0), axis=2, keepdims=True)


def channel_rows(table, count, group):
    owners = table.shape[0]
    width = owners * group
    turned = jnp.concatenate(
        [table if f == 0 else pltpu.roll(table, 128 - group * f, 1) for f in range(count)],
        axis=0,
    )
    channel = lax.broadcasted_iota(jnp.int32, (128, width), 1)
    pick = lax.rem(channel, group) == lax.broadcasted_iota(jnp.int32, (128, width), 0)
    pick = pick.astype(F32).astype(BF16)
    high, low = split(turned)
    wide = (dot(high, pick) + dot(low, pick)).reshape(count, owners, width)
    owner = lax.div(lax.broadcasted_iota(jnp.int32, (owners, width), 1), group)
    keep = owner == lax.broadcasted_iota(jnp.int32, (owners, width), 0)
    return [jnp.sum(jnp.where(keep, wide[f], 0.0), axis=0, keepdims=True) for f in range(count)]


HALO = 16
DEPTH = 8


def farthest(step, length):
    away_by = lax.div(step + 1, 2)
    return jnp.where(lax.rem(step, 2) == 1, length // 2 - away_by, length // 2 + away_by)


def away(me, step, count):
    planes = count // DEPTH
    across = farthest(lax.div(step - 1, DEPTH), planes)
    along = farthest(lax.rem(step - 1, DEPTH), DEPTH)
    plane = lax.rem(lax.div(me, DEPTH) + across, planes)
    return DEPTH * plane + lax.rem(lax.rem(me, DEPTH) + along, DEPTH)


MESSAGES = ("kv", "h", "hs", "qc", "m", "ms", "p", "s", "f", "fs")


def kernel(names, nseq, nchan, group, scale, *refs):
    r = types.SimpleNamespace(**dict(zip(names, refs, strict=True)))
    me = lax.axis_index("seq")
    mine = lax.axis_index("chan")
    rows, width = r.q_hbm.shape
    number = {name: i for i, name in enumerate(MESSAGES)}

    fetched = {}
    pairs = [("k", "k"), ("v", "v"), ("h", "h"), ("q", "q"), ("c", "c"), ("taps", "taps_own")]
    pairs += [("gain", "gain_own"), ("left", "left"), ("twist", "twist")]
    pairs += [("right", "right"), ("back", "back"), ("swing", "swing")]
    for i, (src, dst) in enumerate(pairs):
        fetched[src] = pltpu.make_async_copy(
            getattr(r, src + "_hbm"), getattr(r, dst), r.fetch_sem.at[i]
        )
        fetched[src].start()

    per = nseq // nchan
    to_seq = nchan * lax.rem(me, per) + mine
    to_chan = lax.div(me, per)
    from_seq = per * mine + lax.div(me, nchan)
    from_chan = lax.rem(me, nchan)
    stays = jnp.logical_and(to_seq == me, to_chan == mine)

    barrier = pltpu.get_barrier_semaphore()

    def greet(step, carry):
        peer = lax.rem(me + step, nseq)
        pl.semaphore_signal(barrier, inc=1, device_id=(peer, mine), device_id_type=MESH)
        return carry

    lax.fori_loop(1, nseq, greet, 0)

    @pl.when(jnp.logical_not(stays))
    def _():
        pl.semaphore_signal(
            barrier, inc=1, device_id=(from_seq, from_chan), device_id_type=MESH
        )

    shape = (nseq, group, width)

    def paired(first, second):
        one = first[...].astype(F32).T.reshape(shape)
        two = second[...].astype(F32).T.reshape(shape)
        return jnp.concatenate([one, two], axis=1).astype(BF16)

    fetched["k"].wait()
    fetched["v"].wait()
    r.send_kv[...] = paired(r.k, r.v)

    @pl.when(stays)
    def _():
        pl.semaphore_wait(barrier, nseq - 1)

    @pl.when(jnp.logical_not(stays))
    def _():
        pl.semaphore_wait(barrier, nseq)

    def send_all(name, unroll=1):
        source, target = getattr(r, "send_" + name), getattr(r, "got_" + name)
        index = number[name]

        def body(step, carry):
            peer = away(me, step, nseq)
            pltpu.make_async_remote_copy(
                src_ref=source.at[peer],
                dst_ref=target.at[me],
                send_sem=r.send_sem.at[index],
                recv_sem=r.recv_sem.at[index],
                device_id=(peer, mine),
                device_id_type=MESH,
            ).start()
            return carry

        lax.fori_loop(1, nseq, body, 0, unroll=unroll)
        target[me] = source[me]

    def arrived(name):
        part = getattr(r, "got_" + name).at[pl.ds(0, nseq - 1)]
        pltpu.make_async_copy(part, part, r.recv_sem.at[number[name]]).wait()

    def sent(name):
        part = getattr(r, "send_" + name).at[pl.ds(0, nseq - 1)]
        pltpu.make_async_copy(part, part, r.send_sem.at[number[name]]).wait()

    send_all("kv")

    side_copies = [
        pltpu.make_async_remote_copy(
            src_ref=src,
            dst_ref=dst,
            send_sem=r.side_sem.at[i],
            recv_sem=r.side_sem.at[2 + i],
            device_id=(to_seq, to_chan),
            device_id_type=MESH,
        )
        for i, (src, dst) in enumerate([(r.taps_own, r.taps), (r.gain_own, r.gain)])
    ]
    fetched["taps"].wait()
    fetched["gain"].wait()

    @pl.when(jnp.logical_not(stays))
    def _():
        for copy in side_copies:
            copy.start()

    @pl.when(stays)
    def _():
        r.taps[...] = r.taps_own[...]
        r.gain[...] = r.gain_own[...]

    fetched["h"].wait()
    r.send_h[...], peak = encode(r.h[...].T.reshape(shape))
    r.send_hs[...] = packed_rows(nseq, group, {0: peak})
    send_all("h")
    send_all("hs")

    fetched["q"].wait()
    fetched["c"].wait()
    r.send_qc[...] = paired(r.q, r.c)
    send_all("qc")

    halo_copies = [
        pltpu.make_async_remote_copy(
            src_ref=src.at[pl.ds(rows - HALO, HALO)],
            dst_ref=r.halo.at[i],
            send_sem=r.halo_sem.at[i],
            recv_sem=r.halo_sem.at[3 + i],
            device_id=(lax.rem(me + 1, nseq), mine),
            device_id_type=MESH,
        )
        for i, src in enumerate([r.q, r.k, r.v])
    ]

    @pl.when(me < nseq - 1)
    def _():
        for copy in halo_copies:
            copy.start()

    @pl.when(me == 0)
    def _():
        r.halo[...] = jnp.zeros(r.halo.shape, BF16)

    @pl.when(jnp.logical_not(stays))
    def _():
        for copy in side_copies:
            copy.wait()

    diagonal = field_mask(group, 0)[0, :, :group]

    def column(row):
        spread_out = jnp.broadcast_to(row, (group, group))
        return jnp.sum(jnp.where(diagonal, spread_out, 0.0), axis=1, keepdims=True)

    taps = [[column(r.taps[s, i : i + 1, :]) for i in range(3)] for s in range(3)]
    gain = column(r.gain[...])
    for name in ("left", "twist", "right", "back", "swing"):
        fetched[name].wait()

    half = width // 2
    swing = [r.swing[i, :1, :] for i in range(2)]

    part_rows = rows // 2

    def over_lanes(block, real, imag):
        place = slice(block * rows, (block + 1) * rows)
        high_real, low_real = split(real)
        high_imag, low_imag = split(imag)
        parts = [high_real, high_imag, low_real, low_imag, high_real, high_imag]
        for i, part in enumerate(parts):
            r.lanes[place, i * half : (i + 1) * half] = part
        return dot(r.lanes[place, :], r.right[...])

    def forward(signal, spec):
        high, low = split(signal.reshape(rows, width))
        for i, part in enumerate([high, low, high]):
            r.stack[i * rows : (i + 1) * rows, :] = part
        waves = [
            dot(r.left[block * rows : (block + 1) * rows, :], r.stack[: 3 * rows, :])
            for block in range(2)
        ]
        for block, wave in enumerate(waves):
            real, imag = wave[:part_rows], wave[part_rows:]
            turn = slice(block * part_rows, (block + 1) * part_rows)
            cosine, sine = r.twist[0, turn, :], r.twist[1, turn, :]
            real, imag = real * cosine + imag * sine, imag * cosine - real * sine
            gap_real = real[:, :half] - real[:, half:]
            gap_imag = imag[:, :half] - imag[:, half:]
            even_real, even_imag = real[:, :half] + real[:, half:], imag[:, :half] + imag[:, half:]
            odd_real = gap_real * swing[0] + gap_imag * swing[1]
            odd_imag = gap_imag * swing[0] - gap_real * swing[1]
            spec[block * rows : (block + 1) * rows, :] = over_lanes(
                block,
                jnp.concatenate([even_real, odd_real], axis=0),
                jnp.concatenate([even_imag, odd_imag], axis=0),
            )

    def inverse(left_spec, right_spec, conjugate):
        waves = []
        for block in range(2):
            place = slice(block * rows, (block + 1) * rows)
            a_re, a_im = left_spec[place, :half], left_spec[place, half:]
            b_re, b_im = right_spec[place, :half], right_spec[place, half:]
            if conjugate:
                real, imag = a_re * b_re + a_im * b_im, a_im * b_re - a_re * b_im
            else:
                real, imag = a_re * b_re - a_im * b_im, -(a_re * b_im + a_im * b_re)
            waves.append(over_lanes(block, real, imag))
        for block, wave in enumerate(waves):
            even_real, even_imag = wave[:part_rows, :half], wave[:part_rows, half:]
            odd_real, odd_imag = wave[part_rows:, :half], wave[part_rows:, half:]
            odd_real, odd_imag = (
                odd_real * swing[0] + odd_imag * swing[1],
                odd_imag * swing[0] - odd_real * swing[1],
            )
            wave_real = jnp.concatenate([even_real + odd_real, even_real - odd_real], axis=1)
            wave_imag = jnp.concatenate([even_imag + odd_imag, even_imag - odd_imag], axis=1)
            turn = slice(block * part_rows, (block + 1) * part_rows)
            cosine, sine = r.twist[0, turn, :], r.twist[1, turn, :]
            high_real, low_real = split(wave_real * cosine + wave_imag * sine)
            high_imag, low_imag = split(wave_real * sine - wave_imag * cosine)
            parts = [high_real, high_imag, low_real, low_imag, high_real, high_imag]
            for i, part in enumerate(parts):
                start = i * rows + block * part_rows
                r.stack[start : start + part_rows, :] = part
        return dot(r.back[...], r.stack[...]).reshape(shape)

    def short(value, keep, coeffs):
        one, two = delayed(value, 1), delayed(value, 2)
        keep[0] = one
        keep[1] = two
        return coeffs[0] * value + coeffs[1] * one + coeffs[2] * two

    arrived("kv")
    both = r.got_kv[...].astype(F32)
    r.x_k[...] = both[:, :group]
    r.x_v[...] = both[:, group:]
    r.key_conv[...] = short(r.x_k[...], r.d_k, taps[1])
    r.value_conv[...] = short(r.x_v[...], r.d_v, taps[2])
    r.x_p[...] = r.key_conv[...] * r.value_conv[...]
    forward(r.x_p[...], r.spec_p)

    arrived("h")
    arrived("hs")
    forward(decode(r.got_h[...], unpacked(r.got_hs[...], group, 0)), r.spec_h)
    r.x_m[...] = inverse(r.spec_h, r.spec_p, False) + gain * r.x_p[...]
    r.send_m[...], peak = encode(r.x_m[...])
    fields = {3 * s + i: taps[s][i] for s in range(3) for i in range(3)}
    r.send_ms[...] = packed_rows(nseq, group, {**fields, 9: peak})
    send_all("m")
    send_all("ms")

    arrived("qc")
    both = r.got_qc[...].astype(F32)
    r.x_q[...] = both[:, :group]
    r.x_c[...] = both[:, group:]
    r.x_g[...] = r.x_c[...] * short(r.x_q[...], r.d_q, taps[0])
    forward(r.x_g[...], r.spec_g)
    r.x_pg[...] = inverse(r.spec_h, r.spec_g, True) + gain * r.x_g[...]
    r.send_p[...], peak = encode(r.x_pg[...])
    send_all("p", nseq - 1)

    grads = [
        (r.x_c[...] * r.x_m[...], r.x_q, r.d_q),
        (r.x_pg[...] * r.value_conv[...], r.x_k, r.d_k),
        (r.x_pg[...] * r.key_conv[...], r.x_v, r.d_v),
    ]
    fields = {9: scale * total_of(r.x_g[...] * r.x_p[...])}
    for s, (grad, stream, moved) in enumerate(grads):
        fields[3 * s] = scale * total_of(grad * stream[...])
        fields[3 * s + 1] = scale * total_of(grad * moved[0])
        fields[3 * s + 2] = scale * total_of(grad * moved[1])
        fields[10 + 2 * s], fields[11 + 2 * s] = block_ends(grad, taps[s])
    r.send_s[:, :, :128] = packed_rows(nseq, group, fields)
    r.send_s[:, :, 128:] = packed_rows(nseq, group, {0: peak})
    send_all("s", nseq - 1)
    r.send_f[...], peak = encode(scale * inverse(r.spec_p, r.spec_g, True))
    send_all("f")
    r.send_fs[...] = packed_rows(nseq, group, {0: peak})
    send_all("fs")

    def spread(grad, s):
        return (
            tap_row(s, 0) * grad
            + tap_row(s, 1) * pltpu.roll(grad, rows - 1, 0)
            + tap_row(s, 2) * pltpu.roll(grad, rows - 2, 0)
        ).astype(BF16)

    def in_rows(name, side, field):
        return decode(getattr(r, "got_" + name)[...], unpacked(side, group, field)).reshape(
            rows, width
        ).T

    arrived("ms")
    for i, row in enumerate(channel_rows(r.got_ms[...].reshape(nseq, 128), 9, group)):
        r.taps_row[i : i + 1, :] = row

    @pl.when(me > 0)
    def _():
        for copy in halo_copies:
            copy.wait_recv()

    def tap_row(s, i):
        return r.taps_row[3 * s + i : 3 * s + i + 1, :]

    for s, src in enumerate([r.q, r.k, r.v]):
        own = src[...].astype(F32)
        above = r.halo[s].astype(F32)
        r.conv_rows[s] = (
            tap_row(s, 0) * own
            + tap_row(s, 1) * later(own, above, 1)
            + tap_row(s, 2) * later(own, above, 2)
        )

    arrived("m")
    mixed = in_rows("m", r.got_ms[...], 9)
    r.go[...] = (r.conv_rows[0] * mixed).astype(BF16)
    r.qg[...] = spread(r.c[...].astype(F32) * mixed, 0)
    arrived("p")
    arrived("s")
    product_grad = in_rows("p", r.got_s[:, :, 128:], 0)
    r.kg[...] = spread(product_grad * r.conv_rows[2], 1)
    r.vg[...] = spread(product_grad * r.conv_rows[1], 2)
    finals = channel_rows(r.got_s[:, :, :128].reshape(nseq, 128), 16, group)
    place = lax.broadcasted_iota(jnp.int32, (HALO, width), 0)
    for i, grad in enumerate([r.qg, r.kg, r.vg]):
        last = grad[rows - HALO :, :].astype(F32)
        last = jnp.where(place == HALO - 2, finals[10 + 2 * i], last)
        last = jnp.where(place == HALO - 1, finals[11 + 2 * i], last)
        grad[rows - HALO :, :] = last.astype(BF16)
    for i in range(9):
        r.taps_grad[i // 3, i % 3 : i % 3 + 1, :] = finals[i]
    r.gain_grad[...] = finals[9]
    arrived("f")
    arrived("fs")
    r.fg[...] = in_rows("f", r.got_fs[...], 0)

    for name in MESSAGES:
        sent(name)

    @pl.when(me < nseq - 1)
    def _():
        for copy in halo_copies:
            copy.wait_send()


def deliver(*refs):
    count = len(refs) // 2
    copies = [
        pltpu.make_async_copy(refs[i], refs[count + i], refs[-1].at[i]) for i in range(count)
    ]
    for copy in copies:
        copy.start()
    for copy in copies:
        copy.wait()


def per_device(query_rows, key_rows, value_rows, long_filter, short_taps, skip_gain, cotangent):
    rows, channels = query_rows.shape
    nseq, nchan = lax.axis_size("seq"), lax.axis_size("chan")
    group = channels // nseq
    scale = 1.0 / math.sqrt(rows * nseq)
    tables = [jnp.asarray(t) for t in transform_tables(nseq, rows, group)]
    vmem = pl.BlockSpec(memory_space=pltpu.VMEM)
    hbm = pl.BlockSpec(memory_space=pltpu.HBM)
    inputs = {
        "q_hbm": query_rows,
        "k_hbm": key_rows,
        "v_hbm": value_rows,
        "c_hbm": cotangent,
        "h_hbm": long_filter,
        "taps_hbm": short_taps,
        "gain_hbm": skip_gain[None],
        "left_hbm": tables[0],
        "back_hbm": tables[1],
        "right_hbm": tables[2],
        "twist_hbm": tables[3],
        "swing_hbm": tables[4],
    }
    block = jax.ShapeDtypeStruct((rows, channels), BF16)
    results = {
        "go": block,
        "qg": block,
        "kg": block,
        "vg": block,
        "fg": jax.ShapeDtypeStruct((rows, channels), F32),
        "taps_grad": jax.ShapeDtypeStruct((3, 3, channels), F32),
        "gain_grad": jax.ShapeDtypeStruct((1, channels), F32),
    }
    local = pltpu.VMEM((rows, channels), BF16)
    taps, gain = pltpu.VMEM((3, 3, group), F32), pltpu.VMEM((1, group), F32)
    scratch = dict(
        q=local,
        k=local,
        v=local,
        c=local,
        h=pltpu.VMEM((rows, channels), F32),
        taps_own=taps,
        gain_own=gain,
        taps=taps,
        gain=gain,
        halo=pltpu.VMEM((3, HALO, channels), BF16),
        taps_row=pltpu.VMEM((16, channels), F32),
        conv_rows=pltpu.VMEM((3, rows, channels), F32),
    )
    for name, table in zip(("left", "back", "right", "twist", "swing"), tables):
        scratch[name] = pltpu.VMEM(table.shape, table.dtype)
    for name in MESSAGES:
        if name in ("kv", "qc"):
            kind = pltpu.VMEM((nseq, 2 * group, rows), BF16)
        elif name in ("h", "m", "p", "f"):
            kind = pltpu.VMEM((nseq, 2 * group, rows // 2), BF16)
        else:
            kind = pltpu.VMEM((nseq, 1, 256 if name == "s" else 128), F32)
        scratch["send_" + name] = scratch["got_" + name] = kind
    for name in ("x_q", "x_k", "x_v", "x_c", "x_p", "x_g", "x_m", "x_pg", "key_conv", "value_conv"):
        scratch[name] = pltpu.VMEM((nseq, group, rows), F32)
    for name in ("d_q", "d_k", "d_v"):
        scratch[name] = pltpu.VMEM((2, nseq, group, rows), F32)
    for name in ("spec_h", "spec_p", "spec_g"):
        scratch[name] = pltpu.VMEM((2 * nseq * group, rows), F32)
    scratch["lanes"] = pltpu.VMEM((2 * nseq * group, 3 * rows), BF16)
    scratch["stack"] = pltpu.VMEM((6 * nseq * group, rows), BF16)
    scratch["fetch_sem"] = pltpu.SemaphoreType.DMA((12,))
    scratch["send_sem"] = pltpu.SemaphoreType.DMA((len(MESSAGES),))
    scratch["recv_sem"] = pltpu.SemaphoreType.DMA((len(MESSAGES),))
    scratch["side_sem"] = pltpu.SemaphoreType.DMA((4,))
    scratch["halo_sem"] = pltpu.SemaphoreType.DMA((6,))
    names = tuple(inputs) + tuple(results) + tuple(scratch)
    outs = pl.pallas_call(
        functools.partial(kernel, names, nseq, nchan, group, scale),
        out_shape=tuple(results.values()),
        in_specs=[hbm] * len(inputs),
        out_specs=[vmem] * len(results),
        scratch_shapes=list(scratch.values()),
        compiler_params=pltpu.CompilerParams(
            collective_id=0, has_side_effects=True, vmem_limit_bytes=44 << 20
        ),
        name="hyena",
    )(*[pltpu.with_memory_space_constraint(x, pltpu.HBM) for x in inputs.values()])
    moved = pl.pallas_call(
        deliver,
        out_shape=tuple(results.values()),
        in_specs=[vmem] * len(results),
        out_specs=[hbm] * len(results),
        scratch_shapes=[pltpu.SemaphoreType.DMA((len(results),))],
        compiler_params=pltpu.CompilerParams(vmem_limit_bytes=16 << 20),
        name="deliver",
    )(*outs)
    return tuple(moved[:6]) + (moved[6].reshape(channels),)


def solution(mesh):
    in_specs = (
        P("seq", "chan"),
        P("seq", "chan"),
        P("seq", "chan"),
        P("seq", "chan"),
        P(None, None, ("seq", "chan")),
        P(("seq", "chan")),
        P("seq", "chan"),
    )
    out_specs = (
        P("seq", "chan"),
        P("seq", "chan"),
        P("seq", "chan"),
        P("seq", "chan"),
        P("seq", "chan"),
        P(None, None, "chan"),
        P("chan"),
    )
    return jax.shard_map(
        per_device, mesh=mesh, in_specs=in_specs, out_specs=out_specs, check_vma=False
    )
```

```python
import functools
import math
import types

import jax
import jax.numpy as jnp
import ml_dtypes
import numpy as np
from jax import lax
from jax.experimental import pallas as pl
from jax.experimental.pallas import tpu as pltpu
from jax.sharding import PartitionSpec as P

F32 = jnp.float32
BF16 = jnp.bfloat16
MESH = pl.DeviceIdType.MESH
REACH = 125.0 * math.log(2.0)


def halves(table):
    high = table.astype(np.float32).astype(ml_dtypes.bfloat16)
    low = (table - high.astype(np.float64)).astype(np.float32).astype(ml_dtypes.bfloat16)
    return np.stack([high, low])


def transform_tables(blocks, width, group):
    total = blocks * width
    shifted = np.arange(blocks) - 0.25
    outer = 2.0 * np.pi / blocks * np.outer(shifted, np.arange(blocks))
    eye = np.eye(group)
    left = np.concatenate([np.kron(np.cos(outer), eye), np.kron(-np.sin(outer), eye)], axis=0)
    back = left.T / total
    half = width // 2
    inner = 2.0 * np.pi / half * (np.outer(np.arange(half), np.arange(half)) % half)
    cosine, sine = halves(np.cos(inner)), halves(np.sin(inner))
    right = np.concatenate(
        [np.block([[cosine[i], -sine[i]], [sine[i], cosine[i]]]) for i in (0, 0, 1)]
    )
    step = 2.0 * np.pi / width * np.arange(half)
    swing = np.stack([np.tile(f(step), (8, 1)) for f in (np.cos, np.sin)]).astype(np.float32)
    turn = 2.0 * np.pi / total * np.outer(shifted, np.arange(width))
    twist = np.stack([np.cos(turn), np.sin(turn)]).astype(np.float32)
    twist = np.repeat(twist, group, axis=1)
    left, back = halves(left), halves(back)
    left = np.concatenate([left[0], left[0], left[1]], axis=1)
    left = left.reshape(2, 2, -1, left.shape[1]).swapaxes(0, 1).reshape(left.shape)
    back = np.concatenate([back[0], back[0], back[1]], axis=1)
    return left, back, right, twist, swing


def split(value):
    high = value.astype(BF16)
    return high, (value - high.astype(F32)).astype(BF16)


def dot(left, right):
    return jnp.dot(left, right, preferred_element_type=F32)


def delayed(value, steps):
    before = jnp.concatenate([jnp.zeros_like(value[:1]), value[:-1]], axis=0)
    lane = lax.broadcasted_iota(jnp.int32, value.shape, 2)
    return jnp.where(
        lane < steps, pltpu.roll(before, steps, 2), pltpu.roll(value, steps, 2)
    )


def later(value, head, steps):
    return pltpu.roll(jnp.concatenate([head, value], axis=0), steps, 0)[head.shape[0] :]


def block_ends(grad, coeffs):
    half = grad.shape[2] // 2
    low, high = grad[:, :, :half], grad[:, :, half:]
    after = jnp.concatenate([low[1:], jnp.zeros_like(low[:1])], axis=0)
    lane = lax.broadcasted_iota(jnp.int32, high.shape, 2)
    total = coeffs[0] * high
    for steps in (1, 2):
        moved = jnp.where(
            lane < half - steps,
            pltpu.roll(high, half - steps, 2),
            pltpu.roll(after, half - steps, 2),
        )
        total = total + coeffs[steps] * moved
    return [
        jnp.sum(jnp.where(lane == half - back, total, 0.0), axis=2, keepdims=True)
        for back in (2, 1)
    ]


def total_of(value):
    return jnp.sum(jnp.sum(value, axis=0), axis=1, keepdims=True)


def encode(value):
    peak = jnp.maximum(jnp.max(jnp.abs(value), axis=2, keepdims=True), 1e-30)
    code = jnp.exp(jnp.abs(value) * (2.0 * REACH / peak) - REACH)
    code = jnp.where(value < 0.0, -code, code)
    half = value.shape[2] // 2
    return jnp.concatenate([code[:, :, :half], code[:, :, half:]], axis=1).astype(BF16), peak


def decode(code, peak):
    group = code.shape[1] // 2
    code = code.astype(F32)
    code = jnp.concatenate([code[:, :group], code[:, group:]], axis=2)
    size = (jnp.log(jnp.abs(code)) + REACH) * (peak * (0.5 / REACH))
    return jnp.where(code < 0.0, -size, size)


def field_mask(group, field):
    lane = lax.broadcasted_iota(jnp.int32, (1, group, 128), 2)
    return lane == group * field + lax.broadcasted_iota(jnp.int32, (1, group, 128), 1)


def packed_rows(count, group, fields):
    wide = jnp.zeros((count, group, 128), F32)
    for field, value in fields.items():
        wide = jnp.where(field_mask(group, field), value, wide)
    return jnp.sum(wide, axis=1, keepdims=True)


def unpacked(rows, group, field):
    wide = jnp.broadcast_to(rows, (rows.shape[0], group, 128))
    return jnp.sum(jnp.where(field_mask(group, field), wide, 0.0), axis=2, keepdims=True)


def channel_rows(table, count, group):
    owners = table.shape[0]
    width = owners * group
    turned = jnp.concatenate(
        [table if f == 0 else pltpu.roll(table, 128 - group * f, 1) for f in range(count)],
        axis=0,
    )
    channel = lax.broadcasted_iota(jnp.int32, (128, width), 1)
    pick = lax.rem(channel, group) == lax.broadcasted_iota(jnp.int32, (128, width), 0)
    pick = pick.astype(F32).astype(BF16)
    high, low = split(turned)
    wide = (dot(high, pick) + dot(low, pick)).reshape(count, owners, width)
    owner = lax.div(lax.broadcasted_iota(jnp.int32, (owners, width), 1), group)
    keep = owner == lax.broadcasted_iota(jnp.int32, (owners, width), 0)
    return [jnp.sum(jnp.where(keep, wide[f], 0.0), axis=0, keepdims=True) for f in range(count)]


HALO = 16
DEPTH = 8


def farthest(step, length):
    away_by = lax.div(step + 1, 2)
    return jnp.where(lax.rem(step, 2) == 1, length // 2 - away_by, length // 2 + away_by)


def away(me, step, count):
    planes = count // DEPTH
    across = farthest(lax.div(step - 1, DEPTH), planes)
    along = farthest(lax.rem(step - 1, DEPTH), DEPTH)
    plane = lax.rem(lax.div(me, DEPTH) + across, planes)
    return DEPTH * plane + lax.rem(lax.rem(me, DEPTH) + along, DEPTH)


MESSAGES = ("kv", "h", "hs", "qc", "m", "p", "s", "f", "fs")


def kernel(names, nseq, nchan, group, scale, *refs):
    r = types.SimpleNamespace(**dict(zip(names, refs, strict=True)))
    me = lax.axis_index("seq")
    mine = lax.axis_index("chan")
    rows, width = r.q_hbm.shape
    number = {name: i for i, name in enumerate(MESSAGES)}

    fetched = {}
    pairs = [("k", "k"), ("v", "v"), ("h", "h"), ("q", "q"), ("c", "c"), ("taps", "taps_own")]
    pairs += [("gain", "gain_own"), ("left", "left"), ("twist", "twist")]
    pairs += [("right", "right"), ("back", "back"), ("swing", "swing")]
    for i, (src, dst) in enumerate(pairs):
        fetched[src] = pltpu.make_async_copy(
            getattr(r, src + "_hbm"), getattr(r, dst), r.fetch_sem.at[i]
        )
        fetched[src].start()

    per = nseq // nchan
    to_seq = nchan * lax.rem(me, per) + mine
    to_chan = lax.div(me, per)
    from_seq = per * mine + lax.div(me, nchan)
    from_chan = lax.rem(me, nchan)
    stays = jnp.logical_and(to_seq == me, to_chan == mine)

    barrier = pltpu.get_barrier_semaphore()

    def greet(step, carry):
        peer = lax.rem(me + step, nseq)
        pl.semaphore_signal(barrier, inc=1, device_id=(peer, mine), device_id_type=MESH)
        return carry

    lax.fori_loop(1, nseq, greet, 0)

    @pl.when(jnp.logical_not(stays))
    def _():
        pl.semaphore_signal(
            barrier, inc=1, device_id=(from_seq, from_chan), device_id_type=MESH
        )

    shape = (nseq, group, width)

    def paired(first, second):
        one = first[...].astype(F32).T.reshape(shape)
        two = second[...].astype(F32).T.reshape(shape)
        return jnp.concatenate([one, two], axis=1).astype(BF16)

    fetched["k"].wait()
    fetched["v"].wait()
    r.send_kv[...] = paired(r.k, r.v)

    @pl.when(stays)
    def _():
        pl.semaphore_wait(barrier, nseq - 1)

    @pl.when(jnp.logical_not(stays))
    def _():
        pl.semaphore_wait(barrier, nseq)

    def send_all(name, unroll=1):
        source, target = getattr(r, "send_" + name), getattr(r, "got_" + name)
        index = number[name]

        def body(step, carry):
            peer = away(me, step, nseq)
            pltpu.make_async_remote_copy(
                src_ref=source.at[peer],
                dst_ref=target.at[me],
                send_sem=r.send_sem.at[index],
                recv_sem=r.recv_sem.at[index],
                device_id=(peer, mine),
                device_id_type=MESH,
            ).start()
            return carry

        lax.fori_loop(1, nseq, body, 0, unroll=unroll)
        target[me] = source[me]

    def arrived(name):
        part = getattr(r, "got_" + name).at[pl.ds(0, nseq - 1)]
        pltpu.make_async_copy(part, part, r.recv_sem.at[number[name]]).wait()

    def sent(name):
        part = getattr(r, "send_" + name).at[pl.ds(0, nseq - 1)]
        pltpu.make_async_copy(part, part, r.send_sem.at[number[name]]).wait()

    send_all("kv")

    side_copies = [
        pltpu.make_async_remote_copy(
            src_ref=src,
            dst_ref=dst,
            send_sem=r.side_sem.at[i],
            recv_sem=r.side_sem.at[2 + i],
            device_id=(to_seq, to_chan),
            device_id_type=MESH,
        )
        for i, (src, dst) in enumerate([(r.taps_own, r.taps), (r.gain_own, r.gain)])
    ]
    fetched["taps"].wait()
    fetched["gain"].wait()

    @pl.when(jnp.logical_not(stays))
    def _():
        for copy in side_copies:
            copy.start()

    @pl.when(stays)
    def _():
        r.taps[...] = r.taps_own[...]
        r.gain[...] = r.gain_own[...]

    fetched["h"].wait()
    r.send_h[...], peak = encode(r.h[...].T.reshape(shape))
    r.send_hs[...] = packed_rows(nseq, group, {0: peak})
    send_all("h")
    send_all("hs")

    fetched["q"].wait()
    fetched["c"].wait()
    r.send_qc[...] = paired(r.q, r.c)
    send_all("qc")

    halo_copies = [
        pltpu.make_async_remote_copy(
            src_ref=src.at[pl.ds(rows - HALO, HALO)],
            dst_ref=r.halo.at[i],
            send_sem=r.halo_sem.at[i],
            recv_sem=r.halo_sem.at[3 + i],
            device_id=(lax.rem(me + 1, nseq), mine),
            device_id_type=MESH,
        )
        for i, src in enumerate([r.q, r.k, r.v])
    ]

    @pl.when(me < nseq - 1)
    def _():
        for copy in halo_copies:
            copy.start()

    @pl.when(me == 0)
    def _():
        r.halo[...] = jnp.zeros(r.halo.shape, BF16)

    @pl.when(jnp.logical_not(stays))
    def _():
        for copy in side_copies:
            copy.wait()

    diagonal = field_mask(group, 0)[0, :, :group]

    def column(row):
        spread_out = jnp.broadcast_to(row, (group, group))
        return jnp.sum(jnp.where(diagonal, spread_out, 0.0), axis=1, keepdims=True)

    taps = [[column(r.taps[s, i : i + 1, :]) for i in range(3)] for s in range(3)]
    gain = column(r.gain[...])
    for name in ("left", "twist", "right", "back", "swing"):
        fetched[name].wait()

    half = width // 2
    swing = [r.swing[i, :1, :] for i in range(2)]

    part_rows = rows // 2

    def over_lanes(block, real, imag):
        place = slice(block * rows, (block + 1) * rows)
        high_real, low_real = split(real)
        high_imag, low_imag = split(imag)
        parts = [high_real, high_imag, low_real, low_imag, high_real, high_imag]
        for i, part in enumerate(parts):
            r.lanes[place, i * half : (i + 1) * half] = part
        return dot(r.lanes[place, :], r.right[...])

    def forward(signal, spec):
        high, low = split(signal.reshape(rows, width))
        for i, part in enumerate([high, low, high]):
            r.stack[i * rows : (i + 1) * rows, :] = part
        waves = [
            dot(r.left[block * rows : (block + 1) * rows, :], r.stack[: 3 * rows, :])
            for block in range(2)
        ]
        for block, wave in enumerate(waves):
            real, imag = wave[:part_rows], wave[part_rows:]
            turn = slice(block * part_rows, (block + 1) * part_rows)
            cosine, sine = r.twist[0, turn, :], r.twist[1, turn, :]
            real, imag = real * cosine + imag * sine, imag * cosine - real * sine
            gap_real = real[:, :half] - real[:, half:]
            gap_imag = imag[:, :half] - imag[:, half:]
            even_real, even_imag = real[:, :half] + real[:, half:], imag[:, :half] + imag[:, half:]
            odd_real = gap_real * swing[0] + gap_imag * swing[1]
            odd_imag = gap_imag * swing[0] - gap_real * swing[1]
            spec[block * rows : (block + 1) * rows, :] = over_lanes(
                block,
                jnp.concatenate([even_real, odd_real], axis=0),
                jnp.concatenate([even_imag, odd_imag], axis=0),
            )

    def inverse(left_spec, right_spec, conjugate):
        waves = []
        for block in range(2):
            place = slice(block * rows, (block + 1) * rows)
            a_re, a_im = left_spec[place, :half], left_spec[place, half:]
            b_re, b_im = right_spec[place, :half], right_spec[place, half:]
            if conjugate:
                real, imag = a_re * b_re + a_im * b_im, a_im * b_re - a_re * b_im
            else:
                real, imag = a_re * b_re - a_im * b_im, -(a_re * b_im + a_im * b_re)
            waves.append(over_lanes(block, real, imag))
        for block, wave in enumerate(waves):
            even_real, even_imag = wave[:part_rows, :half], wave[:part_rows, half:]
            odd_real, odd_imag = wave[part_rows:, :half], wave[part_rows:, half:]
            odd_real, odd_imag = (
                odd_real * swing[0] + odd_imag * swing[1],
                odd_imag * swing[0] - odd_real * swing[1],
            )
            wave_real = jnp.concatenate([even_real + odd_real, even_real - odd_real], axis=1)
            wave_imag = jnp.concatenate([even_imag + odd_imag, even_imag - odd_imag], axis=1)
            turn = slice(block * part_rows, (block + 1) * part_rows)
            cosine, sine = r.twist[0, turn, :], r.twist[1, turn, :]
            high_real, low_real = split(wave_real * cosine + wave_imag * sine)
            high_imag, low_imag = split(wave_real * sine - wave_imag * cosine)
            parts = [high_real, high_imag, low_real, low_imag, high_real, high_imag]
            for i, part in enumerate(parts):
                start = i * rows + block * part_rows
                r.stack[start : start + part_rows, :] = part
        return dot(r.back[...], r.stack[...]).reshape(shape)

    def short(value, keep, coeffs):
        one, two = delayed(value, 1), delayed(value, 2)
        keep[0] = one
        keep[1] = two
        return coeffs[0] * value + coeffs[1] * one + coeffs[2] * two

    arrived("kv")
    both = r.got_kv[...].astype(F32)
    r.x_k[...] = both[:, :group]
    r.x_v[...] = both[:, group:]
    r.key_conv[...] = short(r.x_k[...], r.d_k, taps[1])
    r.value_conv[...] = short(r.x_v[...], r.d_v, taps[2])
    r.x_p[...] = r.key_conv[...] * r.value_conv[...]
    forward(r.x_p[...], r.spec_p)

    arrived("h")
    arrived("hs")
    forward(decode(r.got_h[...], unpacked(r.got_hs[...], group, 0)), r.spec_h)
    r.x_m[...] = inverse(r.spec_h, r.spec_p, False) + gain * r.x_p[...]
    r.send_m[...], peak = encode(r.x_m[...])
    send_all("m")
    fields = {2 + 3 * s + i: taps[s][i] for s in range(3) for i in range(3)}
    r.send_s[:, :, 128:] = packed_rows(nseq, group, {**fields, 1: peak})

    arrived("qc")
    both = r.got_qc[...].astype(F32)
    r.x_q[...] = both[:, :group]
    r.x_c[...] = both[:, group:]
    r.x_g[...] = r.x_c[...] * short(r.x_q[...], r.d_q, taps[0])
    forward(r.x_g[...], r.spec_g)
    r.x_pg[...] = inverse(r.spec_h, r.spec_g, True) + gain * r.x_g[...]
    r.send_p[...], peak = encode(r.x_pg[...])
    send_all("p", nseq - 1)

    grads = [
        (r.x_c[...] * r.x_m[...], r.x_q, r.d_q),
        (r.x_pg[...] * r.value_conv[...], r.x_k, r.d_k),
        (r.x_pg[...] * r.key_conv[...], r.x_v, r.d_v),
    ]
    fields = {9: scale * total_of(r.x_g[...] * r.x_p[...])}
    for s, (grad, stream, moved) in enumerate(grads):
        fields[3 * s] = scale * total_of(grad * stream[...])
        fields[3 * s + 1] = scale * total_of(grad * moved[0])
        fields[3 * s + 2] = scale * total_of(grad * moved[1])
        fields[10 + 2 * s], fields[11 + 2 * s] = block_ends(grad, taps[s])
    r.send_s[:, :, :128] = packed_rows(nseq, group, fields)
    r.send_s[:, :, 128:] = r.send_s[:, :, 128:] + packed_rows(nseq, group, {0: peak})
    send_all("s", nseq - 1)
    r.send_f[...], peak = encode(scale * inverse(r.spec_p, r.spec_g, True))
    send_all("f")
    r.send_fs[...] = packed_rows(nseq, group, {0: peak})
    send_all("fs")

    def spread(grad, s):
        return (
            tap_row(s, 0) * grad
            + tap_row(s, 1) * pltpu.roll(grad, rows - 1, 0)
            + tap_row(s, 2) * pltpu.roll(grad, rows - 2, 0)
        ).astype(BF16)

    def in_rows(name, side, field):
        return decode(getattr(r, "got_" + name)[...], unpacked(side, group, field)).reshape(
            rows, width
        ).T

    arrived("s")
    side = r.got_s[:, :, 128:]
    for i, row in enumerate(channel_rows(side.reshape(nseq, 128), 11, group)[2:]):
        r.taps_row[i : i + 1, :] = row

    @pl.when(me > 0)
    def _():
        for copy in halo_copies:
            copy.wait_recv()

    def tap_row(s, i):
        return r.taps_row[3 * s + i : 3 * s + i + 1, :]

    for s, src in enumerate([r.q, r.k, r.v]):
        own = src[...].astype(F32)
        above = r.halo[s].astype(F32)
        r.conv_rows[s] = (
            tap_row(s, 0) * own
            + tap_row(s, 1) * later(own, above, 1)
            + tap_row(s, 2) * later(own, above, 2)
        )

    arrived("m")
    mixed = in_rows("m", side, 1)
    r.go[...] = (r.conv_rows[0] * mixed).astype(BF16)
    r.qg[...] = spread(r.c[...].astype(F32) * mixed, 0)
    arrived("p")
    product_grad = in_rows("p", r.got_s[:, :, 128:], 0)
    r.kg[...] = spread(product_grad * r.conv_rows[2], 1)
    r.vg[...] = spread(product_grad * r.conv_rows[1], 2)
    finals = channel_rows(r.got_s[:, :, :128].reshape(nseq, 128), 16, group)
    place = lax.broadcasted_iota(jnp.int32, (HALO, width), 0)
    for i, grad in enumerate([r.qg, r.kg, r.vg]):
        last = grad[rows - HALO :, :].astype(F32)
        last = jnp.where(place == HALO - 2, finals[10 + 2 * i], last)
        last = jnp.where(place == HALO - 1, finals[11 + 2 * i], last)
        grad[rows - HALO :, :] = last.astype(BF16)
    for i in range(9):
        r.taps_grad[i // 3, i % 3 : i % 3 + 1, :] = finals[i]
    r.gain_grad[...] = finals[9]
    arrived("f")
    arrived("fs")
    r.fg[...] = in_rows("f", r.got_fs[...], 0)

    for name in MESSAGES:
        sent(name)

    @pl.when(me < nseq - 1)
    def _():
        for copy in halo_copies:
            copy.wait_send()


def deliver(*refs):
    count = len(refs) // 2
    copies = [
        pltpu.make_async_copy(refs[i], refs[count + i], refs[-1].at[i]) for i in range(count)
    ]
    for copy in copies:
        copy.start()
    for copy in copies:
        copy.wait()


def per_device(query_rows, key_rows, value_rows, long_filter, short_taps, skip_gain, cotangent):
    rows, channels = query_rows.shape
    nseq, nchan = lax.axis_size("seq"), lax.axis_size("chan")
    group = channels // nseq
    scale = 1.0 / math.sqrt(rows * nseq)
    tables = [jnp.asarray(t) for t in transform_tables(nseq, rows, group)]
    vmem = pl.BlockSpec(memory_space=pltpu.VMEM)
    hbm = pl.BlockSpec(memory_space=pltpu.HBM)
    inputs = {
        "q_hbm": query_rows,
        "k_hbm": key_rows,
        "v_hbm": value_rows,
        "c_hbm": cotangent,
        "h_hbm": long_filter,
        "taps_hbm": short_taps,
        "gain_hbm": skip_gain[None],
        "left_hbm": tables[0],
        "back_hbm": tables[1],
        "right_hbm": tables[2],
        "twist_hbm": tables[3],
        "swing_hbm": tables[4],
    }
    block = jax.ShapeDtypeStruct((rows, channels), BF16)
    results = {
        "go": block,
        "qg": block,
        "kg": block,
        "vg": block,
        "fg": jax.ShapeDtypeStruct((rows, channels), F32),
        "taps_grad": jax.ShapeDtypeStruct((3, 3, channels), F32),
        "gain_grad": jax.ShapeDtypeStruct((1, channels), F32),
    }
    local = pltpu.VMEM((rows, channels), BF16)
    taps, gain = pltpu.VMEM((3, 3, group), F32), pltpu.VMEM((1, group), F32)
    scratch = dict(
        q=local,
        k=local,
        v=local,
        c=local,
        h=pltpu.VMEM((rows, channels), F32),
        taps_own=taps,
        gain_own=gain,
        taps=taps,
        gain=gain,
        halo=pltpu.VMEM((3, HALO, channels), BF16),
        taps_row=pltpu.VMEM((16, channels), F32),
        conv_rows=pltpu.VMEM((3, rows, channels), F32),
    )
    for name, table in zip(("left", "back", "right", "twist", "swing"), tables):
        scratch[name] = pltpu.VMEM(table.shape, table.dtype)
    for name in MESSAGES:
        if name in ("kv", "qc"):
            kind = pltpu.VMEM((nseq, 2 * group, rows), BF16)
        elif name in ("h", "m", "p", "f"):
            kind = pltpu.VMEM((nseq, 2 * group, rows // 2), BF16)
        else:
            kind = pltpu.VMEM((nseq, 1, 256 if name == "s" else 128), F32)
        scratch["send_" + name] = scratch["got_" + name] = kind
    for name in ("x_q", "x_k", "x_v", "x_c", "x_p", "x_g", "x_m", "x_pg", "key_conv", "value_conv"):
        scratch[name] = pltpu.VMEM((nseq, group, rows), F32)
    for name in ("d_q", "d_k", "d_v"):
        scratch[name] = pltpu.VMEM((2, nseq, group, rows), F32)
    for name in ("spec_h", "spec_p", "spec_g"):
        scratch[name] = pltpu.VMEM((2 * nseq * group, rows), F32)
    scratch["lanes"] = pltpu.VMEM((2 * nseq * group, 3 * rows), BF16)
    scratch["stack"] = pltpu.VMEM((6 * nseq * group, rows), BF16)
    scratch["fetch_sem"] = pltpu.SemaphoreType.DMA((12,))
    scratch["send_sem"] = pltpu.SemaphoreType.DMA((len(MESSAGES),))
    scratch["recv_sem"] = pltpu.SemaphoreType.DMA((len(MESSAGES),))
    scratch["side_sem"] = pltpu.SemaphoreType.DMA((4,))
    scratch["halo_sem"] = pltpu.SemaphoreType.DMA((6,))
    names = tuple(inputs) + tuple(results) + tuple(scratch)
    outs = pl.pallas_call(
        functools.partial(kernel, names, nseq, nchan, group, scale),
        out_shape=tuple(results.values()),
        in_specs=[hbm] * len(inputs),
        out_specs=[vmem] * len(results),
        scratch_shapes=list(scratch.values()),
        compiler_params=pltpu.CompilerParams(
            collective_id=0, has_side_effects=True, vmem_limit_bytes=44 << 20
        ),
        name="hyena",
    )(*[pltpu.with_memory_space_constraint(x, pltpu.HBM) for x in inputs.values()])
    moved = pl.pallas_call(
        deliver,
        out_shape=tuple(results.values()),
        in_specs=[vmem] * len(results),
        out_specs=[hbm] * len(results),
        scratch_shapes=[pltpu.SemaphoreType.DMA((len(results),))],
        compiler_params=pltpu.CompilerParams(vmem_limit_bytes=16 << 20),
        name="deliver",
    )(*outs)
    return tuple(moved[:6]) + (moved[6].reshape(channels),)


def solution(mesh):
    in_specs = (
        P("seq", "chan"),
        P("seq", "chan"),
        P("seq", "chan"),
        P("seq", "chan"),
        P(None, None, ("seq", "chan")),
        P(("seq", "chan")),
        P("seq", "chan"),
    )
    out_specs = (
        P("seq", "chan"),
        P("seq", "chan"),
        P("seq", "chan"),
        P("seq", "chan"),
        P("seq", "chan"),
        P(None, None, "chan"),
        P("chan"),
    )
    return jax.shard_map(
        per_device, mesh=mesh, in_specs=in_specs, out_specs=out_specs, check_vma=False
    )
```

```python
import functools
import math
import types

import jax
import jax.numpy as jnp
import ml_dtypes
import numpy as np
from jax import lax
from jax.experimental import pallas as pl
from jax.experimental.pallas import tpu as pltpu
from jax.sharding import PartitionSpec as P

F32 = jnp.float32
BF16 = jnp.bfloat16
MESH = pl.DeviceIdType.MESH
REACH = 125.0 * math.log(2.0)


def halves(table):
    high = table.astype(np.float32).astype(ml_dtypes.bfloat16)
    low = (table - high.astype(np.float64)).astype(np.float32).astype(ml_dtypes.bfloat16)
    return np.stack([high, low])


def transform_tables(blocks, width, group):
    total = blocks * width
    shifted = np.arange(blocks) - 0.25
    outer = 2.0 * np.pi / blocks * np.outer(shifted, np.arange(blocks))
    eye = np.eye(group)
    left = np.concatenate([np.kron(np.cos(outer), eye), np.kron(-np.sin(outer), eye)], axis=0)
    back = left.T / total
    half = width // 2
    inner = 2.0 * np.pi / half * (np.outer(np.arange(half), np.arange(half)) % half)
    cosine, sine = halves(np.cos(inner)), halves(np.sin(inner))
    right = np.concatenate(
        [np.block([[cosine[i], -sine[i]], [sine[i], cosine[i]]]) for i in (0, 0, 1)]
    )
    step = 2.0 * np.pi / width * np.arange(half)
    swing = np.stack([np.tile(f(step), (8, 1)) for f in (np.cos, np.sin)]).astype(np.float32)
    turn = 2.0 * np.pi / total * np.outer(shifted, np.arange(width))
    twist = np.stack([np.cos(turn), np.sin(turn)]).astype(np.float32)
    twist = np.repeat(twist, group, axis=1)
    left, back = halves(left), halves(back)
    left = np.concatenate([left[0], left[0], left[1]], axis=1)
    left = left.reshape(2, 2, -1, left.shape[1]).swapaxes(0, 1).reshape(left.shape)
    back = np.concatenate([back[0], back[0], back[1]], axis=1)
    return left, back, right, twist, swing


def split(value):
    high = value.astype(BF16)
    return high, (value - high.astype(F32)).astype(BF16)


def dot(left, right):
    return jnp.dot(left, right, preferred_element_type=F32)


def delayed(value, steps):
    before = jnp.concatenate([jnp.zeros_like(value[:1]), value[:-1]], axis=0)
    lane = lax.broadcasted_iota(jnp.int32, value.shape, 2)
    return jnp.where(
        lane < steps, pltpu.roll(before, steps, 2), pltpu.roll(value, steps, 2)
    )


def later(value, head, steps):
    return pltpu.roll(jnp.concatenate([head, value], axis=0), steps, 0)[head.shape[0] :]


def block_ends(grad, coeffs):
    half = grad.shape[2] // 2
    low, high = grad[:, :, :half], grad[:, :, half:]
    after = jnp.concatenate([low[1:], jnp.zeros_like(low[:1])], axis=0)
    lane = lax.broadcasted_iota(jnp.int32, high.shape, 2)
    total = coeffs[0] * high
    for steps in (1, 2):
        moved = jnp.where(
            lane < half - steps,
            pltpu.roll(high, half - steps, 2),
            pltpu.roll(after, half - steps, 2),
        )
        total = total + coeffs[steps] * moved
    return [
        jnp.sum(jnp.where(lane == half - back, total, 0.0), axis=2, keepdims=True)
        for back in (2, 1)
    ]


def total_of(value):
    return jnp.sum(jnp.sum(value, axis=0), axis=1, keepdims=True)


def encode(value):
    peak = jnp.maximum(jnp.max(jnp.abs(value), axis=2, keepdims=True), 1e-30)
    code = jnp.exp(jnp.abs(value) * (2.0 * REACH / peak) - REACH)
    code = jnp.where(value < 0.0, -code, code)
    half = value.shape[2] // 2
    return jnp.concatenate([code[:, :, :half], code[:, :, half:]], axis=1).astype(BF16), peak


def decode(code, peak):
    group = code.shape[1] // 2
    code = code.astype(F32)
    code = jnp.concatenate([code[:, :group], code[:, group:]], axis=2)
    size = (jnp.log(jnp.abs(code)) + REACH) * (peak * (0.5 / REACH))
    return jnp.where(code < 0.0, -size, size)


def field_mask(group, field):
    lane = lax.broadcasted_iota(jnp.int32, (1, group, 128), 2)
    return lane == group * field + lax.broadcasted_iota(jnp.int32, (1, group, 128), 1)


def packed_rows(count, group, fields):
    wide = jnp.zeros((count, group, 128), F32)
    for field, value in fields.items():
        wide = jnp.where(field_mask(group, field), value, wide)
    return jnp.sum(wide, axis=1, keepdims=True)


def unpacked(rows, group, field):
    wide = jnp.broadcast_to(rows, (rows.shape[0], group, 128))
    return jnp.sum(jnp.where(field_mask(group, field), wide, 0.0), axis=2, keepdims=True)


def channel_rows(table, count, group):
    owners = table.shape[0]
    width = owners * group
    turned = jnp.concatenate(
        [table if f == 0 else pltpu.roll(table, 128 - group * f, 1) for f in range(count)],
        axis=0,
    )
    channel = lax.broadcasted_iota(jnp.int32, (128, width), 1)
    pick = lax.rem(channel, group) == lax.broadcasted_iota(jnp.int32, (128, width), 0)
    pick = pick.astype(F32).astype(BF16)
    high, low = split(turned)
    wide = (dot(high, pick) + dot(low, pick)).reshape(count, owners, width)
    owner = lax.div(lax.broadcasted_iota(jnp.int32, (owners, width), 1), group)
    keep = owner == lax.broadcasted_iota(jnp.int32, (owners, width), 0)
    return [jnp.sum(jnp.where(keep, wide[f], 0.0), axis=0, keepdims=True) for f in range(count)]


HALO = 16
DEPTH = 8


def farthest(step, length):
    away_by = lax.div(step + 1, 2)
    return jnp.where(lax.rem(step, 2) == 1, length // 2 - away_by, length // 2 + away_by)


def away(me, step, count):
    planes = count // DEPTH
    across = farthest(lax.div(step - 1, DEPTH), planes)
    along = farthest(lax.rem(step - 1, DEPTH), DEPTH)
    plane = lax.rem(lax.div(me, DEPTH) + across, planes)
    return DEPTH * plane + lax.rem(lax.rem(me, DEPTH) + along, DEPTH)


MESSAGES = ("kv", "h", "hs", "qc", "m", "p", "s", "f", "fs")


def kernel(names, nseq, nchan, group, scale, *refs):
    r = types.SimpleNamespace(**dict(zip(names, refs, strict=True)))
    me = lax.axis_index("seq")
    mine = lax.axis_index("chan")
    rows, width = r.q_hbm.shape
    number = {name: i for i, name in enumerate(MESSAGES)}

    fetched = {}
    pairs = [("k", "k"), ("v", "v"), ("h", "h"), ("q", "q"), ("c", "c"), ("taps", "taps_own")]
    pairs += [("gain", "gain_own"), ("left", "left"), ("twist", "twist")]
    pairs += [("right", "right"), ("back", "back"), ("swing", "swing")]
    for i, (src, dst) in enumerate(pairs):
        fetched[src] = pltpu.make_async_copy(
            getattr(r, src + "_hbm"), getattr(r, dst), r.fetch_sem.at[i]
        )
        fetched[src].start()

    per = nseq // nchan
    to_seq = nchan * lax.rem(me, per) + mine
    to_chan = lax.div(me, per)
    from_seq = per * mine + lax.div(me, nchan)
    from_chan = lax.rem(me, nchan)
    stays = jnp.logical_and(to_seq == me, to_chan == mine)

    barrier = pltpu.get_barrier_semaphore()

    def greet(step, carry):
        peer = lax.rem(me + step, nseq)
        pl.semaphore_signal(barrier, inc=1, device_id=(peer, mine), device_id_type=MESH)
        return carry

    lax.fori_loop(1, nseq, greet, 0)

    @pl.when(jnp.logical_not(stays))
    def _():
        pl.semaphore_signal(
            barrier, inc=1, device_id=(from_seq, from_chan), device_id_type=MESH
        )

    shape = (nseq, group, width)

    def paired(first, second):
        one = first[...].astype(F32).T.reshape(shape)
        two = second[...].astype(F32).T.reshape(shape)
        return jnp.concatenate([one, two], axis=1).astype(BF16)

    fetched["k"].wait()
    fetched["v"].wait()
    r.send_kv[...] = paired(r.k, r.v)

    @pl.when(stays)
    def _():
        pl.semaphore_wait(barrier, nseq - 1)

    @pl.when(jnp.logical_not(stays))
    def _():
        pl.semaphore_wait(barrier, nseq)

    def send_all(name, unroll=1):
        source, target = getattr(r, "send_" + name), getattr(r, "got_" + name)
        index = number[name]

        def body(step, carry):
            peer = away(me, step, nseq)
            pltpu.make_async_remote_copy(
                src_ref=source.at[peer],
                dst_ref=target.at[me],
                send_sem=r.send_sem.at[index],
                recv_sem=r.recv_sem.at[index],
                device_id=(peer, mine),
                device_id_type=MESH,
            ).start()
            return carry

        lax.fori_loop(1, nseq, body, 0, unroll=unroll)
        target[me] = source[me]

    def arrived(name):
        part = getattr(r, "got_" + name).at[pl.ds(0, nseq - 1)]
        pltpu.make_async_copy(part, part, r.recv_sem.at[number[name]]).wait()

    def sent(name):
        part = getattr(r, "send_" + name).at[pl.ds(0, nseq - 1)]
        pltpu.make_async_copy(part, part, r.send_sem.at[number[name]]).wait()

    send_all("kv")

    side_copies = [
        pltpu.make_async_remote_copy(
            src_ref=src,
            dst_ref=dst,
            send_sem=r.side_sem.at[i],
            recv_sem=r.side_sem.at[2 + i],
            device_id=(to_seq, to_chan),
            device_id_type=MESH,
        )
        for i, (src, dst) in enumerate([(r.taps_own, r.taps), (r.gain_own, r.gain)])
    ]
    fetched["taps"].wait()
    fetched["gain"].wait()

    @pl.when(jnp.logical_not(stays))
    def _():
        for copy in side_copies:
            copy.start()

    @pl.when(stays)
    def _():
        r.taps[...] = r.taps_own[...]
        r.gain[...] = r.gain_own[...]

    fetched["h"].wait()
    r.send_h[...], peak = encode(r.h[...].T.reshape(shape))
    r.send_hs[...] = packed_rows(nseq, group, {0: peak})
    send_all("h")
    send_all("hs")

    fetched["q"].wait()
    fetched["c"].wait()
    r.send_qc[...] = paired(r.q, r.c)
    send_all("qc")

    halo_copies = [
        pltpu.make_async_remote_copy(
            src_ref=src.at[pl.ds(rows - HALO, HALO)],
            dst_ref=r.halo.at[i],
            send_sem=r.halo_sem.at[i],
            recv_sem=r.halo_sem.at[3 + i],
            device_id=(lax.rem(me + 1, nseq), mine),
            device_id_type=MESH,
        )
        for i, src in enumerate([r.q, r.k, r.v])
    ]

    @pl.when(me < nseq - 1)
    def _():
        for copy in halo_copies:
            copy.start()

    @pl.when(me == 0)
    def _():
        r.halo[...] = jnp.zeros(r.halo.shape, BF16)

    @pl.when(jnp.logical_not(stays))
    def _():
        for copy in side_copies:
            copy.wait()

    diagonal = field_mask(group, 0)[0, :, :group]

    def column(row):
        spread_out = jnp.broadcast_to(row, (group, group))
        return jnp.sum(jnp.where(diagonal, spread_out, 0.0), axis=1, keepdims=True)

    taps = [[column(r.taps[s, i : i + 1, :]) for i in range(3)] for s in range(3)]
    gain = column(r.gain[...])
    for name in ("left", "twist", "right", "back", "swing"):
        fetched[name].wait()

    half = width // 2
    swing = [r.swing[i, :1, :] for i in range(2)]

    part_rows = rows // 2

    def over_lanes(block, real, imag):
        place = slice(block * rows, (block + 1) * rows)
        high_real, low_real = split(real)
        high_imag, low_imag = split(imag)
        parts = [high_real, high_imag, low_real, low_imag, high_real, high_imag]
        for i, part in enumerate(parts):
            r.lanes[place, i * half : (i + 1) * half] = part
        return dot(r.lanes[place, :], r.right[...])

    def forward(signal, spec):
        high, low = split(signal.reshape(rows, width))
        for i, part in enumerate([high, low, high]):
            r.stack[i * rows : (i + 1) * rows, :] = part
        waves = [
            dot(r.left[block * rows : (block + 1) * rows, :], r.stack[: 3 * rows, :])
            for block in range(2)
        ]
        for block, wave in enumerate(waves):
            real, imag = wave[:part_rows], wave[part_rows:]
            turn = slice(block * part_rows, (block + 1) * part_rows)
            cosine, sine = r.twist[0, turn, :], r.twist[1, turn, :]
            real, imag = real * cosine + imag * sine, imag * cosine - real * sine
            gap_real = real[:, :half] - real[:, half:]
            gap_imag = imag[:, :half] - imag[:, half:]
            even_real, even_imag = real[:, :half] + real[:, half:], imag[:, :half] + imag[:, half:]
            odd_real = gap_real * swing[0] + gap_imag * swing[1]
            odd_imag = gap_imag * swing[0] - gap_real * swing[1]
            spec[block * rows : (block + 1) * rows, :] = over_lanes(
                block,
                jnp.concatenate([even_real, odd_real], axis=0),
                jnp.concatenate([even_imag, odd_imag], axis=0),
            )

    def inverse(left_spec, right_spec, conjugate):
        waves = []
        for block in range(2):
            place = slice(block * rows, (block + 1) * rows)
            a_re, a_im = left_spec[place, :half], left_spec[place, half:]
            b_re, b_im = right_spec[place, :half], right_spec[place, half:]
            if conjugate:
                real, imag = a_re * b_re + a_im * b_im, a_im * b_re - a_re * b_im
            else:
                real, imag = a_re * b_re - a_im * b_im, -(a_re * b_im + a_im * b_re)
            waves.append(over_lanes(block, real, imag))
        for block, wave in enumerate(waves):
            even_real, even_imag = wave[:part_rows, :half], wave[:part_rows, half:]
            odd_real, odd_imag = wave[part_rows:, :half], wave[part_rows:, half:]
            odd_real, odd_imag = (
                odd_real * swing[0] + odd_imag * swing[1],
                odd_imag * swing[0] - odd_real * swing[1],
            )
            wave_real = jnp.concatenate([even_real + odd_real, even_real - odd_real], axis=1)
            wave_imag = jnp.concatenate([even_imag + odd_imag, even_imag - odd_imag], axis=1)
            turn = slice(block * part_rows, (block + 1) * part_rows)
            cosine, sine = r.twist[0, turn, :], r.twist[1, turn, :]
            high_real, low_real = split(wave_real * cosine + wave_imag * sine)
            high_imag, low_imag = split(wave_real * sine - wave_imag * cosine)
            parts = [high_real, high_imag, low_real, low_imag, high_real, high_imag]
            for i, part in enumerate(parts):
                start = i * rows + block * part_rows
                r.stack[start : start + part_rows, :] = part
        return dot(r.back[...], r.stack[...]).reshape(shape)

    def short(value, keep, coeffs):
        one, two = delayed(value, 1), delayed(value, 2)
        keep[0] = one
        keep[1] = two
        return coeffs[0] * value + coeffs[1] * one + coeffs[2] * two

    arrived("kv")
    both = r.got_kv[...].astype(F32)
    r.x_k[...] = both[:, :group]
    r.x_v[...] = both[:, group:]
    r.key_conv[...] = short(r.x_k[...], r.d_k, taps[1])
    r.value_conv[...] = short(r.x_v[...], r.d_v, taps[2])
    r.x_p[...] = r.key_conv[...] * r.value_conv[...]
    forward(r.x_p[...], r.spec_p)

    arrived("h")
    arrived("hs")
    forward(decode(r.got_h[...], unpacked(r.got_hs[...], group, 0)), r.spec_h)
    r.x_m[...] = inverse(r.spec_h, r.spec_p, False) + gain * r.x_p[...]
    r.send_m[...], peak = encode(r.x_m[...])
    send_all("m")
    fields = {2 + 3 * s + i: taps[s][i] for s in range(3) for i in range(3)}
    r.send_s[:, :, 128:] = packed_rows(nseq, group, {**fields, 1: peak})

    arrived("qc")
    both = r.got_qc[...].astype(F32)
    r.x_q[...] = both[:, :group]
    r.x_c[...] = both[:, group:]
    r.x_g[...] = r.x_c[...] * short(r.x_q[...], r.d_q, taps[0])
    forward(r.x_g[...], r.spec_g)
    r.x_pg[...] = inverse(r.spec_h, r.spec_g, True) + gain * r.x_g[...]
    r.send_p[...], peak = encode(r.x_pg[...])
    send_all("p", nseq - 1)

    grads = [
        (r.x_c[...] * r.x_m[...], r.x_q, r.d_q),
        (r.x_pg[...] * r.value_conv[...], r.x_k, r.d_k),
        (r.x_pg[...] * r.key_conv[...], r.x_v, r.d_v),
    ]
    fields = {9: scale * total_of(r.x_g[...] * r.x_p[...])}
    for s, (grad, stream, moved) in enumerate(grads):
        fields[3 * s] = scale * total_of(grad * stream[...])
        fields[3 * s + 1] = scale * total_of(grad * moved[0])
        fields[3 * s + 2] = scale * total_of(grad * moved[1])
        fields[10 + 2 * s], fields[11 + 2 * s] = block_ends(grad, taps[s])
    r.send_s[:, :, :128] = packed_rows(nseq, group, fields)
    r.send_s[:, :, 128:] = r.send_s[:, :, 128:] + packed_rows(nseq, group, {0: peak})
    send_all("s", nseq - 1)
    r.send_f[...], peak = encode(scale * inverse(r.spec_p, r.spec_g, True))
    send_all("f")
    r.send_fs[...] = packed_rows(nseq, group, {0: peak})
    send_all("fs")

    def spread(grad, s):
        return (
            tap_row(s, 0) * grad
            + tap_row(s, 1) * pltpu.roll(grad, rows - 1, 0)
            + tap_row(s, 2) * pltpu.roll(grad, rows - 2, 0)
        ).astype(BF16)

    def in_rows(name, peaks):
        return decode(getattr(r, "got_" + name)[...], peaks).reshape(rows, width).T

    unit = jnp.ones((nseq, group, 1), F32)
    arrived("m")
    r.mixed_rows[...] = in_rows("m", unit)

    arrived("s")
    side = r.got_s[:, :, 128:]
    for i, row in enumerate(channel_rows(side.reshape(nseq, 128), 11, group)):
        r.taps_row[i : i + 1, :] = row

    @pl.when(me > 0)
    def _():
        for copy in halo_copies:
            copy.wait_recv()

    def tap_row(s, i):
        return r.taps_row[2 + 3 * s + i : 3 + 3 * s + i, :]

    for s, src in enumerate([r.q, r.k, r.v]):
        own = src[...].astype(F32)
        above = r.halo[s].astype(F32)
        r.conv_rows[s] = (
            tap_row(s, 0) * own
            + tap_row(s, 1) * later(own, above, 1)
            + tap_row(s, 2) * later(own, above, 2)
        )

    mixed = r.mixed_rows[...] * r.taps_row[1:2, :]
    r.go[...] = (r.conv_rows[0] * mixed).astype(BF16)
    r.qg[...] = spread(r.c[...].astype(F32) * mixed, 0)
    arrived("p")
    product_grad = in_rows("p", unit) * r.taps_row[0:1, :]
    r.kg[...] = spread(product_grad * r.conv_rows[2], 1)
    r.vg[...] = spread(product_grad * r.conv_rows[1], 2)
    finals = channel_rows(r.got_s[:, :, :128].reshape(nseq, 128), 16, group)
    place = lax.broadcasted_iota(jnp.int32, (HALO, width), 0)
    for i, grad in enumerate([r.qg, r.kg, r.vg]):
        last = grad[rows - HALO :, :].astype(F32)
        last = jnp.where(place == HALO - 2, finals[10 + 2 * i], last)
        last = jnp.where(place == HALO - 1, finals[11 + 2 * i], last)
        grad[rows - HALO :, :] = last.astype(BF16)
    for i in range(9):
        r.taps_grad[i // 3, i % 3 : i % 3 + 1, :] = finals[i]
    r.gain_grad[...] = finals[9]
    arrived("f")
    arrived("fs")
    r.fg[...] = in_rows("f", unpacked(r.got_fs[...], group, 0))

    for name in MESSAGES:
        sent(name)

    @pl.when(me < nseq - 1)
    def _():
        for copy in halo_copies:
            copy.wait_send()


def deliver(*refs):
    count = len(refs) // 2
    copies = [
        pltpu.make_async_copy(refs[i], refs[count + i], refs[-1].at[i]) for i in range(count)
    ]
    for copy in copies:
        copy.start()
    for copy in copies:
        copy.wait()


def per_device(query_rows, key_rows, value_rows, long_filter, short_taps, skip_gain, cotangent):
    rows, channels = query_rows.shape
    nseq, nchan = lax.axis_size("seq"), lax.axis_size("chan")
    group = channels // nseq
    scale = 1.0 / math.sqrt(rows * nseq)
    tables = [jnp.asarray(t) for t in transform_tables(nseq, rows, group)]
    vmem = pl.BlockSpec(memory_space=pltpu.VMEM)
    hbm = pl.BlockSpec(memory_space=pltpu.HBM)
    inputs = {
        "q_hbm": query_rows,
        "k_hbm": key_rows,
        "v_hbm": value_rows,
        "c_hbm": cotangent,
        "h_hbm": long_filter,
        "taps_hbm": short_taps,
        "gain_hbm": skip_gain[None],
        "left_hbm": tables[0],
        "back_hbm": tables[1],
        "right_hbm": tables[2],
        "twist_hbm": tables[3],
        "swing_hbm": tables[4],
    }
    block = jax.ShapeDtypeStruct((rows, channels), BF16)
    results = {
        "go": block,
        "qg": block,
        "kg": block,
        "vg": block,
        "fg": jax.ShapeDtypeStruct((rows, channels), F32),
        "taps_grad": jax.ShapeDtypeStruct((3, 3, channels), F32),
        "gain_grad": jax.ShapeDtypeStruct((1, channels), F32),
    }
    local = pltpu.VMEM((rows, channels), BF16)
    taps, gain = pltpu.VMEM((3, 3, group), F32), pltpu.VMEM((1, group), F32)
    scratch = dict(
        q=local,
        k=local,
        v=local,
        c=local,
        h=pltpu.VMEM((rows, channels), F32),
        taps_own=taps,
        gain_own=gain,
        taps=taps,
        gain=gain,
        halo=pltpu.VMEM((3, HALO, channels), BF16),
        taps_row=pltpu.VMEM((16, channels), F32),
        mixed_rows=pltpu.VMEM((rows, channels), F32),
        conv_rows=pltpu.VMEM((3, rows, channels), F32),
    )
    for name, table in zip(("left", "back", "right", "twist", "swing"), tables):
        scratch[name] = pltpu.VMEM(table.shape, table.dtype)
    for name in MESSAGES:
        if name in ("kv", "qc"):
            kind = pltpu.VMEM((nseq, 2 * group, rows), BF16)
        elif name in ("h", "m", "p", "f"):
            kind = pltpu.VMEM((nseq, 2 * group, rows // 2), BF16)
        else:
            kind = pltpu.VMEM((nseq, 1, 256 if name == "s" else 128), F32)
        scratch["send_" + name] = scratch["got_" + name] = kind
    for name in ("x_q", "x_k", "x_v", "x_c", "x_p", "x_g", "x_m", "x_pg", "key_conv", "value_conv"):
        scratch[name] = pltpu.VMEM((nseq, group, rows), F32)
    for name in ("d_q", "d_k", "d_v"):
        scratch[name] = pltpu.VMEM((2, nseq, group, rows), F32)
    for name in ("spec_h", "spec_p", "spec_g"):
        scratch[name] = pltpu.VMEM((2 * nseq * group, rows), F32)
    scratch["lanes"] = pltpu.VMEM((2 * nseq * group, 3 * rows), BF16)
    scratch["stack"] = pltpu.VMEM((6 * nseq * group, rows), BF16)
    scratch["fetch_sem"] = pltpu.SemaphoreType.DMA((12,))
    scratch["send_sem"] = pltpu.SemaphoreType.DMA((len(MESSAGES),))
    scratch["recv_sem"] = pltpu.SemaphoreType.DMA((len(MESSAGES),))
    scratch["side_sem"] = pltpu.SemaphoreType.DMA((4,))
    scratch["halo_sem"] = pltpu.SemaphoreType.DMA((6,))
    names = tuple(inputs) + tuple(results) + tuple(scratch)
    outs = pl.pallas_call(
        functools.partial(kernel, names, nseq, nchan, group, scale),
        out_shape=tuple(results.values()),
        in_specs=[hbm] * len(inputs),
        out_specs=[vmem] * len(results),
        scratch_shapes=list(scratch.values()),
        compiler_params=pltpu.CompilerParams(
            collective_id=0, has_side_effects=True, vmem_limit_bytes=44 << 20
        ),
        name="hyena",
    )(*[pltpu.with_memory_space_constraint(x, pltpu.HBM) for x in inputs.values()])
    moved = pl.pallas_call(
        deliver,
        out_shape=tuple(results.values()),
        in_specs=[vmem] * len(results),
        out_specs=[hbm] * len(results),
        scratch_shapes=[pltpu.SemaphoreType.DMA((len(results),))],
        compiler_params=pltpu.CompilerParams(vmem_limit_bytes=16 << 20),
        name="deliver",
    )(*outs)
    return tuple(moved[:6]) + (moved[6].reshape(channels),)


def solution(mesh):
    in_specs = (
        P("seq", "chan"),
        P("seq", "chan"),
        P("seq", "chan"),
        P("seq", "chan"),
        P(None, None, ("seq", "chan")),
        P(("seq", "chan")),
        P("seq", "chan"),
    )
    out_specs = (
        P("seq", "chan"),
        P("seq", "chan"),
        P("seq", "chan"),
        P("seq", "chan"),
        P("seq", "chan"),
        P(None, None, "chan"),
        P("chan"),
    )
    return jax.shard_map(
        per_device, mesh=mesh, in_specs=in_specs, out_specs=out_specs, check_vma=False
    )
```

```python
import functools
import math
import types

import jax
import jax.numpy as jnp
import ml_dtypes
import numpy as np
from jax import lax
from jax.experimental import pallas as pl
from jax.experimental.pallas import tpu as pltpu
from jax.sharding import PartitionSpec as P

F32 = jnp.float32
BF16 = jnp.bfloat16
MESH = pl.DeviceIdType.MESH
REACH = 125.0 * math.log(2.0)


def halves(table):
    high = table.astype(np.float32).astype(ml_dtypes.bfloat16)
    low = (table - high.astype(np.float64)).astype(np.float32).astype(ml_dtypes.bfloat16)
    return np.stack([high, low])


def transform_tables(blocks, width, group):
    total = blocks * width
    shifted = np.arange(blocks) - 0.25
    outer = 2.0 * np.pi / blocks * np.outer(shifted, np.arange(blocks))
    eye = np.eye(group)
    left = np.concatenate([np.kron(np.cos(outer), eye), np.kron(-np.sin(outer), eye)], axis=0)
    back = left.T / total
    half = width // 2
    inner = 2.0 * np.pi / half * (np.outer(np.arange(half), np.arange(half)) % half)
    cosine, sine = halves(np.cos(inner)), halves(np.sin(inner))
    right = np.concatenate(
        [np.block([[cosine[i], -sine[i]], [sine[i], cosine[i]]]) for i in (0, 0, 1)]
    )
    step = 2.0 * np.pi / width * np.arange(half)
    swing = np.stack([np.tile(f(step), (8, 1)) for f in (np.cos, np.sin)]).astype(np.float32)
    turn = 2.0 * np.pi / total * np.outer(shifted, np.arange(width))
    twist = np.stack([np.cos(turn), np.sin(turn)]).astype(np.float32)
    twist = np.repeat(twist, group, axis=1)
    left, back = halves(left), halves(back)
    left = np.concatenate([left[0], left[0], left[1]], axis=1)
    left = left.reshape(2, 2, -1, left.shape[1]).swapaxes(0, 1).reshape(left.shape)
    back = np.concatenate([back[0], back[0], back[1]], axis=1)
    return left, back, right, twist, swing


def split(value):
    high = value.astype(BF16)
    return high, (value - high.astype(F32)).astype(BF16)


def dot(left, right):
    return jnp.dot(left, right, preferred_element_type=F32)


def delayed(value, steps):
    before = jnp.concatenate([jnp.zeros_like(value[:1]), value[:-1]], axis=0)
    lane = lax.broadcasted_iota(jnp.int32, value.shape, 2)
    return jnp.where(
        lane < steps, pltpu.roll(before, steps, 2), pltpu.roll(value, steps, 2)
    )


def later(value, head, steps):
    return pltpu.roll(jnp.concatenate([head, value], axis=0), steps, 0)[head.shape[0] :]


def block_ends(grad, coeffs):
    half = grad.shape[2] // 2
    low, high = grad[:, :, :half], grad[:, :, half:]
    after = jnp.concatenate([low[1:], jnp.zeros_like(low[:1])], axis=0)
    lane = lax.broadcasted_iota(jnp.int32, high.shape, 2)
    total = coeffs[0] * high
    for steps in (1, 2):
        moved = jnp.where(
            lane < half - steps,
            pltpu.roll(high, half - steps, 2),
            pltpu.roll(after, half - steps, 2),
        )
        total = total + coeffs[steps] * moved
    return [
        jnp.sum(jnp.where(lane == half - back, total, 0.0), axis=2, keepdims=True)
        for back in (2, 1)
    ]


def total_of(value):
    return jnp.sum(jnp.sum(value, axis=0), axis=1, keepdims=True)


def encode(value):
    peak = jnp.maximum(jnp.max(jnp.abs(value), axis=2, keepdims=True), 1e-30)
    code = jnp.exp(jnp.abs(value) * (2.0 * REACH / peak) - REACH)
    code = jnp.where(value < 0.0, -code, code)
    half = value.shape[2] // 2
    return jnp.concatenate([code[:, :, :half], code[:, :, half:]], axis=1).astype(BF16), peak


def decode(code, peak):
    group = code.shape[1] // 2
    code = code.astype(F32)
    code = jnp.concatenate([code[:, :group], code[:, group:]], axis=2)
    size = (jnp.log(jnp.abs(code)) + REACH) * (peak * (0.5 / REACH))
    return jnp.where(code < 0.0, -size, size)


def field_mask(group, field):
    lane = lax.broadcasted_iota(jnp.int32, (1, group, 128), 2)
    return lane == group * field + lax.broadcasted_iota(jnp.int32, (1, group, 128), 1)


def packed_rows(count, group, fields):
    wide = jnp.zeros((count, group, 128), F32)
    for field, value in fields.items():
        wide = jnp.where(field_mask(group, field), value, wide)
    return jnp.sum(wide, axis=1, keepdims=True)


def unpacked(rows, group, field):
    wide = jnp.broadcast_to(rows, (rows.shape[0], group, 128))
    return jnp.sum(jnp.where(field_mask(group, field), wide, 0.0), axis=2, keepdims=True)


def channel_rows(table, count, group):
    owners = table.shape[0]
    width = owners * group
    turned = jnp.concatenate(
        [table if f == 0 else pltpu.roll(table, 128 - group * f, 1) for f in range(count)],
        axis=0,
    )
    channel = lax.broadcasted_iota(jnp.int32, (128, width), 1)
    pick = lax.rem(channel, group) == lax.broadcasted_iota(jnp.int32, (128, width), 0)
    pick = pick.astype(F32).astype(BF16)
    high, low = split(turned)
    wide = (dot(high, pick) + dot(low, pick)).reshape(count, owners, width)
    owner = lax.div(lax.broadcasted_iota(jnp.int32, (owners, width), 1), group)
    keep = owner == lax.broadcasted_iota(jnp.int32, (owners, width), 0)
    return [jnp.sum(jnp.where(keep, wide[f], 0.0), axis=0, keepdims=True) for f in range(count)]


HALO = 16
DEPTH = 8


def farthest(step, length):
    away_by = lax.div(step + 1, 2)
    return jnp.where(lax.rem(step, 2) == 1, length // 2 - away_by, length // 2 + away_by)


def away(me, step, count):
    planes = count // DEPTH
    across = farthest(lax.div(step - 1, DEPTH), planes)
    along = farthest(lax.rem(step - 1, DEPTH), DEPTH)
    plane = lax.rem(lax.div(me, DEPTH) + across, planes)
    return DEPTH * plane + lax.rem(lax.rem(me, DEPTH) + along, DEPTH)


MESSAGES = ("kv", "h", "hs", "qc", "m", "p", "s", "f", "fs")


def kernel(names, nseq, nchan, group, scale, *refs):
    r = types.SimpleNamespace(**dict(zip(names, refs, strict=True)))
    me = lax.axis_index("seq")
    mine = lax.axis_index("chan")
    rows, width = r.q_hbm.shape
    number = {name: i for i, name in enumerate(MESSAGES)}

    fetched = {}
    pairs = [("k", "k"), ("v", "v"), ("h", "h"), ("q", "q"), ("c", "c"), ("taps", "taps_own")]
    pairs += [("gain", "gain_own"), ("left", "left"), ("twist", "twist")]
    pairs += [("right", "right"), ("back", "back"), ("swing", "swing")]
    for i, (src, dst) in enumerate(pairs):
        fetched[src] = pltpu.make_async_copy(
            getattr(r, src + "_hbm"), getattr(r, dst), r.fetch_sem.at[i]
        )
        fetched[src].start()

    per = nseq // nchan
    to_seq = nchan * lax.rem(me, per) + mine
    to_chan = lax.div(me, per)
    from_seq = per * mine + lax.div(me, nchan)
    from_chan = lax.rem(me, nchan)
    stays = jnp.logical_and(to_seq == me, to_chan == mine)

    barrier = pltpu.get_barrier_semaphore()

    def greet(step, carry):
        peer = lax.rem(me + step, nseq)
        pl.semaphore_signal(barrier, inc=1, device_id=(peer, mine), device_id_type=MESH)
        return carry

    lax.fori_loop(1, nseq, greet, 0)

    @pl.when(jnp.logical_not(stays))
    def _():
        pl.semaphore_signal(
            barrier, inc=1, device_id=(from_seq, from_chan), device_id_type=MESH
        )

    shape = (nseq, group, width)

    def paired(first, second):
        one = first[...].astype(F32).T.reshape(shape)
        two = second[...].astype(F32).T.reshape(shape)
        return jnp.concatenate([one, two], axis=1).astype(BF16)

    fetched["k"].wait()
    fetched["v"].wait()
    r.send_kv[...] = paired(r.k, r.v)

    @pl.when(stays)
    def _():
        pl.semaphore_wait(barrier, nseq - 1)

    @pl.when(jnp.logical_not(stays))
    def _():
        pl.semaphore_wait(barrier, nseq)

    def send_all(name, unroll=1):
        source, target = getattr(r, "send_" + name), getattr(r, "got_" + name)
        index = number[name]

        def body(step, carry):
            peer = away(me, step, nseq)
            pltpu.make_async_remote_copy(
                src_ref=source.at[peer],
                dst_ref=target.at[me],
                send_sem=r.send_sem.at[index],
                recv_sem=r.recv_sem.at[index],
                device_id=(peer, mine),
                device_id_type=MESH,
            ).start()
            return carry

        lax.fori_loop(1, nseq, body, 0, unroll=unroll)
        target[me] = source[me]

    def arrived(name):
        part = getattr(r, "got_" + name).at[pl.ds(0, nseq - 1)]
        pltpu.make_async_copy(part, part, r.recv_sem.at[number[name]]).wait()

    def sent(name):
        part = getattr(r, "send_" + name).at[pl.ds(0, nseq - 1)]
        pltpu.make_async_copy(part, part, r.send_sem.at[number[name]]).wait()

    send_all("kv")

    side_copies = [
        pltpu.make_async_remote_copy(
            src_ref=src,
            dst_ref=dst,
            send_sem=r.side_sem.at[i],
            recv_sem=r.side_sem.at[2 + i],
            device_id=(to_seq, to_chan),
            device_id_type=MESH,
        )
        for i, (src, dst) in enumerate([(r.taps_own, r.taps), (r.gain_own, r.gain)])
    ]
    fetched["taps"].wait()
    fetched["gain"].wait()

    @pl.when(jnp.logical_not(stays))
    def _():
        for copy in side_copies:
            copy.start()

    @pl.when(stays)
    def _():
        r.taps[...] = r.taps_own[...]
        r.gain[...] = r.gain_own[...]

    fetched["h"].wait()
    r.send_h[...], peak = encode(r.h[...].T.reshape(shape))
    r.send_hs[...] = packed_rows(nseq, group, {0: peak})
    send_all("h")
    send_all("hs")

    fetched["q"].wait()
    fetched["c"].wait()
    r.send_qc[...] = paired(r.q, r.c)
    send_all("qc")

    halo_copies = [
        pltpu.make_async_remote_copy(
            src_ref=src.at[pl.ds(rows - HALO, HALO)],
            dst_ref=r.halo.at[i],
            send_sem=r.halo_sem.at[i],
            recv_sem=r.halo_sem.at[3 + i],
            device_id=(lax.rem(me + 1, nseq), mine),
            device_id_type=MESH,
        )
        for i, src in enumerate([r.q, r.k, r.v])
    ]

    @pl.when(me < nseq - 1)
    def _():
        for copy in halo_copies:
            copy.start()

    @pl.when(me == 0)
    def _():
        r.halo[...] = jnp.zeros(r.halo.shape, BF16)

    @pl.when(jnp.logical_not(stays))
    def _():
        for copy in side_copies:
            copy.wait()

    diagonal = field_mask(group, 0)[0, :, :group]

    def column(row):
        spread_out = jnp.broadcast_to(row, (group, group))
        return jnp.sum(jnp.where(diagonal, spread_out, 0.0), axis=1, keepdims=True)

    taps = [[column(r.taps[s, i : i + 1, :]) for i in range(3)] for s in range(3)]
    gain = column(r.gain[...])
    for name in ("left", "twist", "right", "back", "swing"):
        fetched[name].wait()

    half = width // 2
    swing = [r.swing[i, :1, :] for i in range(2)]

    part_rows = rows // 2

    def over_lanes(block, real, imag):
        place = slice(block * rows, (block + 1) * rows)
        high_real, low_real = split(real)
        high_imag, low_imag = split(imag)
        parts = [high_real, high_imag, low_real, low_imag, high_real, high_imag]
        for i, part in enumerate(parts):
            r.lanes[place, i * half : (i + 1) * half] = part
        return dot(r.lanes[place, :], r.right[...])

    def forward(signal, spec):
        high, low = split(signal.reshape(rows, width))
        for i, part in enumerate([high, low, high]):
            r.stack[i * rows : (i + 1) * rows, :] = part
        waves = [
            dot(r.left[block * rows : (block + 1) * rows, :], r.stack[: 3 * rows, :])
            for block in range(2)
        ]
        for block, wave in enumerate(waves):
            real, imag = wave[:part_rows], wave[part_rows:]
            turn = slice(block * part_rows, (block + 1) * part_rows)
            cosine, sine = r.twist[0, turn, :], r.twist[1, turn, :]
            real, imag = real * cosine + imag * sine, imag * cosine - real * sine
            gap_real = real[:, :half] - real[:, half:]
            gap_imag = imag[:, :half] - imag[:, half:]
            even_real, even_imag = real[:, :half] + real[:, half:], imag[:, :half] + imag[:, half:]
            odd_real = gap_real * swing[0] + gap_imag * swing[1]
            odd_imag = gap_imag * swing[0] - gap_real * swing[1]
            spec[block * rows : (block + 1) * rows, :] = over_lanes(
                block,
                jnp.concatenate([even_real, odd_real], axis=0),
                jnp.concatenate([even_imag, odd_imag], axis=0),
            )

    def inverse(left_spec, right_spec, conjugate):
        waves = []
        for block in range(2):
            place = slice(block * rows, (block + 1) * rows)
            a_re, a_im = left_spec[place, :half], left_spec[place, half:]
            b_re, b_im = right_spec[place, :half], right_spec[place, half:]
            if conjugate:
                real, imag = a_re * b_re + a_im * b_im, a_im * b_re - a_re * b_im
            else:
                real, imag = a_re * b_re - a_im * b_im, -(a_re * b_im + a_im * b_re)
            waves.append(over_lanes(block, real, imag))
        for block, wave in enumerate(waves):
            even_real, even_imag = wave[:part_rows, :half], wave[:part_rows, half:]
            odd_real, odd_imag = wave[part_rows:, :half], wave[part_rows:, half:]
            odd_real, odd_imag = (
                odd_real * swing[0] + odd_imag * swing[1],
                odd_imag * swing[0] - odd_real * swing[1],
            )
            wave_real = jnp.concatenate([even_real + odd_real, even_real - odd_real], axis=1)
            wave_imag = jnp.concatenate([even_imag + odd_imag, even_imag - odd_imag], axis=1)
            turn = slice(block * part_rows, (block + 1) * part_rows)
            cosine, sine = r.twist[0, turn, :], r.twist[1, turn, :]
            high_real, low_real = split(wave_real * cosine + wave_imag * sine)
            high_imag, low_imag = split(wave_real * sine - wave_imag * cosine)
            parts = [high_real, high_imag, low_real, low_imag, high_real, high_imag]
            for i, part in enumerate(parts):
                start = i * rows + block * part_rows
                r.stack[start : start + part_rows, :] = part
        return dot(r.back[...], r.stack[...]).reshape(shape)

    def short(value, keep, coeffs):
        one, two = delayed(value, 1), delayed(value, 2)
        keep[0] = one
        keep[1] = two
        return coeffs[0] * value + coeffs[1] * one + coeffs[2] * two

    arrived("kv")
    both = r.got_kv[...].astype(F32)
    r.x_k[...] = both[:, :group]
    r.x_v[...] = both[:, group:]
    r.key_conv[...] = short(r.x_k[...], r.d_k, taps[1])
    r.value_conv[...] = short(r.x_v[...], r.d_v, taps[2])
    r.x_p[...] = r.key_conv[...] * r.value_conv[...]
    forward(r.x_p[...], r.spec_p)

    arrived("h")
    arrived("hs")
    forward(decode(r.got_h[...], unpacked(r.got_hs[...], group, 0)), r.spec_h)
    r.x_m[...] = inverse(r.spec_h, r.spec_p, False) + gain * r.x_p[...]
    r.send_m[...], peak = encode(r.x_m[...])
    send_all("m")
    fields = {2 + 3 * s + i: taps[s][i] for s in range(3) for i in range(3)}
    r.send_s[:, :, 128:] = packed_rows(nseq, group, {**fields, 1: peak})

    arrived("qc")
    both = r.got_qc[...].astype(F32)
    r.x_q[...] = both[:, :group]
    r.x_c[...] = both[:, group:]
    r.x_g[...] = r.x_c[...] * short(r.x_q[...], r.d_q, taps[0])
    forward(r.x_g[...], r.spec_g)
    r.x_pg[...] = inverse(r.spec_h, r.spec_g, True) + gain * r.x_g[...]
    r.send_p[...], peak = encode(r.x_pg[...])
    send_all("p", nseq - 1)

    grads = [
        (r.x_c[...] * r.x_m[...], r.x_q, r.d_q),
        (r.x_pg[...] * r.value_conv[...], r.x_k, r.d_k),
        (r.x_pg[...] * r.key_conv[...], r.x_v, r.d_v),
    ]
    fields = {9: scale * total_of(r.x_g[...] * r.x_p[...])}
    for s, (grad, stream, moved) in enumerate(grads):
        fields[3 * s] = scale * total_of(grad * stream[...])
        fields[3 * s + 1] = scale * total_of(grad * moved[0])
        fields[3 * s + 2] = scale * total_of(grad * moved[1])
        fields[10 + 2 * s], fields[11 + 2 * s] = block_ends(grad, taps[s])
    r.send_s[:, :, :128] = packed_rows(nseq, group, fields)
    r.send_s[:, :, 128:] = r.send_s[:, :, 128:] + packed_rows(nseq, group, {0: peak})
    send_all("s", nseq - 1)
    r.send_f[...], peak = encode(scale * inverse(r.spec_p, r.spec_g, True))
    send_all("f", nseq - 1)
    r.send_fs[...] = packed_rows(nseq, group, {0: peak})
    send_all("fs")

    def spread(grad, s):
        return (
            tap_row(s, 0) * grad
            + tap_row(s, 1) * pltpu.roll(grad, rows - 1, 0)
            + tap_row(s, 2) * pltpu.roll(grad, rows - 2, 0)
        ).astype(BF16)

    def in_rows(name, side, field):
        return decode(getattr(r, "got_" + name)[...], unpacked(side, group, field)).reshape(
            rows, width
        ).T

    arrived("s")
    side = r.got_s[:, :, 128:]
    for i, row in enumerate(channel_rows(side.reshape(nseq, 128), 11, group)[2:]):
        r.taps_row[i : i + 1, :] = row

    @pl.when(me > 0)
    def _():
        for copy in halo_copies:
            copy.wait_recv()

    def tap_row(s, i):
        return r.taps_row[3 * s + i : 3 * s + i + 1, :]

    for s, src in enumerate([r.q, r.k, r.v]):
        own = src[...].astype(F32)
        above = r.halo[s].astype(F32)
        r.conv_rows[s] = (
            tap_row(s, 0) * own
            + tap_row(s, 1) * later(own, above, 1)
            + tap_row(s, 2) * later(own, above, 2)
        )

    arrived("m")
    mixed = in_rows("m", side, 1)
    r.go[...] = (r.conv_rows[0] * mixed).astype(BF16)
    r.qg[...] = spread(r.c[...].astype(F32) * mixed, 0)
    arrived("p")
    product_grad = in_rows("p", r.got_s[:, :, 128:], 0)
    r.kg[...] = spread(product_grad * r.conv_rows[2], 1)
    r.vg[...] = spread(product_grad * r.conv_rows[1], 2)
    finals = channel_rows(r.got_s[:, :, :128].reshape(nseq, 128), 16, group)
    place = lax.broadcasted_iota(jnp.int32, (HALO, width), 0)
    for i, grad in enumerate([r.qg, r.kg, r.vg]):
        last = grad[rows - HALO :, :].astype(F32)
        last = jnp.where(place == HALO - 2, finals[10 + 2 * i], last)
        last = jnp.where(place == HALO - 1, finals[11 + 2 * i], last)
        grad[rows - HALO :, :] = last.astype(BF16)
    for i in range(9):
        r.taps_grad[i // 3, i % 3 : i % 3 + 1, :] = finals[i]
    r.gain_grad[...] = finals[9]
    arrived("f")
    arrived("fs")
    r.fg[...] = in_rows("f", r.got_fs[...], 0)

    for name in MESSAGES:
        sent(name)

    @pl.when(me < nseq - 1)
    def _():
        for copy in halo_copies:
            copy.wait_send()


def deliver(*refs):
    count = len(refs) // 2
    copies = [
        pltpu.make_async_copy(refs[i], refs[count + i], refs[-1].at[i]) for i in range(count)
    ]
    for copy in copies:
        copy.start()
    for copy in copies:
        copy.wait()


def per_device(query_rows, key_rows, value_rows, long_filter, short_taps, skip_gain, cotangent):
    rows, channels = query_rows.shape
    nseq, nchan = lax.axis_size("seq"), lax.axis_size("chan")
    group = channels // nseq
    scale = 1.0 / math.sqrt(rows * nseq)
    tables = [jnp.asarray(t) for t in transform_tables(nseq, rows, group)]
    vmem = pl.BlockSpec(memory_space=pltpu.VMEM)
    hbm = pl.BlockSpec(memory_space=pltpu.HBM)
    inputs = {
        "q_hbm": query_rows,
        "k_hbm": key_rows,
        "v_hbm": value_rows,
        "c_hbm": cotangent,
        "h_hbm": long_filter,
        "taps_hbm": short_taps,
        "gain_hbm": skip_gain[None],
        "left_hbm": tables[0],
        "back_hbm": tables[1],
        "right_hbm": tables[2],
        "twist_hbm": tables[3],
        "swing_hbm": tables[4],
    }
    block = jax.ShapeDtypeStruct((rows, channels), BF16)
    results = {
        "go": block,
        "qg": block,
        "kg": block,
        "vg": block,
        "fg": jax.ShapeDtypeStruct((rows, channels), F32),
        "taps_grad": jax.ShapeDtypeStruct((3, 3, channels), F32),
        "gain_grad": jax.ShapeDtypeStruct((1, channels), F32),
    }
    local = pltpu.VMEM((rows, channels), BF16)
    taps, gain = pltpu.VMEM((3, 3, group), F32), pltpu.VMEM((1, group), F32)
    scratch = dict(
        q=local,
        k=local,
        v=local,
        c=local,
        h=pltpu.VMEM((rows, channels), F32),
        taps_own=taps,
        gain_own=gain,
        taps=taps,
        gain=gain,
        halo=pltpu.VMEM((3, HALO, channels), BF16),
        taps_row=pltpu.VMEM((16, channels), F32),
        conv_rows=pltpu.VMEM((3, rows, channels), F32),
    )
    for name, table in zip(("left", "back", "right", "twist", "swing"), tables):
        scratch[name] = pltpu.VMEM(table.shape, table.dtype)
    for name in MESSAGES:
        if name in ("kv", "qc"):
            kind = pltpu.VMEM((nseq, 2 * group, rows), BF16)
        elif name in ("h", "m", "p", "f"):
            kind = pltpu.VMEM((nseq, 2 * group, rows // 2), BF16)
        else:
            kind = pltpu.VMEM((nseq, 1, 256 if name == "s" else 128), F32)
        scratch["send_" + name] = scratch["got_" + name] = kind
    for name in ("x_q", "x_k", "x_v", "x_c", "x_p", "x_g", "x_m", "x_pg", "key_conv", "value_conv"):
        scratch[name] = pltpu.VMEM((nseq, group, rows), F32)
    for name in ("d_q", "d_k", "d_v"):
        scratch[name] = pltpu.VMEM((2, nseq, group, rows), F32)
    for name in ("spec_h", "spec_p", "spec_g"):
        scratch[name] = pltpu.VMEM((2 * nseq * group, rows), F32)
    scratch["lanes"] = pltpu.VMEM((2 * nseq * group, 3 * rows), BF16)
    scratch["stack"] = pltpu.VMEM((6 * nseq * group, rows), BF16)
    scratch["fetch_sem"] = pltpu.SemaphoreType.DMA((12,))
    scratch["send_sem"] = pltpu.SemaphoreType.DMA((len(MESSAGES),))
    scratch["recv_sem"] = pltpu.SemaphoreType.DMA((len(MESSAGES),))
    scratch["side_sem"] = pltpu.SemaphoreType.DMA((4,))
    scratch["halo_sem"] = pltpu.SemaphoreType.DMA((6,))
    names = tuple(inputs) + tuple(results) + tuple(scratch)
    outs = pl.pallas_call(
        functools.partial(kernel, names, nseq, nchan, group, scale),
        out_shape=tuple(results.values()),
        in_specs=[hbm] * len(inputs),
        out_specs=[vmem] * len(results),
        scratch_shapes=list(scratch.values()),
        compiler_params=pltpu.CompilerParams(
            collective_id=0, has_side_effects=True, vmem_limit_bytes=44 << 20
        ),
        name="hyena",
    )(*[pltpu.with_memory_space_constraint(x, pltpu.HBM) for x in inputs.values()])
    moved = pl.pallas_call(
        deliver,
        out_shape=tuple(results.values()),
        in_specs=[vmem] * len(results),
        out_specs=[hbm] * len(results),
        scratch_shapes=[pltpu.SemaphoreType.DMA((len(results),))],
        compiler_params=pltpu.CompilerParams(vmem_limit_bytes=16 << 20),
        name="deliver",
    )(*outs)
    return tuple(moved[:6]) + (moved[6].reshape(channels),)


def solution(mesh):
    in_specs = (
        P("seq", "chan"),
        P("seq", "chan"),
        P("seq", "chan"),
        P("seq", "chan"),
        P(None, None, ("seq", "chan")),
        P(("seq", "chan")),
        P("seq", "chan"),
    )
    out_specs = (
        P("seq", "chan"),
        P("seq", "chan"),
        P("seq", "chan"),
        P("seq", "chan"),
        P("seq", "chan"),
        P(None, None, "chan"),
        P("chan"),
    )
    return jax.shard_map(
        per_device, mesh=mesh, in_specs=in_specs, out_specs=out_specs, check_vma=False
    )
```
